256 devices in a mesh: sub: 32 (over z, x), layer: 8 (over y, core).
Axes of the slice: x: 4, y: 4, z: 8, core: 2. Of those that a mesh axis runs over, the one named last changes fastest.
Arguments:
- local_gap: float32 [32, 8, 1152, 128], P('sub', 'layer'), may hold values from -6 to 6
- route_codes: int32 [32, 8, 1152], P('sub', 'layer'), may hold values from 0 to 1152, as said below
- flexibility: float32 [32, 8, 1152, 1152], P('sub', 'layer'), may hold values from -1 to 3
- dirichlet: float32 [32, 8, 1152, 1152], P('sub', 'layer'), may hold values from -1 to 3
- rigid_modes: float32 [32, 8, 6, 1152], P('sub', 'layer'), may hold values from -6 to 6
- coarse_inverse: float32 [1536, 1536], P(('sub', 'layer')), may hold values from -1 to 1
- rigid_load: float32 [1536, 128], P(('sub', 'layer')), may hold values from -360 to 360
Outputs:
- multipliers: float32 [32, 8, 1152, 128], P('sub', 'layer')
- residual: float32 [32, 8, 1152, 128], P('sub', 'layer')
The draws below stay inside these ranges and needn't reach their ends.
Inputs may be any that keep to these rules, and one draw needn't show every extreme that they name: `route_codes`: row r of subdomain (i, j) carries d * 288 + k when it is the k-th row it shares with neighbour d (0: sub index i - 1, 1: i + 1, 2: layer index j - 1, 3: j + 1); the row of that neighbour carrying e * 288 + k, e the opposite direction, is the same interface row. 4 * 288 marks a row shared with nobody. Neighbouring subdomains share between 144 and 288 rows, some pair exactly 288; there is no neighbour beyond the ends of an axis.
All inputs are finite; a program needn't handle non-finite values.
Results may differ from the reference program's by a relative error of at most 0.00017.
Values sent between devices are 32-bit elements; how exact they have to be, the bound alone decides.
A program may use at most 128 MiB of HBM per device.

```python
import math
import jax
import jax.numpy as jnp
from jax import lax

NI = 1152
CAP = 288
MODES = 6
RHS = 128
SUBS = 32
LAYERS = 8
COARSE = 1536


def permute_rows(row_seed):
    return jax.random.permutation(row_seed, 4 * CAP)


def interface_maps(key):
    across_key = jax.random.fold_in(key, 11)
    upward_key = jax.random.fold_in(key, 12)
    order_key = jax.random.fold_in(key, 13)
    across = jax.random.randint(across_key, (SUBS, LAYERS), CAP // 2, CAP + 1).astype(jnp.int32)
    across = across.at[0, 0].set(CAP)
    upward = jax.random.randint(upward_key, (SUBS, LAYERS), CAP // 2, CAP + 1).astype(jnp.int32)
    sub_index = jnp.arange(SUBS)[:, None]
    layer_index = jnp.arange(LAYERS)[None, :]
    left_count = jnp.where(sub_index > 0, jnp.roll(across, 1, 0), 0)
    right_count = jnp.where(sub_index < SUBS - 1, across, 0)
    lower_count = jnp.where(layer_index > 0, jnp.roll(upward, 1, 1), 0)
    upper_count = jnp.where(layer_index < LAYERS - 1, upward, 0)
    counts = jnp.stack([left_count, right_count, lower_count, upper_count], axis=-1)
    code_values = jnp.arange(4 * CAP, dtype=jnp.int32)
    valid_slot = (code_values % CAP)[None, None, :] < jnp.repeat(counts, CAP, axis=-1)
    slot_codes = jnp.where(valid_slot, code_values[None, None, :], 4 * CAP).astype(jnp.int32)
    device_keys = jax.random.split(order_key, SUBS * LAYERS)
    row_order = jax.vmap(permute_rows)(device_keys).reshape(SUBS, LAYERS, 4 * CAP)
    return (valid_slot, row_order, slot_codes)


def mode_codes(key):
    valid_slot, row_order, slot_codes = interface_maps(key)
    base_shape = (SUBS, LAYERS, CAP, MODES)
    noise_shape = (SUBS, LAYERS, 4 * CAP, MODES)
    across_base = jnp.clip(jax.random.normal(jax.random.fold_in(key, 21), base_shape, jnp.float32), -4.0, 4.0)
    upward_base = jnp.clip(jax.random.normal(jax.random.fold_in(key, 22), base_shape, jnp.float32), -4.0, 4.0)
    own_noise = 0.5 * jnp.clip(jax.random.normal(jax.random.fold_in(key, 23), noise_shape, jnp.float32), -4.0, 4.0)
    shared_base = jnp.concatenate([jnp.roll(across_base, 1, 0), across_base, jnp.roll(upward_base, 1, 1), upward_base], axis=2)
    mode_values = jnp.where(valid_slot[..., None], shared_base + own_noise, 0.0)
    return (row_order, mode_values)


def local_operator(key):
    full_shape = (SUBS, LAYERS, NI, NI)
    normal_draw = jnp.clip(jax.random.normal(jax.random.fold_in(key, 1), full_shape, jnp.float32), -6.0, 6.0)
    diagonal_values = jax.random.uniform(jax.random.fold_in(key, 2), (SUBS, LAYERS, NI), jnp.float32, 1.0, 2.0)
    symmetric = (normal_draw + jnp.swapaxes(normal_draw, 2, 3)) * (0.4 / math.sqrt(2.0 * NI))
    on_diagonal = jnp.arange(NI)[:, None] == jnp.arange(NI)[None, :]
    return symmetric + jnp.where(on_diagonal, diagonal_values[..., None], 0.0)


def draw_route_codes(key, part):
    valid_slot, row_order, slot_codes = interface_maps(key)
    return jnp.take_along_axis(slot_codes, row_order, axis=2).astype(jnp.int32)


def draw_flexibility(key, part):
    return local_operator(jax.random.fold_in(key, 31))


def draw_dirichlet(key, part):
    return local_operator(jax.random.fold_in(key, 41))


def draw_rigid_modes(key, part):
    row_order, mode_values = mode_codes(key)
    placed = jnp.take_along_axis(mode_values, row_order[..., None], axis=2)
    return jnp.transpose(placed, (0, 1, 3, 2))


def draw_coarse_inverse(key, part):
    full_shape = (COARSE, COARSE)
    raw_draw = jnp.clip(jax.random.normal(jax.random.fold_in(key, 51), full_shape, jnp.float32), -4.0, 4.0)
    dense_part = (raw_draw + raw_draw.T) * (0.25 / math.sqrt(2.0 * COARSE))
    row_scales = jax.random.uniform(jax.random.fold_in(key, 52), (COARSE,), jnp.float32, 0.75, 1.25) / (3.0 * CAP)
    root_scales = jnp.sqrt(row_scales)
    on_diagonal = jnp.arange(COARSE)[:, None] == jnp.arange(COARSE)[None, :]
    core = dense_part + jnp.where(on_diagonal, 1.0, 0.0)
    return root_scales[:, None] * root_scales[None, :] * core


def level_of(key, shape, cuts, low, largest):
    level = 1.0
    for position, shards_of in cuts:
        heights = jax.random.uniform(jax.random.fold_in(jax.random.fold_in(key, 6), position), (shards_of,), jnp.float32, low / len(cuts), largest / len(cuts))
        level = level * jnp.repeat(jnp.exp(heights), shape[position] // shards_of).reshape((-1,) + (1,) * (len(shape) - 1 - position))
    return level


def centred(key, dims, deviation, bound, shards=(), kind=jnp.bfloat16):
    drawn = jax.random.normal(key, dims, jnp.float32) * deviation
    if len(shards) > 0:
        drawn = level_of(key, dims, shards, -0.22, 0.18) * drawn
    return jnp.clip(drawn, min=-bound, max=bound).astype(kind)


def setup_inputs(seed: int = 0) -> dict:
    splits = jax.random.split(jax.random.key(seed), 8)
    return {
        "local_gap": centred(splits[0], (SUBS, LAYERS, NI, RHS), 1.0, 6.0, ((0, 32), (1, 8)), jnp.float32),
        "route_codes": draw_route_codes(jax.random.fold_in(splits[7], 71), 0),
        "flexibility": draw_flexibility(jax.random.fold_in(splits[7], 71), 0),
        "dirichlet": draw_dirichlet(jax.random.fold_in(splits[7], 71), 0),
        "rigid_modes": draw_rigid_modes(jax.random.fold_in(splits[7], 71), 0),
        "coarse_inverse": draw_coarse_inverse(jax.random.fold_in(splits[7], 71), 0),
        "rigid_load": centred(splits[6], (COARSE, RHS), 60.0, 360.0, ((0, 256),), jnp.float32),
    }


exact_mode = lax.Precision.HIGHEST
theta_mid = 4.25
delta_half = 3.75

def interface_jump(values, route_codes):
    live_rows = route_codes < 4 * CAP
    heading = jnp.minimum(route_codes // CAP, 3)
    slot_index = route_codes % CAP
    sub_index = jnp.arange(SUBS, dtype=jnp.int32)[:, None, None]
    layer_index = jnp.arange(LAYERS, dtype=jnp.int32)[None, :, None]
    row_index = jnp.arange(NI, dtype=jnp.int32)
    sub_step = jnp.where(heading == 0, -1, jnp.where(heading == 1, 1, 0)).astype(jnp.int32)
    layer_step = jnp.where(heading == 2, -1, jnp.where(heading == 3, 1, 0)).astype(jnp.int32)
    partner_sub = jnp.clip(sub_index + sub_step, 0, SUBS - 1).astype(jnp.int32)
    partner_layer = jnp.clip(layer_index + layer_step, 0, LAYERS - 1).astype(jnp.int32)
    opposite = heading + 1 - 2 * (heading % 2)
    row_table = jnp.zeros((SUBS, LAYERS, 4 * CAP + 1), jnp.int32)
    row_table = row_table.at[sub_index, layer_index, route_codes].set(jnp.broadcast_to(row_index, route_codes.shape).astype(jnp.int32))
    partner_row = row_table[partner_sub, partner_layer, (opposite * CAP + slot_index).astype(jnp.int32)]
    received = values[partner_sub, partner_layer, partner_row]
    return jnp.where(live_rows[..., None], values - received, 0.0)

def correction(coefficients, rigid_modes, route_codes):
    shaped = coefficients.reshape(SUBS, LAYERS, MODES, -1)
    traces = jnp.einsum('slkn,slkr->slnr', rigid_modes, shaped, precision=exact_mode)
    return interface_jump(traces, route_codes)

def project(values, rigid_modes, coarse_inverse, route_codes):
    components = jnp.einsum('slkn,slnr->slkr', rigid_modes, values, precision=exact_mode).reshape(COARSE, -1)
    coefficients = jnp.dot(coarse_inverse.astype(jnp.float32), components.astype(jnp.float32), precision=exact_mode, preferred_element_type=jnp.float32)
    return values - correction(coefficients, rigid_modes, route_codes)

def apply_local(matrix, values):
    return jnp.einsum('slij,sljr->slir', matrix, values, precision=exact_mode)

def reference(local_gap, route_codes, flexibility, dirichlet, rigid_modes, coarse_inverse, rigid_load):
    sigma_ratio = theta_mid / delta_half

    def operator(values):
        return project(interface_jump(apply_local(flexibility, values), route_codes), rigid_modes, coarse_inverse, route_codes)

    def precond(values):
        return project(0.5 * interface_jump(apply_local(dirichlet, values), route_codes), rigid_modes, coarse_inverse, route_codes)
    gap_jump = interface_jump(local_gap, route_codes)
    start = correction(jnp.dot(coarse_inverse.astype(jnp.float32), rigid_load.astype(jnp.float32), precision=exact_mode, preferred_element_type=jnp.float32), rigid_modes, route_codes)
    residual = project(gap_jump - interface_jump(apply_local(flexibility, start), route_codes), rigid_modes, coarse_inverse, route_codes)
    step_value = precond(residual) / theta_mid
    damping = delta_half / theta_mid
    multipliers = start + step_value
    residual = residual - operator(step_value)
    damping_next = 1.0 / (2.0 * sigma_ratio - damping)
    step_value = damping_next * damping * step_value + 2.0 * damping_next / delta_half * precond(residual)
    multipliers = multipliers + step_value
    residual = residual - operator(step_value)
    return (multipliers, residual)
```

```python
import functools

import jax
import jax.numpy as jnp
from jax import lax
from jax.experimental import pallas as pl
from jax.experimental.pallas import tpu as pltpu
from jax.sharding import PartitionSpec as P

MESH = pl.DeviceIdType.MESH
THETA = 4.25
DELTA = 3.75
SIGMA = THETA / DELTA
RHO0 = DELTA / THETA
RHO1 = 1.0 / (2.0 * SIGMA - RHO0)
CORES = 2
MODES = 6
BF = jnp.bfloat16
F32 = jnp.float32


def split2(v):
    hi = v.astype(BF)
    lo = (v - hi.astype(F32)).astype(BF)
    return hi, lo


def dot(a, b):
    return jnp.dot(a, b, preferred_element_type=F32)


def row_loop(rows, chunk, body):
    @pl.loop(0, rows // chunk)
    def _(t):
        body(pl.ds(pl.multiple_of(t * chunk, chunk), chunk))


def kernel(
    dims, gap, codes, flex, diri, modes, cmat, load, mult, res,
    stage, mats_hi, mats_lo, sel, sel_t, xs, xn, vn, state, total, gapc,
    cvec, vsrc, xrecv, comp, gath, part, redu, coef, cnb, rown, rnb, cblk,
    chi, clo, rstk, astk,
    mat_sem, s1, r1, s2, r2, s3, r3, s4, r4, s5, r5, s6, r6,
):
    Z, X, Y = dims
    ni, rhs = gap.shape
    cap = ni // 4
    nq, np_ = Z * CORES, X * Y
    i = lax.axis_index("sub")
    j = lax.axis_index("layer")
    z, x = i // X, i % X
    y, core = j // CORES, j % CORES
    q = z * CORES + core
    p = x * Y + y
    subs, layers = Z * X, Y * CORES
    has = (i > 0, i < subs - 1, j > 0, j < layers - 1)
    near = (
        (jnp.maximum(i - 1, 0), j),
        (jnp.minimum(i + 1, subs - 1), j),
        (i, jnp.maximum(j - 1, 0)),
        (i, jnp.minimum(j + 1, layers - 1)),
    )
    opp = (1, 0, 3, 2)

    def q_peer(t):
        return ((t // CORES) * X + x, y * CORES + t % CORES)

    def p_peer(t):
        return (z * X + t // Y, (t % Y) * CORES + core)

    loads = [
        pltpu.make_async_copy(flex, stage.at[0], mat_sem.at[0]),
        pltpu.make_async_copy(diri, stage.at[1], mat_sem.at[1]),
    ]
    for cp in loads:
        cp.start()

    cnb[...] = jnp.zeros_like(cnb)
    for d in range(4):
        @pl.when(jnp.logical_not(has[d]))
        def _():
            rnb[d] = jnp.zeros_like(rnb[d])

            @pl.loop(0, xrecv.shape[0])
            def _(k):
                xrecv[k, pl.ds(d * cap, cap), :] = jnp.zeros((cap, rhs), F32)

    barrier = pltpu.get_barrier_semaphore()

    def greet(device):
        pl.semaphore_signal(barrier, inc=1, device_id=device, device_id_type=MESH)

    @pl.loop(1, nq)
    def _(t):
        greet(q_peer((q + t) % nq))

    @pl.loop(1, np_)
    def _(t):
        greet(p_peer((p + t) % np_))

    count = nq + np_ - 2
    for d in range(4):
        @pl.when(has[d])
        def _():
            greet(near[d])

        count = count + has[d].astype(jnp.int32)

    code_row = codes[...]
    for b in range(ni // 128):
        block = slice(b * 128, b * 128 + 128)
        slot = lax.broadcasted_iota(jnp.int32, (128, ni), 0) + b * 128
        sel[block, :] = jnp.where(code_row == slot, 1.0, 0.0).astype(BF)
        column = jnp.broadcast_to(code_row[:, block].astype(F32), (128, 128)).T.astype(jnp.int32)
        for c in range(ni // 128):
            lane = lax.broadcasted_iota(jnp.int32, (128, 128), 1) + c * 128
            sel_t[block, c * 128 : c * 128 + 128] = jnp.where(column == lane, 1.0, 0.0).astype(BF)

    wide = jnp.concatenate([modes[...], jnp.zeros((16 - MODES, ni), F32)], axis=0)
    m1 = wide.astype(BF)
    m2, m3 = split2(wide - m1.astype(F32))
    in_slots = dot(m1, sel_t[...]) + dot(m2, sel_t[...]) + dot(m3, sel_t[...])
    rown[...] = in_slots[:8]
    own_hi = rown[...].astype(BF).astype(F32)
    rstk[...] = jnp.concatenate([own_hi, rown[...] - own_hi], axis=0).astype(BF)

    comp[0] = jnp.concatenate([load[...], jnp.zeros((8 - MODES, rhs), F32)], axis=0)

    pl.semaphore_wait(barrier, count)

    def remote(src, dst, send, recv, device):
        return pltpu.make_async_remote_copy(
            src_ref=src, dst_ref=dst, send_sem=send, recv_sem=recv,
            device_id=device, device_id_type=MESH,
        )

    def wait_bytes(ref, sem):
        pltpu.make_async_copy(ref, ref, sem).wait()

    def gather_start(k):
        gath[k, q] = comp[k]

        @pl.loop(1, nq)
        def _(t):
            remote(comp.at[k], gath.at[k, q], s1.at[k], r1.at[k], q_peer((q + t) % nq)).start()

    def near_copies(src_of, dst_of, send, recv, k):
        return [
            remote(src_of(d), dst_of(opp[d]), send.at[k, d], recv.at[k, opp[d]], near[d])
            for d in range(4)
        ]

    def near_start(copies):
        for d in range(4):
            @pl.when(has[d])
            def _():
                copies[d].start()

    def near_recv(dst_of, recv, k):
        for d in range(4):
            @pl.when(has[d])
            def _():
                wait_bytes(dst_of(d), recv.at[k, d])

    def near_sent(src_of, send, k):
        for d in range(4):
            @pl.when(has[d])
            def _():
                wait_bytes(src_of(d), send.at[k, d])

    def slots(ref, k, d):
        return ref.at[k, pl.ds(d * cap, cap), :]

    gather_start(0)
    near_start(near_copies(lambda d: rown, lambda d: rnb.at[d], s5, r5, 0))
    cblk[p] = cmat[p]

    @pl.loop(1, np_)
    def _(t):
        peer = (p + t) % np_
        remote(cmat.at[peer], cblk.at[p], s6.at[0], r6.at[0], p_peer(peer)).start()

    def split_mat(n):
        def body(rows):
            hi, lo = split2(stage[n, rows, :])
            mats_hi[n, rows, :] = hi
            mats_lo[n, rows, :] = lo

        row_loop(ni, 128, body)

    def put_pieces(rows, value, ref):
        hi, lo = split2(value)
        ref[rows, :rhs] = hi
        ref[rows, rhs:] = lo

    row_loop(ni, 128, lambda rows: put_pieces(rows, gap[rows, :], xs))

    def gap_body(rows):
        both = dot(sel[rows, :], xs[...])
        gapc[rows, :] = both[:, :rhs] + both[:, rhs:]

    row_loop(ni, 128, gap_body)
    loads[0].wait()
    split_mat(0)

    near_recv(lambda d: rnb.at[d], r5, 0)
    lane = lax.broadcasted_iota(jnp.int32, (8, ni), 1)
    parts = [rown[...]]
    for d in range(4):
        moved = pltpu.roll(rnb[d], ((d - opp[d]) * cap) % ni, 1)
        inside = (lane >= d * cap) & (lane < (d + 1) * cap)
        parts.append(jnp.where(inside, -moved, 0.0))
    acols = jnp.concatenate(parts, axis=0)
    a_hi = acols.astype(BF).astype(F32)
    acols = jnp.concatenate([a_hi, a_hi, acols - a_hi, jnp.zeros((8, ni), F32)], axis=0)
    for b in range(ni // 128):
        block = slice(b * 128, b * 128 + 128)
        astk[block, :] = acols[:, block].T.astype(BF)

    wait_bytes(cblk.at[pl.ds(0, np_ - 1)], r6.at[0])
    hi, lo = split2(cblk[...].reshape(np_ * 8, nq * 8))
    chi[...] = hi
    clo[...] = lo

    def coarse(k):
        wait_bytes(gath.at[k, pl.ds(0, nq - 1)], r1.at[k])
        g_hi, g_lo = split2(gath[k].reshape(nq * 8, rhs))
        out = dot(chi[...], g_hi) + (dot(chi[...], g_lo) + dot(clo[...], g_hi))
        part[k] = out.reshape(np_, 8, rhs)

        @pl.loop(1, np_)
        def _(t):
            peer = (p + t) % np_
            remote(part.at[k, peer], redu.at[k, p], s2.at[k], r2.at[k], p_peer(peer)).start()

        redu[k, p] = part[k, p]
        wait_bytes(redu.at[k, pl.ds(0, np_ - 1)], r2.at[k])
        coef[k] = jnp.sum(redu[k], axis=0)
        near_start(near_copies(lambda d: coef.at[k], lambda d: cnb.at[k, d], s3, r3, k))
        near_recv(lambda d: cnb.at[k, d], r3, k)
        c = jnp.concatenate([coef[k], cnb[k].reshape(32, rhs)], axis=0)
        c_hi = c.astype(BF).astype(F32)
        cvec[...] = jnp.concatenate(
            [c_hi, c - c_hi, c_hi, jnp.zeros((8, rhs), F32)], axis=0
        ).astype(BF)

    coarse(0)

    def start_body(rows):
        begin = dot(astk[rows, :], cvec[...])
        total[rows, :] = begin
        state[0, rows, :] = jnp.zeros_like(begin)
        state[1, rows, :] = jnp.zeros_like(begin)
        put_pieces(rows, begin, xs)

    row_loop(ni, 128, start_body)
    loads[1].wait()
    split_mat(1)

    @pl.loop(0, 5)
    def _(k):
        n = k % 2
        odd = n == 1

        def to_rows(rows):
            xn[rows, :] = dot(sel_t[rows, :], xs[...]).astype(BF)

        row_loop(ni, 128, to_rows)

        def multiply(rows):
            both = dot(mats_hi[n, rows, :], xn[...]) + dot(mats_lo[n, rows, :], xn[...])
            put_pieces(rows, both[:, :rhs] + both[:, rhs:], vn)

        row_loop(ni, 128, multiply)
        keep = jnp.where(k == 0, 1.0, 0.0)

        def to_slots(rows):
            both = dot(sel[rows, :], vn[...])
            vsrc[k, rows, :] = both[:, :rhs] + both[:, rhs:] - keep * gapc[rows, :]

        row_loop(ni, 128, to_slots)
        near_start(
            near_copies(lambda d: slots(vsrc, k, d), lambda d: slots(xrecv, k, d), s4, r4, k)
        )
        near_recv(lambda d: slots(xrecv, k, d), r4, k)
        row_loop(ni, 128, lambda rows: put_pieces(rows, vsrc[k, rows, :] - xrecv[k, rows, :], xs))
        comps = dot(rstk[...], xs[...])
        comp[k + 1] = comps[:8, :rhs] + (comps[:8, rhs:] + comps[8:, :rhs])
        gather_start(k + 1)
        coarse(k + 1)
        scale_old = jnp.where(odd, jnp.where(k == 1, 0.0, RHO1 * RHO0), 1.0)
        scale_new = jnp.where(odd, jnp.where(k == 1, 0.5 / THETA, RHO1 / DELTA), -1.0)
        share = jnp.where(odd, 1.0, 0.0)

        def update(rows):
            fresh = vsrc[k, rows, :] - xrecv[k, rows, :] - dot(astk[rows, :], cvec[...])
            value = scale_old * state[n, rows, :] + scale_new * fresh
            state[n, rows, :] = value
            total[rows, :] = total[rows, :] + share * value
            put_pieces(rows, value, xs)

        row_loop(ni, 128, update)

    def pieces_of_total(rows):
        put_pieces(rows, total[rows, :], xn)

    row_loop(ni, 128, pieces_of_total)

    def finish(rows):
        both = dot(sel_t[rows, :], xn[...])
        mult[rows, :] = both[:, :rhs] + both[:, rhs:]
        both = dot(sel_t[rows, :], xs[...])
        res[rows, :] = both[:, :rhs] + both[:, rhs:]

    row_loop(ni, 128, finish)

    near_sent(lambda d: rown, s5, 0)
    wait_bytes(cblk.at[pl.ds(0, np_ - 1)], s6.at[0])

    @pl.loop(0, 6)
    def _(k):
        wait_bytes(gath.at[k, pl.ds(0, nq - 1)], s1.at[k])
        wait_bytes(redu.at[k, pl.ds(0, np_ - 1)], s2.at[k])
        near_sent(lambda d: coef.at[k], s3, k)

    @pl.loop(0, 5)
    def _(k):
        near_sent(lambda d: slots(vsrc, k, d), s4, k)


def per_device(dims, local_gap, route_codes, flexibility, dirichlet, rigid_modes, coarse_inverse, rigid_load):
    Z, X, Y = dims
    ni, rhs = local_gap.shape[2:]
    nq, np_ = Z * CORES, X * Y
    cols = coarse_inverse.reshape(MODES, Z, X, Y, CORES, MODES).transpose(2, 3, 0, 1, 4, 5)
    cols = jnp.pad(cols, ((0, 0), (0, 0), (0, 2), (0, 0), (0, 0), (0, 2)))
    cmat = cols.reshape(np_, 8, nq * 8)
    vmem = pl.BlockSpec(memory_space=pltpu.VMEM)
    hbm = pl.BlockSpec(memory_space=pl.ANY)
    field = jax.ShapeDtypeStruct((ni, rhs), F32)
    dma = pltpu.SemaphoreType.DMA
    V = pltpu.VMEM
    mult, res = pl.pallas_call(
        functools.partial(kernel, dims),
        out_shape=(field, field),
        in_specs=[vmem, vmem, hbm, hbm, vmem, vmem, vmem],
        out_specs=(vmem, vmem),
        scratch_shapes=[
            V((2, ni, ni), F32), V((2, ni, ni), BF), V((2, ni, ni), BF),
            V((ni, ni), BF), V((ni, ni), BF),
            V((ni, 2 * rhs), BF), V((ni, 2 * rhs), BF), V((ni, 2 * rhs), BF),
            V((2, ni, rhs), F32), V((ni, rhs), F32), V((ni, rhs), F32),
            V((128, rhs), BF), V((5, ni, rhs), F32), V((5, ni, rhs), F32),
            V((6, 8, rhs), F32), V((6, nq, 8, rhs), F32),
            V((6, np_, 8, rhs), F32), V((6, np_, 8, rhs), F32),
            V((6, 8, rhs), F32), V((6, 4, 8, rhs), F32),
            V((8, ni), F32), V((4, 8, ni), F32), V((np_, 8, nq * 8), F32),
            V((np_ * 8, nq * 8), BF), V((np_ * 8, nq * 8), BF),
            V((16, ni), BF), V((ni, 128), BF),
            dma((2,)), dma((6,)), dma((6,)), dma((6,)), dma((6,)),
            dma((6, 4)), dma((6, 4)), dma((5, 4)), dma((5, 4)),
            dma((1, 4)), dma((1, 4)), dma((1,)), dma((1,)),
        ],
        compiler_params=pltpu.CompilerParams(
            collective_id=0, has_side_effects=True, vmem_limit_bytes=63 * 1024 * 1024
        ),
    )(
        local_gap[0, 0], route_codes[0], flexibility[0, 0], dirichlet[0, 0],
        rigid_modes[0, 0], cmat, rigid_load,
    )
    return mult[None, None], res[None, None]


def solution(mesh):
    placed = (
        P("sub", "layer", None, None),
        P("sub", "layer", None),
        P("sub", "layer", None, None),
        P("sub", "layer", None, None),
        P("sub", "layer", None, None),
        P(("sub", "layer"), None),
        P(("sub", "layer"), None),
    )
    subs, layers = mesh.shape["sub"], mesh.shape["layer"]
    across = 4 if subs % 4 == 0 and subs > 4 else 2
    dims = (subs // across, across, layers // CORES)
    return jax.shard_map(
        functools.partial(per_device, dims),
        mesh=mesh,
        in_specs=placed,
        out_specs=(P("sub", "layer", None, None), P("sub", "layer", None, None)),
        check_vma=False,
    )
```

```python
import functools

import jax
import jax.numpy as jnp
from jax import lax
from jax.experimental import pallas as pl
from jax.experimental.pallas import tpu as pltpu
from jax.sharding import PartitionSpec as P

MESH = pl.DeviceIdType.MESH
THETA = 4.25
DELTA = 3.75
SIGMA = THETA / DELTA
RHO0 = DELTA / THETA
RHO1 = 1.0 / (2.0 * SIGMA - RHO0)
CORES = 2
MODES = 6
BF = jnp.bfloat16
F32 = jnp.float32
CHUNK = 384


def split2(v):
    hi = v.astype(BF)
    lo = (v - hi.astype(F32)).astype(BF)
    return hi, lo


def dot(a, b):
    return jnp.dot(a, b, preferred_element_type=F32)


def row_loop(rows, chunk, body):
    chunk = min(chunk, rows)

    @pl.loop(0, rows // chunk)
    def _(t):
        body(pl.ds(pl.multiple_of(t * chunk, chunk), chunk))


def kernel(
    dims, gap, codes, flex, diri, modes, cmat, load, mult, res,
    stage, mats_hi, mats_lo, sel, sel_t, xs, xn, xa, vn, state, total, ahead,
    wide_w, mstk, cvec, vsrc, xrecv, comp, gath, part, redu, coef, cnb, rown, rnb, cblk,
    chi, clo, rstk, astk,
    mat_sem, s1, r1, s2, r2, s3, r3, s4, r4, s5, r5, s6, r6,
):
    Z, X, Y = dims
    ni, rhs = gap.shape
    cap = ni // 4
    nq, np_ = Z * CORES, X * Y
    i = lax.axis_index("sub")
    j = lax.axis_index("layer")
    z, x = i // X, i % X
    y, core = j // CORES, j % CORES
    q = z * CORES + core
    p = x * Y + y
    subs, layers = Z * X, Y * CORES
    has = (i > 0, i < subs - 1, j > 0, j < layers - 1)
    near = (
        (jnp.maximum(i - 1, 0), j),
        (jnp.minimum(i + 1, subs - 1), j),
        (i, jnp.maximum(j - 1, 0)),
        (i, jnp.minimum(j + 1, layers - 1)),
    )
    opp = (1, 0, 3, 2)

    def q_peer(t):
        return ((t // CORES) * X + x, y * CORES + t % CORES)

    def p_peer(t):
        return (z * X + t // Y, (t % Y) * CORES + core)

    loads = [
        pltpu.make_async_copy(flex, stage.at[0], mat_sem.at[0]),
        pltpu.make_async_copy(diri, stage.at[1], mat_sem.at[1]),
    ]
    for cp in loads:
        cp.start()

    cnb[...] = jnp.zeros_like(cnb)
    for d in range(4):
        @pl.when(jnp.logical_not(has[d]))
        def _():
            rnb[d] = jnp.zeros_like(rnb[d])

            @pl.loop(0, xrecv.shape[0])
            def _(k):
                xrecv[k, pl.ds(d * cap, cap), :] = jnp.zeros((cap, rhs), F32)

    barrier = pltpu.get_barrier_semaphore()

    def greet(device):
        pl.semaphore_signal(barrier, inc=1, device_id=device, device_id_type=MESH)

    @pl.loop(1, nq)
    def _(t):
        greet(q_peer((q + t) % nq))

    @pl.loop(1, np_)
    def _(t):
        greet(p_peer((p + t) % np_))

    count = nq + np_ - 2
    for d in range(4):
        @pl.when(has[d])
        def _():
            greet(near[d])

        count = count + has[d].astype(jnp.int32)

    code_row = codes[...]
    for b in range(ni // 128):
        block = slice(b * 128, b * 128 + 128)
        slot = lax.broadcasted_iota(jnp.int32, (128, ni), 0) + b * 128
        sel[block, :] = jnp.where(code_row == slot, 1.0, 0.0).astype(BF)
        column = jnp.broadcast_to(code_row[:, block].astype(F32), (128, 128)).T.astype(jnp.int32)
        for c in range(ni // 128):
            lane = lax.broadcasted_iota(jnp.int32, (128, 128), 1) + c * 128
            sel_t[block, c * 128 : c * 128 + 128] = jnp.where(column == lane, 1.0, 0.0).astype(BF)

    wide = jnp.concatenate([modes[...], jnp.zeros((16 - MODES, ni), F32)], axis=0)
    m1 = wide.astype(BF)
    m2, m3 = split2(wide - m1.astype(F32))
    in_slots = dot(m1, sel_t[...]) + dot(m2, sel_t[...]) + dot(m3, sel_t[...])
    rown[...] = in_slots[:8]
    own_hi = rown[...].astype(BF).astype(F32)
    rstk[...] = jnp.concatenate([own_hi, rown[...] - own_hi], axis=0).astype(BF)

    comp[0] = jnp.concatenate([load[...], jnp.zeros((8 - MODES, rhs), F32)], axis=0)

    pl.semaphore_wait(barrier, count)

    def remote(src, dst, send, recv, device):
        return pltpu.make_async_remote_copy(
            src_ref=src, dst_ref=dst, send_sem=send, recv_sem=recv,
            device_id=device, device_id_type=MESH,
        )

    def wait_bytes(ref, sem):
        pltpu.make_async_copy(ref, ref, sem).wait()

    def gather_start(k):
        gath[k, q] = comp[k]

        @pl.loop(1, nq)
        def _(t):
            remote(comp.at[k], gath.at[k, q], s1.at[k], r1.at[k], q_peer((q + t) % nq)).start()

    def near_copies(src_of, dst_of, send, recv, k):
        return [
            remote(src_of(d), dst_of(opp[d]), send.at[k, d], recv.at[k, opp[d]], near[d])
            for d in range(4)
        ]

    def near_start(copies):
        for d in range(4):
            @pl.when(has[d])
            def _():
                copies[d].start()

    def near_recv(dst_of, recv, k):
        for d in range(4):
            @pl.when(has[d])
            def _():
                wait_bytes(dst_of(d), recv.at[k, d])

    def near_sent(src_of, send, k):
        for d in range(4):
            @pl.when(has[d])
            def _():
                wait_bytes(src_of(d), send.at[k, d])

    def slots(ref, k, d):
        return ref.at[k, pl.ds(d * cap, cap), :]

    gather_start(0)
    near_start(near_copies(lambda d: rown, lambda d: rnb.at[d], s5, r5, 0))
    cblk[p] = cmat[p]

    @pl.loop(1, np_)
    def _(t):
        peer = (p + t) % np_
        remote(cmat.at[peer], cblk.at[p], s6.at[0], r6.at[0], p_peer(peer)).start()

    whole = pl.ds(0, ni)

    def split_mat(n):
        loads[n].wait()

        def body(rows):
            hi, lo = split2(stage[n, rows, :])
            mats_hi[n, rows, :] = hi
            mats_lo[n, rows, :] = lo

        row_loop(ni, 128, body)

    def put_pieces(rows, value, ref):
        hi, lo = split2(value)
        ref[rows, :rhs] = hi
        ref[rows, rhs:] = lo

    def both_halves(both):
        return both[:, :rhs] + both[:, rhs:]

    def to_rows(src, dst):
        dst[...] = dot(sel_t[...], src[...]).astype(BF)

    def multiply(n, src):
        both = dot(mats_hi[n], src[...]) + dot(mats_lo[n], src[...])
        put_pieces(whole, both_halves(both), vn)

    def to_slots():
        return both_halves(dot(sel[...], vn[...]))

    row_loop(ni, CHUNK, lambda rows: put_pieces(rows, gap[rows, :], vn))
    ahead[...] = -to_slots()
    split_mat(0)

    near_recv(lambda d: rnb.at[d], r5, 0)
    lane = lax.broadcasted_iota(jnp.int32, (8, ni), 1)
    parts = [rown[...]]
    for d in range(4):
        moved = pltpu.roll(rnb[d], ((d - opp[d]) * cap) % ni, 1)
        inside = (lane >= d * cap) & (lane < (d + 1) * cap)
        parts.append(jnp.where(inside, -moved, 0.0))
    acols = jnp.concatenate(parts + [jnp.zeros((88, ni), F32)], axis=0)

    def stacked(rows, cols, out):
        hi = cols.astype(BF).astype(F32)
        low = cols - hi
        out[rows, :] = (hi + pltpu.roll(hi, 40, 1) + pltpu.roll(low, 80, 1)).astype(BF)

    for b in range(ni // 128):
        block = slice(b * 128, b * 128 + 128)
        cols = acols[:, block].T
        stacked(block, cols, astk)
        put_pieces(block, cols, xs)

    to_rows(xs, xa)
    wait_bytes(cblk.at[pl.ds(0, np_ - 1)], r6.at[0])
    hi, lo = split2(cblk[...].reshape(np_ * 8, nq * 8))
    chi[...] = hi
    clo[...] = lo

    def coarse_scatter(k):
        wait_bytes(gath.at[k, pl.ds(0, nq - 1)], r1.at[k])
        g_hi, g_lo = split2(gath[k].reshape(nq * 8, rhs))
        out = dot(chi[...], g_hi) + (dot(chi[...], g_lo) + dot(clo[...], g_hi))
        part[k] = out.reshape(np_, 8, rhs)

        @pl.loop(1, np_)
        def _(t):
            peer = (p + t) % np_
            remote(part.at[k, peer], redu.at[k, p], s2.at[k], r2.at[k], p_peer(peer)).start()

        redu[k, p] = part[k, p]

    def coarse_finish(k):
        wait_bytes(redu.at[k, pl.ds(0, np_ - 1)], r2.at[k])
        coef[k] = jnp.sum(redu[k], axis=0)
        near_start(near_copies(lambda d: coef.at[k], lambda d: cnb.at[k, d], s3, r3, k))
        near_recv(lambda d: cnb.at[k, d], r3, k)
        c = jnp.concatenate([coef[k], cnb[k].reshape(32, rhs)], axis=0)
        c_hi = c.astype(BF).astype(F32)
        cvec[...] = jnp.concatenate(
            [c_hi, c - c_hi, c_hi, jnp.zeros((8, rhs), F32)], axis=0
        ).astype(BF)

    def settle(n, last_new):
        share = jnp.where(n == 1, 1.0, 0.0)
        value = wide_w[...] + last_new * dot(astk[...], cvec[...])
        state[n] = value
        total[...] = total[...] + share * value

    coarse_scatter(0)
    multiply(0, xa)
    stacked(whole, to_slots(), mstk.at[0])
    state[...] = jnp.zeros_like(state)
    coarse_finish(0)

    @pl.loop(0, 5)
    def _(k):
        n = k % 2
        odd = n == 1
        last_new = jnp.where(odd, 1.0, jnp.where(k == 0, 1.0, jnp.where(k == 2, -0.5 / THETA, -RHO1 / DELTA)))
        vsrc[k] = ahead[...] + last_new * dot(mstk[n], cvec[...])
        near_start(
            near_copies(lambda d: slots(vsrc, k, d), lambda d: slots(xrecv, k, d), s4, r4, k)
        )

        @pl.when(k == 0)
        def _():
            total[...] = dot(astk[...], cvec[...])
            split_mat(1)
            multiply(1, xa)
            stacked(whole, to_slots(), mstk.at[1])

        @pl.when(k > 0)
        def _():
            settle(1 - n, last_new)

        near_recv(lambda d: slots(xrecv, k, d), r4, k)
        scale_old = jnp.where(odd, jnp.where(k == 1, 0.0, RHO1 * RHO0), 1.0)
        scale_new = jnp.where(odd, jnp.where(k == 1, 0.5 / THETA, RHO1 / DELTA), -1.0)

        def fresh(rows):
            y = vsrc[k, rows, :] - xrecv[k, rows, :]
            put_pieces(rows, y, xs)
            wide_w[rows, :] = scale_old * state[n, rows, :] + scale_new * y

        row_loop(ni, CHUNK, fresh)
        comps = dot(rstk[...], xs[...])
        comp[k + 1] = comps[:8, :rhs] + (comps[:8, rhs:] + comps[8:, :rhs])
        gather_start(k + 1)

        @pl.when(k < 4)
        def _():
            row_loop(ni, CHUNK, lambda rows: put_pieces(rows, wide_w[rows, :], xs))
            to_rows(xs, xn)
            multiply(1 - n, xn)

        coarse_scatter(k + 1)

        @pl.when(k < 4)
        def _():
            ahead[...] = to_slots()

        coarse_finish(k + 1)

    settle(0, 1.0)
    row_loop(ni, CHUNK, lambda rows: put_pieces(rows, total[rows, :], xn))
    row_loop(ni, CHUNK, lambda rows: put_pieces(rows, state[0, rows, :], xs))
    mult[...] = both_halves(dot(sel_t[...], xn[...]))
    res[...] = both_halves(dot(sel_t[...], xs[...]))

    near_sent(lambda d: rown, s5, 0)
    wait_bytes(cblk.at[pl.ds(0, np_ - 1)], s6.at[0])

    @pl.loop(0, 6)
    def _(k):
        wait_bytes(gath.at[k, pl.ds(0, nq - 1)], s1.at[k])
        wait_bytes(redu.at[k, pl.ds(0, np_ - 1)], s2.at[k])
        near_sent(lambda d: coef.at[k], s3, k)

    @pl.loop(0, 5)
    def _(k):
        near_sent(lambda d: slots(vsrc, k, d), s4, k)


def per_device(dims, local_gap, route_codes, flexibility, dirichlet, rigid_modes, coarse_inverse, rigid_load):
    Z, X, Y = dims
    ni, rhs = local_gap.shape[2:]
    nq, np_ = Z * CORES, X * Y
    cols = coarse_inverse.reshape(MODES, Z, X, Y, CORES, MODES).transpose(2, 3, 0, 1, 4, 5)
    cols = jnp.pad(cols, ((0, 0), (0, 0), (0, 2), (0, 0), (0, 0), (0, 2)))
    cmat = cols.reshape(np_, 8, nq * 8)
    vmem = pl.BlockSpec(memory_space=pltpu.VMEM)
    hbm = pl.BlockSpec(memory_space=pl.ANY)
    field = jax.ShapeDtypeStruct((ni, rhs), F32)
    dma = pltpu.SemaphoreType.DMA
    V = pltpu.VMEM
    mult, res = pl.pallas_call(
        functools.partial(kernel, dims),
        out_shape=(field, field),
        in_specs=[vmem, vmem, hbm, hbm, vmem, vmem, vmem],
        out_specs=(vmem, vmem),
        scratch_shapes=[
            V((2, ni, ni), F32), V((2, ni, ni), BF), V((2, ni, ni), BF),
            V((ni, ni), BF), V((ni, ni), BF),
            V((ni, 2 * rhs), BF), V((ni, 2 * rhs), BF), V((ni, 2 * rhs), BF),
            V((ni, 2 * rhs), BF), V((2, ni, rhs), F32), V((ni, rhs), F32),
            V((ni, rhs), F32), V((ni, rhs), F32), V((2, ni, 128), BF),
            V((128, rhs), BF), V((5, ni, rhs), F32), V((5, ni, rhs), F32),
            V((6, 8, rhs), F32), V((6, nq, 8, rhs), F32),
            V((6, np_, 8, rhs), F32), V((6, np_, 8, rhs), F32),
            V((6, 8, rhs), F32), V((6, 4, 8, rhs), F32),
            V((8, ni), F32), V((4, 8, ni), F32), V((np_, 8, nq * 8), F32),
            V((np_ * 8, nq * 8), BF), V((np_ * 8, nq * 8), BF),
            V((16, ni), BF), V((ni, 128), BF),
            dma((2,)), dma((6,)), dma((6,)), dma((6,)), dma((6,)),
            dma((6, 4)), dma((6, 4)), dma((5, 4)), dma((5, 4)),
            dma((1, 4)), dma((1, 4)), dma((1,)), dma((1,)),
        ],
        compiler_params=pltpu.CompilerParams(
            collective_id=0, has_side_effects=True, vmem_limit_bytes=63 * 1024 * 1024
        ),
    )(
        local_gap[0, 0], route_codes[0], flexibility[0, 0], dirichlet[0, 0],
        rigid_modes[0, 0], cmat, rigid_load,
    )
    return mult[None, None], res[None, None]


def solution(mesh):
    placed = (
        P("sub", "layer", None, None),
        P("sub", "layer", None),
        P("sub", "layer", None, None),
        P("sub", "layer", None, None),
        P("sub", "layer", None, None),
        P(("sub", "layer"), None),
        P(("sub", "layer"), None),
    )
    subs, layers = mesh.shape["sub"], mesh.shape["layer"]
    across = 4 if subs % 4 == 0 and subs > 4 else 2
    dims = (subs // across, across, layers // CORES)
    return jax.shard_map(
        functools.partial(per_device, dims),
        mesh=mesh,
        in_specs=placed,
        out_specs=(P("sub", "layer", None, None), P("sub", "layer", None, None)),
        check_vma=False,
    )
```

```python
import functools

import jax
import jax.numpy as jnp
from jax import lax
from jax.experimental import pallas as pl
from jax.experimental.pallas import tpu as pltpu
from jax.sharding import PartitionSpec as P

MESH = pl.DeviceIdType.MESH
THETA = 4.25
DELTA = 3.75
SIGMA = THETA / DELTA
RHO0 = DELTA / THETA
RHO1 = 1.0 / (2.0 * SIGMA - RHO0)
CORES = 2
MODES = 6
BF = jnp.bfloat16
F32 = jnp.float32
CHUNK = 384
OFFSETS = [
    (0, 0), (-1, 0), (1, 0), (0, -1), (0, 1), (-2, 0), (2, 0),
    (0, -2), (0, 2), (-1, -1), (-1, 1), (1, -1), (1, 1),
]


def split2(v):
    hi = v.astype(BF)
    lo = (v - hi.astype(F32)).astype(BF)
    return hi, lo


def dot(a, b):
    return jnp.dot(a, b, preferred_element_type=F32)


def row_loop(rows, chunk, body):
    chunk = min(chunk, rows)

    @pl.loop(0, rows // chunk)
    def _(t):
        body(pl.ds(pl.multiple_of(t * chunk, chunk), chunk))


def kernel(
    dims, gap, codes, flex, diri, modes, cmat, load, mult, res,
    stage, mats_hi, mats_lo, sel, sel_t, xs, xn, xa, vn, state, total, ahead,
    wide_w, mstk, cvec, vsrc, xrecv, comp, gath, part, redu, coef, call, rown, rnb, cblk,
    chi, clo, astk, arow, anat, bstk, tsend, tnb, kstk, psend, pnb,
    mat_sem, s1, r1, s2, r2, s3, r3, s4, r4, s5, r5, s6, r6, s7, r7, s8, r8,
):
    Z, X, Y = dims
    ni, rhs = gap.shape
    cap = ni // 4
    nq, np_ = Z * CORES, X * Y
    i = lax.axis_index("sub")
    j = lax.axis_index("layer")
    z, x = i // X, i % X
    y, core = j // CORES, j % CORES
    q = z * CORES + core
    p = x * Y + y
    subs, layers = Z * X, Y * CORES
    opp = (1, 0, 3, 2)

    def inside(di, dj):
        checks = []
        if di:
            checks.append(i + di >= 0 if di < 0 else i + di < subs)
        if dj:
            checks.append(j + dj >= 0 if dj < 0 else j + dj < layers)
        return checks[0] if len(checks) == 1 else jnp.logical_and(*checks)

    def clipped(di, dj):
        return (jnp.clip(i + di, 0, subs - 1), jnp.clip(j + dj, 0, layers - 1))

    has = [None] + [inside(*o) for o in OFFSETS[1:]]
    away = [None] + [clipped(*o) for o in OFFSETS[1:]]
    back = [OFFSETS.index((-o[0], -o[1])) for o in OFFSETS]
    far = len(OFFSETS)

    def q_peer(t):
        return ((t // CORES) * X + x, y * CORES + t % CORES)

    def p_peer(t):
        return (z * X + t // Y, (t % Y) * CORES + core)

    loads = [
        pltpu.make_async_copy(flex, stage.at[0], mat_sem.at[0]),
        pltpu.make_async_copy(diri, stage.at[1], mat_sem.at[1]),
    ]
    for cp in loads:
        cp.start()

    call[...] = jnp.zeros_like(call)
    pnb[...] = jnp.zeros_like(pnb)
    tnb[...] = jnp.zeros_like(tnb)
    for d in range(4):
        @pl.when(jnp.logical_not(has[d + 1]))
        def _():
            rnb[d] = jnp.zeros_like(rnb[d])

            @pl.loop(0, xrecv.shape[0])
            def _(k):
                xrecv[k, pl.ds(d * cap, cap), :] = jnp.zeros((cap, rhs), F32)

    barrier = pltpu.get_barrier_semaphore()

    def greet(device):
        pl.semaphore_signal(barrier, inc=1, device_id=device, device_id_type=MESH)

    @pl.loop(1, nq)
    def _(t):
        greet(q_peer((q + t) % nq))

    @pl.loop(1, np_)
    def _(t):
        greet(p_peer((p + t) % np_))

    count = nq + np_ - 2
    for o in range(1, far):
        @pl.when(has[o])
        def _():
            greet(away[o])

        count = count + has[o].astype(jnp.int32)

    code_row = codes[...]
    for b in range(ni // 128):
        block = slice(b * 128, b * 128 + 128)
        slot = lax.broadcasted_iota(jnp.int32, (128, ni), 0) + b * 128
        sel[block, :] = jnp.where(code_row == slot, 1.0, 0.0).astype(BF)
        column = jnp.broadcast_to(code_row[:, block].astype(F32), (128, 128)).T.astype(jnp.int32)
        for c in range(ni // 128):
            lane = lax.broadcasted_iota(jnp.int32, (128, 128), 1) + c * 128
            sel_t[block, c * 128 : c * 128 + 128] = jnp.where(column == lane, 1.0, 0.0).astype(BF)

    wide = jnp.concatenate([modes[...], jnp.zeros((16 - MODES, ni), F32)], axis=0)
    m1 = wide.astype(BF)
    m2, m3 = split2(wide - m1.astype(F32))
    pieces = dot(jnp.concatenate([m1, m2, m3], axis=0), sel_t[...])
    rown[...] = pieces[:8] + (pieces[16:24] + pieces[32:40])

    comp[0] = jnp.concatenate([load[...], jnp.zeros((8 - MODES, rhs), F32)], axis=0)

    pl.semaphore_wait(barrier, count)

    def remote(src, dst, send, recv, device):
        return pltpu.make_async_remote_copy(
            src_ref=src, dst_ref=dst, send_sem=send, recv_sem=recv,
            device_id=device, device_id_type=MESH,
        )

    def wait_bytes(ref, sem):
        pltpu.make_async_copy(ref, ref, sem).wait()

    def gather_start(k):
        gath[k, q] = comp[k]

        @pl.loop(1, nq)
        def _(t):
            remote(comp.at[k], gath.at[k, q], s1.at[k], r1.at[k], q_peer((q + t) % nq)).start()

    def near_start(src_of, dst_of, send, recv, k, many=5):
        for o in range(1, many):
            @pl.when(has[o])
            def _():
                remote(src_of(o), dst_of(back[o]), send.at[k, o], recv.at[k, back[o]], away[o]).start()

    def near_wait(ref_of, sem, k, many=5):
        for o in range(1, many):
            @pl.when(has[o])
            def _():
                wait_bytes(ref_of(o), sem.at[k, o])

    def slots(ref, k):
        return lambda o: ref.at[k, pl.ds((o - 1) * cap, cap), :]

    def rows8(ref, k):
        return lambda o: ref.at[k, pl.ds(8 * o, 8), :]

    gather_start(0)
    near_start(lambda o: rown, lambda o: rnb.at[o - 1], s5, r5, 0)
    cblk[p] = cmat[p]

    @pl.loop(1, np_)
    def _(t):
        peer = (p + t) % np_
        remote(cmat.at[peer], cblk.at[p], s6.at[0], r6.at[0], p_peer(peer)).start()

    whole = pl.ds(0, ni)

    def split_mat(n):
        loads[n].wait()

        def body(rows):
            hi, lo = split2(stage[n, rows, :])
            mats_hi[n, rows, :] = hi
            mats_lo[n, rows, :] = lo

        row_loop(ni, 128, body)

    def put_pieces(rows, value, ref):
        hi, lo = split2(value)
        ref[rows, :rhs] = hi
        ref[rows, rhs:] = lo

    def both_halves(both):
        return both[:, :rhs] + both[:, rhs:]

    def to_rows(src, dst):
        dst[...] = dot(sel_t[...], src[...]).astype(BF)

    def multiply(n, src):
        both = dot(mats_hi[n], src[...]) + dot(mats_lo[n], src[...])
        put_pieces(whole, both_halves(both), vn)

    def to_slots():
        return both_halves(dot(sel[...], vn[...]))

    def tall_pieces(value):
        hi = value.astype(BF)
        return jnp.concatenate([hi, (value - hi.astype(F32)).astype(BF)], axis=0)

    def skinny(lhs, rhs_pieces):
        out = dot(lhs, rhs_pieces)
        return out[:48, :rhs] + (out[:48, rhs:] + out[48:, :rhs])

    row_loop(ni, CHUNK, lambda rows: put_pieces(rows, gap[rows, :], vn))
    ahead[...] = -to_slots()
    split_mat(0)

    near_wait(lambda o: rnb.at[o - 1], r5, 0)
    lane = lax.broadcasted_iota(jnp.int32, (8, ni), 1)
    parts = [rown[...]]
    for d in range(4):
        moved = pltpu.roll(rnb[d], ((d - opp[d]) * cap) % ni, 1)
        live = (lane >= d * cap) & (lane < (d + 1) * cap)
        parts.append(jnp.where(live, -moved, 0.0))
    acols = jnp.concatenate(parts + [jnp.zeros((88, ni), F32)], axis=0)

    def stacked(cols):
        hi = cols.astype(BF).astype(F32)
        low = cols - hi
        return (hi + pltpu.roll(hi, 40, 1) + pltpu.roll(low, 80, 1)).astype(BF)

    arow[...] = tall_pieces(acols[:48])
    for b in range(ni // 128):
        block = slice(b * 128, b * 128 + 128)
        cols = acols[:, block].T
        astk[block, :] = stacked(cols)
        put_pieces(block, cols, xs)

    to_rows(xs, xa)

    def partial_start(k, lhs, pieces):
        psend[k] = skinny(lhs, pieces)
        near_start(rows8(psend, k), rows8(pnb, k), s7, r7, k)

    row_loop(ni, CHUNK, lambda rows: put_pieces(rows, ahead[rows, :], xs))
    partial_start(0, arow[...], xs[...])
    wait_bytes(cblk.at[pl.ds(0, np_ - 1)], r6.at[0])
    hi, lo = split2(cblk[...].reshape(np_ * 8, nq * 8))
    chi[...] = hi
    clo[...] = lo

    def coarse_scatter(k):
        wait_bytes(gath.at[k, pl.ds(0, nq - 1)], r1.at[k])
        g_hi, g_lo = split2(gath[k].reshape(nq * 8, rhs))
        out = dot(chi[...], g_hi) + (dot(chi[...], g_lo) + dot(clo[...], g_hi))
        part[k] = out.reshape(np_, 8, rhs)

        @pl.loop(1, np_)
        def _(t):
            peer = (p + t) % np_
            remote(part.at[k, peer], redu.at[k, p], s2.at[k], r2.at[k], p_peer(peer)).start()

        redu[k, p] = part[k, p]

    def coarse_finish(k):
        wait_bytes(redu.at[k, pl.ds(0, np_ - 1)], r2.at[k])
        coef[k] = jnp.sum(redu[k], axis=0)
        near_start(lambda o: coef.at[k], lambda o: call.at[k, o], s3, r3, k, far)

    def around(k, base):
        picks = []
        for step in OFFSETS[:5]:
            o = OFFSETS.index((base[0] + step[0], base[1] + step[1]))
            picks.append(coef[k] if o == 0 else call[k, o])
        c = jnp.concatenate(picks, axis=0)
        c_hi = c.astype(BF).astype(F32)
        return jnp.concatenate(
            [c_hi, c - c_hi, c_hi, jnp.zeros((8, rhs), F32)], axis=0
        ).astype(BF)

    def prepare(n):
        multiply(n, xa)
        cols = to_slots()
        mstk[n] = stacked(cols)
        put_pieces(whole, cols, vn)
        tsend[n] = skinny(arow[...], vn[...])
        near_start(rows8(tsend, n), rows8(tnb, n), s8, r8, n)

    def prepare_end(n):
        near_wait(rows8(tnb, n), r8, n)
        for o in range(5):
            block = tsend[n, 0:8, :] if o == 0 else tnb[n, 8 * o : 8 * o + 8, :]
            kstk[n, :, o * 128 : o * 128 + 128] = stacked(
                jnp.concatenate([block, jnp.zeros((8, 128), F32)], axis=0)
            )

    def prepare_rows(n):
        out = dot(anat[...], mats_hi[n])
        out = out[:48] + out[48:] + dot(anat[:48, :], mats_lo[n])
        out = dot(tall_pieces(out), sel_t[...])
        bstk[n] = tall_pieces(out[:48] + out[48:])

    def settle(n, last_new):
        share = jnp.where(n == 1, 1.0, 0.0)
        value = wide_w[...] + last_new * dot(astk[...], cvec[...])
        state[n] = value
        total[...] = total[...] + share * value

    coarse_scatter(0)
    prepare(0)
    state[...] = jnp.zeros_like(state)
    coarse_finish(0)
    split_mat(1)
    anat[...] = dot(arow[...], sel[...]).astype(BF)
    prepare_rows(1)
    prepare_end(0)

    @pl.loop(0, 5)
    def _(k):
        n = k % 2
        odd = n == 1
        last_new = jnp.where(odd | (k == 0), 1.0, jnp.where(k == 2, -0.5 / THETA, -RHO1 / DELTA))

        @pl.when(k > 0)
        def _():
            ahead[...] = to_slots()

        near_wait(lambda o: call.at[k, o], r3, k, far)
        near_wait(rows8(pnb, k), r7, k)
        hood = [around(k, o) for o in OFFSETS[:5]]
        cvec[...] = hood[0]
        early = psend[k, 0:8, :]
        for o in range(1, 5):
            early = early + pnb[k, 8 * o : 8 * o + 8, :]
        moved = dot(kstk[n], jnp.concatenate(hood, axis=0))
        comp[k + 1] = early + last_new * moved[:8]
        gather_start(k + 1)
        vsrc[k] = ahead[...] + last_new * dot(mstk[n], cvec[...])
        near_start(slots(vsrc, k), slots(xrecv, k), s4, r4, k)

        @pl.when(k == 0)
        def _():
            total[...] = dot(astk[...], cvec[...])
            prepare(1)

        @pl.when(k > 0)
        def _():
            settle(1 - n, last_new)

        @pl.when(k == 1)
        def _():
            prepare_rows(0)

        coarse_scatter(k + 1)
        near_wait(slots(xrecv, k), r4, k)
        scale_old = jnp.where(odd, jnp.where(k == 1, 0.0, RHO1 * RHO0), 1.0)
        scale_new = jnp.where(odd, jnp.where(k == 1, 0.5 / THETA, RHO1 / DELTA), -1.0)

        def fresh(rows):
            jumped = vsrc[k, rows, :] - xrecv[k, rows, :]
            w = scale_old * state[n, rows, :] + scale_new * jumped
            wide_w[rows, :] = w
            put_pieces(rows, w, xs)

        row_loop(ni, CHUNK, fresh)

        @pl.when(k < 4)
        def _():
            partial_start(k + 1, bstk[1 - n], xs[...])
            to_rows(xs, xn)
            multiply(1 - n, xn)

        coarse_finish(k + 1)

        @pl.when(k == 0)
        def _():
            prepare_end(1)

    near_wait(lambda o: call.at[5, o], r3, 5, far)
    cvec[...] = around(5, (0, 0))
    settle(0, 1.0)
    row_loop(ni, CHUNK, lambda rows: put_pieces(rows, total[rows, :], xn))
    row_loop(ni, CHUNK, lambda rows: put_pieces(rows, state[0, rows, :], xs))
    mult[...] = both_halves(dot(sel_t[...], xn[...]))
    res[...] = both_halves(dot(sel_t[...], xs[...]))

    near_wait(lambda o: rown, s5, 0)
    wait_bytes(cblk.at[pl.ds(0, np_ - 1)], s6.at[0])
    for n in range(2):
        near_wait(rows8(tsend, n), s8, n)

    @pl.loop(0, 6)
    def _(k):
        wait_bytes(gath.at[k, pl.ds(0, nq - 1)], s1.at[k])
        wait_bytes(redu.at[k, pl.ds(0, np_ - 1)], s2.at[k])
        near_wait(lambda o: coef.at[k], s3, k, far)

    @pl.loop(0, 5)
    def _(k):
        near_wait(slots(vsrc, k), s4, k)
        near_wait(rows8(psend, k), s7, k)


def per_device(dims, local_gap, route_codes, flexibility, dirichlet, rigid_modes, coarse_inverse, rigid_load):
    Z, X, Y = dims
    ni, rhs = local_gap.shape[2:]
    nq, np_ = Z * CORES, X * Y
    cols = coarse_inverse.reshape(MODES, Z, X, Y, CORES, MODES).transpose(2, 3, 0, 1, 4, 5)
    cols = jnp.pad(cols, ((0, 0), (0, 0), (0, 2), (0, 0), (0, 0), (0, 2)))
    cmat = cols.reshape(np_, 8, nq * 8)
    far = len(OFFSETS)
    vmem = pl.BlockSpec(memory_space=pltpu.VMEM)
    hbm = pl.BlockSpec(memory_space=pl.ANY)
    field = jax.ShapeDtypeStruct((ni, rhs), F32)
    dma = pltpu.SemaphoreType.DMA
    V = pltpu.VMEM
    mult, res = pl.pallas_call(
        functools.partial(kernel, dims),
        out_shape=(field, field),
        in_specs=[vmem, vmem, hbm, hbm, vmem, vmem, vmem],
        out_specs=(vmem, vmem),
        scratch_shapes=[
            V((2, ni, ni), F32), V((2, ni, ni), BF), V((2, ni, ni), BF),
            V((ni, ni), BF), V((ni, ni), BF),
            V((ni, 2 * rhs), BF), V((ni, 2 * rhs), BF), V((ni, 2 * rhs), BF),
            V((ni, 2 * rhs), BF), V((2, ni, rhs), F32), V((ni, rhs), F32),
            V((ni, rhs), F32), V((ni, rhs), F32), V((2, ni, 128), BF),
            V((128, rhs), BF), V((5, ni, rhs), F32), V((5, ni, rhs), F32),
            V((6, 8, rhs), F32), V((6, nq, 8, rhs), F32),
            V((6, np_, 8, rhs), F32), V((6, np_, 8, rhs), F32),
            V((6, 8, rhs), F32), V((6, far, 8, rhs), F32),
            V((8, ni), F32), V((4, 8, ni), F32), V((np_, 8, nq * 8), F32),
            V((np_ * 8, nq * 8), BF), V((np_ * 8, nq * 8), BF), V((ni, 128), BF),
            V((96, ni), BF), V((96, ni), BF), V((2, 96, ni), BF),
            V((2, 48, rhs), F32), V((2, 40, rhs), F32), V((2, 16, 640), BF),
            V((5, 48, rhs), F32), V((5, 40, rhs), F32),
            dma((2,)), dma((6,)), dma((6,)), dma((6,)), dma((6,)),
            dma((6, far)), dma((6, far)), dma((5, 5)), dma((5, 5)),
            dma((1, 5)), dma((1, 5)), dma((1,)), dma((1,)),
            dma((5, 5)), dma((5, 5)), dma((2, 5)), dma((2, 5)),
        ],
        compiler_params=pltpu.CompilerParams(
            collective_id=0, has_side_effects=True, vmem_limit_bytes=63 * 1024 * 1024
        ),
    )(
        local_gap[0, 0], route_codes[0], flexibility[0, 0], dirichlet[0, 0],
        rigid_modes[0, 0], cmat, rigid_load,
    )
    return mult[None, None], res[None, None]


def solution(mesh):
    placed = (
        P("sub", "layer", None, None),
        P("sub", "layer", None),
        P("sub", "layer", None, None),
        P("sub", "layer", None, None),
        P("sub", "layer", None, None),
        P(("sub", "layer"), None),
        P(("sub", "layer"), None),
    )
    subs, layers = mesh.shape["sub"], mesh.shape["layer"]
    across = 4 if subs % 4 == 0 and subs > 4 else 2
    dims = (subs // across, across, layers // CORES)
    return jax.shard_map(
        functools.partial(per_device, dims),
        mesh=mesh,
        in_specs=placed,
        out_specs=(P("sub", "layer", None, None), P("sub", "layer", None, None)),
        check_vma=False,
    )
```

```python
import functools

import jax
import jax.numpy as jnp
from jax import lax
from jax.experimental import pallas as pl
from jax.experimental.pallas import tpu as pltpu
from jax.sharding import PartitionSpec as P

MESH = pl.DeviceIdType.MESH
THETA = 4.25
DELTA = 3.75
SIGMA = THETA / DELTA
RHO0 = DELTA / THETA
RHO1 = 1.0 / (2.0 * SIGMA - RHO0)
CORES = 2
MODES = 6
BF = jnp.bfloat16
F32 = jnp.float32
CHUNK = 384
TALL = 576
OFFSETS = [
    (0, 0), (-1, 0), (1, 0), (0, -1), (0, 1), (-2, 0), (2, 0),
    (0, -2), (0, 2), (-1, -1), (-1, 1), (1, -1), (1, 1),
]


def split2(v):
    hi = v.astype(BF)
    lo = (v - hi.astype(F32)).astype(BF)
    return hi, lo


def dot(a, b):
    return jnp.dot(a, b, preferred_element_type=F32)


def row_loop(rows, chunk, body):
    chunk = min(chunk, rows)

    @pl.loop(0, rows // chunk)
    def _(t):
        body(pl.ds(pl.multiple_of(t * chunk, chunk), chunk))


def coarse_sizes(dims):
    Z, X, Y = dims
    plane = X * Y * CORES
    cols = plane * MODES
    shift = max(cols * t % 128 for t in range(Z))
    return plane, Z, cols, (shift + cols + 127) // 128 * 128


def kernel(
    dims, gap, codes, flex, diri, modes, cinv, load, mult, res,
    stage, mats_hi, mats_lo, sel, sel_t, xs, xn, xa, vn, state, total, ahead,
    wide_w, mstk, cvec, vsrc, xrecv, comp, gath, part, redu, coef, call, rown, rnb, cpad, cblk,
    chi, clo, astk, arow, anat, bstk, tsend, tnb, kstk, psend, pnb,
    mat_sem, s1, r1, s2, r2, s3, r3, s4, r4, s5, r5, s6, r6, s7, r7, s8, r8,
):
    Z, X, Y = dims
    ni, rhs = gap.shape
    cap = ni // 4
    nq, np_, cols_z, window = coarse_sizes(dims)
    i = lax.axis_index("sub")
    j = lax.axis_index("layer")
    z, x = i // X, i % X
    subs, layers = Z * X, Y * CORES
    q = x * layers + j
    p = z
    opp = (1, 0, 3, 2)

    def inside(di, dj):
        checks = []
        if di:
            checks.append(i + di >= 0 if di < 0 else i + di < subs)
        if dj:
            checks.append(j + dj >= 0 if dj < 0 else j + dj < layers)
        return checks[0] if len(checks) == 1 else jnp.logical_and(*checks)

    def clipped(di, dj):
        return (jnp.clip(i + di, 0, subs - 1), jnp.clip(j + dj, 0, layers - 1))

    has = [None] + [inside(*o) for o in OFFSETS[1:]]
    away = [None] + [clipped(*o) for o in OFFSETS[1:]]
    back = [OFFSETS.index((-o[0], -o[1])) for o in OFFSETS]
    far = len(OFFSETS)

    def q_peer(t):
        return (z * X + t // layers, t % layers)

    def p_peer(t):
        return (t * X + x, j)

    loads = [
        pltpu.make_async_copy(flex, stage.at[0], mat_sem.at[0]),
        pltpu.make_async_copy(diri, stage.at[1], mat_sem.at[1]),
    ]
    for cp in loads:
        cp.start()

    call[...] = jnp.zeros_like(call)
    pnb[...] = jnp.zeros_like(pnb)
    tnb[...] = jnp.zeros_like(tnb)
    for d in range(4):
        @pl.when(jnp.logical_not(has[d + 1]))
        def _():
            rnb[d] = jnp.zeros_like(rnb[d])

            @pl.loop(0, xrecv.shape[0])
            def _(k):
                xrecv[k, pl.ds(d * cap, cap), :] = jnp.zeros((cap, rhs), F32)

    barrier = pltpu.get_barrier_semaphore()

    def greet(device):
        pl.semaphore_signal(barrier, inc=1, device_id=device, device_id_type=MESH)

    @pl.loop(1, nq)
    def _(t):
        greet(q_peer((q + t) % nq))

    @pl.loop(1, np_)
    def _(t):
        greet(p_peer((p + t) % np_))

    count = nq + np_ - 2
    for o in range(1, far):
        @pl.when(has[o])
        def _():
            greet(away[o])

        count = count + has[o].astype(jnp.int32)

    code_row = codes[...]
    for b in range(ni // 128):
        block = slice(b * 128, b * 128 + 128)
        slot = lax.broadcasted_iota(jnp.int32, (128, ni), 0) + b * 128
        sel[block, :] = jnp.where(code_row == slot, 1.0, 0.0).astype(BF)
        column = jnp.broadcast_to(code_row[:, block].astype(F32), (128, 128)).T.astype(jnp.int32)
        for c in range(ni // 128):
            lane = lax.broadcasted_iota(jnp.int32, (128, 128), 1) + c * 128
            sel_t[block, c * 128 : c * 128 + 128] = jnp.where(column == lane, 1.0, 0.0).astype(BF)

    wide = jnp.concatenate([modes[m] for m in range(MODES)] + [jnp.zeros((16 - MODES, ni), F32)], axis=0)
    m1 = wide.astype(BF)
    m2, m3 = split2(wide - m1.astype(F32))
    pieces = dot(jnp.concatenate([m1, m2, m3], axis=0), sel_t[...])
    rown[...] = pieces[:8] + (pieces[16:24] + pieces[32:40])

    comp[0] = jnp.concatenate([load[...], jnp.zeros((8 - MODES, rhs), F32)], axis=0)

    cpad[...] = jnp.zeros_like(cpad)
    cpad[:MODES, : cinv.shape[1]] = cinv[...]

    pl.semaphore_wait(barrier, count)

    def remote(src, dst, send, recv, device):
        return pltpu.make_async_remote_copy(
            src_ref=src, dst_ref=dst, send_sem=send, recv_sem=recv,
            device_id=device, device_id_type=MESH,
        )

    def wait_bytes(ref, sem):
        pltpu.make_async_copy(ref, ref, sem).wait()

    def gather_start(k):
        gath[k, q] = comp[k]

        @pl.loop(1, nq)
        def _(t):
            remote(comp.at[k], gath.at[k, q], s1.at[k], r1.at[k], q_peer((q + t) % nq)).start()

    def near_start(src_of, dst_of, send, recv, k, many=5):
        for o in range(1, many):
            @pl.when(has[o])
            def _():
                remote(src_of(o), dst_of(back[o]), send.at[k, o], recv.at[k, back[o]], away[o]).start()

    def near_wait(ref_of, sem, k, many=5):
        for o in range(1, many):
            @pl.when(has[o])
            def _():
                wait_bytes(ref_of(o), sem.at[k, o])

    def slots(ref, k):
        return lambda o: ref.at[k, pl.ds((o - 1) * cap, cap), :]

    def rows8(ref, k):
        return lambda o: ref.at[k, pl.ds(8 * o, 8), :]

    gather_start(0)
    near_start(lambda o: rown, lambda o: rnb.at[o - 1], s5, r5, 0)

    def columns(t):
        return pl.ds(pl.multiple_of(t * cols_z // 128 * 128, 128), window)

    @pl.loop(1, np_)
    def _(t):
        peer = (p + t) % np_
        remote(cpad.at[:, columns(peer)], cblk.at[p], s6.at[0], r6.at[0], p_peer(peer)).start()

    cblk[p] = cpad[:, columns(p)]

    def split_mat(n):
        loads[n].wait()

        def body(rows):
            hi, lo = split2(stage[n, rows, :])
            mats_hi[n, rows, :] = hi
            mats_lo[n, rows, :] = lo

        row_loop(ni, 128, body)

    def put_pieces(rows, value, ref):
        hi, lo = split2(value)
        ref[rows, :rhs] = hi
        ref[rows, rhs:] = lo

    def both_halves(both):
        return both[:, :rhs] + both[:, rhs:]

    def to_rows(src, dst):
        def body(rows):
            dst[rows, :] = dot(sel_t[rows, :], src[...]).astype(BF)

        row_loop(ni, TALL, body)

    def multiply(n, src):
        def body(rows):
            both = dot(mats_hi[n, rows, :], src[...]) + dot(mats_lo[n, rows, :], src[...])
            put_pieces(rows, both_halves(both), vn)

        row_loop(ni, TALL, body)

    def to_slots(put):
        row_loop(ni, TALL, lambda rows: put(rows, both_halves(dot(sel[rows, :], vn[...]))))

    def put_ahead(rows, value):
        ahead[rows, :] = value

    def tall_pieces(value):
        hi = value.astype(BF)
        return jnp.concatenate([hi, (value - hi.astype(F32)).astype(BF)], axis=0)

    def skinny(lhs, rhs_pieces):
        out = dot(lhs, rhs_pieces)
        return out[:48, :rhs] + (out[:48, rhs:] + out[48:, :rhs])

    split_mat(0)
    row_loop(ni, CHUNK, lambda rows: put_pieces(rows, -gap[rows, :], vn))
    to_slots(put_ahead)

    wait_bytes(cblk.at[pl.ds(0, np_ - 1)], r6.at[0])
    place = lax.broadcasted_iota(jnp.int32, (window, nq * 8), 0)
    target = lax.broadcasted_iota(jnp.int32, (window, nq * 8), 1)
    live = (place == (z * cols_z) % 128 + target // 8 * MODES + target % 8) & (target % 8 < MODES)
    spread = jnp.where(live, 1.0, 0.0).astype(BF)
    block = cblk[...].reshape(np_ * 8, window)
    c1 = block.astype(BF)
    c2, c3 = split2(block - c1.astype(F32))
    block = dot(c1, spread) + (dot(c2, spread) + dot(c3, spread))
    hi, lo = split2(block)
    chi[...] = hi
    clo[...] = lo

    def coarse_scatter(k):
        wait_bytes(gath.at[k, pl.ds(0, nq - 1)], r1.at[k])
        g_hi, g_lo = split2(gath[k].reshape(nq * 8, rhs))
        out = dot(chi[...], g_hi) + (dot(chi[...], g_lo) + dot(clo[...], g_hi))
        part[k] = out.reshape(np_, 8, rhs)

        @pl.loop(1, np_)
        def _(t):
            peer = (p + t) % np_
            remote(part.at[k, peer], redu.at[k, p], s2.at[k], r2.at[k], p_peer(peer)).start()

        redu[k, p] = part[k, p]

    def coarse_finish(k):
        wait_bytes(redu.at[k, pl.ds(0, np_ - 1)], r2.at[k])
        coef[k] = jnp.sum(redu[k], axis=0)
        near_start(lambda o: coef.at[k], lambda o: call.at[k, o], s3, r3, k, far)

    coarse_scatter(0)

    near_wait(lambda o: rnb.at[o - 1], r5, 0)
    lane = lax.broadcasted_iota(jnp.int32, (8, ni), 1)
    parts = [rown[...]]
    for d in range(4):
        moved = pltpu.roll(rnb[d], ((d - opp[d]) * cap) % ni, 1)
        live = (lane >= d * cap) & (lane < (d + 1) * cap)
        parts.append(jnp.where(live, -moved, 0.0))
    acols = jnp.concatenate(parts + [jnp.zeros((88, ni), F32)], axis=0)

    def stacked(cols):
        hi = cols.astype(BF).astype(F32)
        low = cols - hi
        return (hi + pltpu.roll(hi, 40, 1) + pltpu.roll(low, 80, 1)).astype(BF)

    arow[...] = tall_pieces(acols[:48])
    for b in range(ni // 128):
        block = slice(b * 128, b * 128 + 128)
        cols = acols[:, block].T
        astk[block, :] = stacked(cols)
        put_pieces(block, cols, xs)

    to_rows(xs, xa)

    def partial_start(k, lhs, pieces):
        psend[k] = skinny(lhs, pieces)
        near_start(rows8(psend, k), rows8(pnb, k), s7, r7, k)

    row_loop(ni, CHUNK, lambda rows: put_pieces(rows, ahead[rows, :], xs))
    partial_start(0, arow[...], xs[...])
    def around(k, base):
        picks = []
        for step in OFFSETS[:5]:
            o = OFFSETS.index((base[0] + step[0], base[1] + step[1]))
            picks.append(coef[k] if o == 0 else call[k, o])
        c = jnp.concatenate(picks, axis=0)
        c_hi = c.astype(BF).astype(F32)
        return jnp.concatenate(
            [c_hi, c - c_hi, c_hi, jnp.zeros((8, rhs), F32)], axis=0
        ).astype(BF)

    def prepare(n):
        multiply(n, xa)

        def put(rows, cols):
            mstk[n, rows, :] = stacked(cols)
            put_pieces(rows, cols, xs)

        to_slots(put)
        tsend[n] = skinny(arow[...], xs[...])
        near_start(rows8(tsend, n), rows8(tnb, n), s8, r8, n)

    def prepare_end(n):
        near_wait(rows8(tnb, n), r8, n)
        for o in range(5):
            block = tsend[n, 0:8, :] if o == 0 else tnb[n, 8 * o : 8 * o + 8, :]
            kstk[n, :, o * 128 : o * 128 + 128] = stacked(
                jnp.concatenate([block, jnp.zeros((8, 128), F32)], axis=0)
            )

    def prepare_rows(n):
        out = dot(anat[...], mats_hi[n])
        out = out[:48] + out[48:] + dot(anat[:48, :], mats_lo[n])
        out = dot(tall_pieces(out), sel_t[...])
        bstk[n] = tall_pieces(out[:48] + out[48:])

    def settle(n, last_new):
        share = jnp.where(n == 1, 1.0, 0.0)
        value = wide_w[...] + last_new * dot(astk[...], cvec[...])
        state[n] = value
        total[...] = total[...] + share * value

    coarse_finish(0)
    prepare(0)
    state[...] = jnp.zeros_like(state)
    split_mat(1)
    prepare_end(0)

    @pl.loop(0, 5)
    def _(k):
        n = k % 2
        odd = n == 1
        last_new = jnp.where(odd | (k == 0), 1.0, jnp.where(k == 2, -0.5 / THETA, -RHO1 / DELTA))

        @pl.when(k > 0)
        def _():
            to_slots(put_ahead)

        near_wait(lambda o: call.at[k, o], r3, k, far)
        near_wait(rows8(pnb, k), r7, k)
        hood = [around(k, o) for o in OFFSETS[:5]]
        cvec[...] = hood[0]
        early = psend[k, 0:8, :]
        for o in range(1, 5):
            early = early + pnb[k, 8 * o : 8 * o + 8, :]
        moved = dot(kstk[n], jnp.concatenate(hood, axis=0))
        comp[k + 1] = early + last_new * moved[:8]
        gather_start(k + 1)
        vsrc[k] = ahead[...] + last_new * dot(mstk[n], cvec[...])
        near_start(slots(vsrc, k), slots(xrecv, k), s4, r4, k)

        @pl.when(k == 0)
        def _():
            total[...] = dot(astk[...], cvec[...])

        @pl.when(k > 0)
        def _():
            settle(1 - n, last_new)

        coarse_scatter(k + 1)

        @pl.when(k == 0)
        def _():
            prepare(1)

        coarse_finish(k + 1)

        @pl.when(k == 0)
        def _():
            anat[...] = dot(arow[...], sel[...]).astype(BF)
            prepare_rows(1)

        @pl.when(k == 1)
        def _():
            prepare_rows(0)

        near_wait(slots(xrecv, k), r4, k)
        scale_old = jnp.where(odd, jnp.where(k == 1, 0.0, RHO1 * RHO0), 1.0)
        scale_new = jnp.where(odd, jnp.where(k == 1, 0.5 / THETA, RHO1 / DELTA), -1.0)

        def fresh(rows):
            jumped = vsrc[k, rows, :] - xrecv[k, rows, :]
            w = scale_old * state[n, rows, :] + scale_new * jumped
            wide_w[rows, :] = w
            put_pieces(rows, w, xs)

        row_loop(ni, CHUNK, fresh)

        @pl.when(k < 4)
        def _():
            partial_start(k + 1, bstk[1 - n], xs[...])
            to_rows(xs, xn)
            multiply(1 - n, xn)

        @pl.when(k == 0)
        def _():
            prepare_end(1)

    near_wait(lambda o: call.at[5, o], r3, 5, far)
    cvec[...] = around(5, (0, 0))
    settle(0, 1.0)
    row_loop(ni, CHUNK, lambda rows: put_pieces(rows, total[rows, :], xn))
    row_loop(ni, CHUNK, lambda rows: put_pieces(rows, state[0, rows, :], xs))

    def finish(rows):
        mult[rows, :] = both_halves(dot(sel_t[rows, :], xn[...]))
        res[rows, :] = both_halves(dot(sel_t[rows, :], xs[...]))

    row_loop(ni, TALL, finish)

    near_wait(lambda o: rown, s5, 0)
    wait_bytes(cblk.at[pl.ds(0, np_ - 1)], s6.at[0])
    for n in range(2):
        near_wait(rows8(tsend, n), s8, n)

    @pl.loop(0, 6)
    def _(k):
        wait_bytes(gath.at[k, pl.ds(0, nq - 1)], s1.at[k])
        wait_bytes(redu.at[k, pl.ds(0, np_ - 1)], s2.at[k])
        near_wait(lambda o: coef.at[k], s3, k, far)

    @pl.loop(0, 5)
    def _(k):
        near_wait(slots(vsrc, k), s4, k)
        near_wait(rows8(psend, k), s7, k)


def per_device(dims, local_gap, route_codes, flexibility, dirichlet, rigid_modes, coarse_inverse, rigid_load):
    ni, rhs = local_gap.shape[2:]
    nq, np_, cols_z, window = coarse_sizes(dims)
    far = len(OFFSETS)
    vmem = pl.BlockSpec(memory_space=pltpu.VMEM)
    hbm = pl.BlockSpec(memory_space=pl.ANY)
    field = jax.ShapeDtypeStruct((ni, rhs), F32)
    dma = pltpu.SemaphoreType.DMA
    V = pltpu.VMEM
    mult, res = pl.pallas_call(
        functools.partial(kernel, dims),
        out_shape=(field, field),
        in_specs=[vmem, vmem, hbm, hbm, vmem, vmem, vmem],
        out_specs=(vmem, vmem),
        scratch_shapes=[
            V((2, ni, ni), F32), V((2, ni, ni), BF), V((2, ni, ni), BF),
            V((ni, ni), BF), V((ni, ni), BF),
            V((ni, 2 * rhs), BF), V((ni, 2 * rhs), BF), V((ni, 2 * rhs), BF),
            V((ni, 2 * rhs), BF), V((2, ni, rhs), F32), V((ni, rhs), F32),
            V((ni, rhs), F32), V((ni, rhs), F32), V((2, ni, 128), BF),
            V((128, rhs), BF), V((5, ni, rhs), F32), V((5, ni, rhs), F32),
            V((6, 8, rhs), F32), V((6, nq, 8, rhs), F32),
            V((6, np_, 8, rhs), F32), V((6, np_, 8, rhs), F32),
            V((6, 8, rhs), F32), V((6, far, 8, rhs), F32),
            V((8, ni), F32), V((4, 8, ni), F32), V((8, (np_ - 1) * cols_z // 128 * 128 + window), F32), V((np_, 8, window), F32),
            V((np_ * 8, nq * 8), BF), V((np_ * 8, nq * 8), BF), V((ni, 128), BF),
            V((96, ni), BF), V((96, ni), BF), V((2, 96, ni), BF),
            V((2, 48, rhs), F32), V((2, 40, rhs), F32), V((2, 16, 640), BF),
            V((5, 48, rhs), F32), V((5, 40, rhs), F32),
            dma((2,)), dma((6,)), dma((6,)), dma((6,)), dma((6,)),
            dma((6, far)), dma((6, far)), dma((5, 5)), dma((5, 5)),
            dma((1, 5)), dma((1, 5)), dma((1,)), dma((1,)),
            dma((5, 5)), dma((5, 5)), dma((2, 5)), dma((2, 5)),
        ],
        compiler_params=pltpu.CompilerParams(
            collective_id=0, has_side_effects=True, vmem_limit_bytes=63 * 1024 * 1024
        ),
    )(
        local_gap[0, 0], route_codes[0], flexibility[0, 0], dirichlet[0, 0],
        rigid_modes.reshape(MODES, 1, ni), coarse_inverse, rigid_load,
    )
    return mult[None, None], res[None, None]


def solution(mesh):
    placed = (
        P("sub", "layer", None, None),
        P("sub", "layer", None),
        P("sub", "layer", None, None),
        P("sub", "layer", None, None),
        P("sub", "layer", None, None),
        P(("sub", "layer"), None),
        P(("sub", "layer"), None),
    )
    subs, layers = mesh.shape["sub"], mesh.shape["layer"]
    across = 4 if subs % 4 == 0 and subs > 4 else 2
    dims = (subs // across, across, layers // CORES)
    return jax.shard_map(
        functools.partial(per_device, dims),
        mesh=mesh,
        in_specs=placed,
        out_specs=(P("sub", "layer", None, None), P("sub", "layer", None, None)),
        check_vma=False,
    )
```

```python
import functools

import jax
import jax.numpy as jnp
from jax import lax
from jax.experimental import pallas as pl
from jax.experimental.pallas import tpu as pltpu
from jax.sharding import PartitionSpec as P

MESH = pl.DeviceIdType.MESH
THETA = 4.25
DELTA = 3.75
SIGMA = THETA / DELTA
RHO0 = DELTA / THETA
RHO1 = 1.0 / (2.0 * SIGMA - RHO0)
CORES = 2
MODES = 6
BF = jnp.bfloat16
F32 = jnp.float32
CHUNK = 384
TALL = 576
OFFSETS = [
    (0, 0), (-1, 0), (1, 0), (0, -1), (0, 1), (-2, 0), (2, 0),
    (0, -2), (0, 2), (-1, -1), (-1, 1), (1, -1), (1, 1),
]


def split2(v):
    hi = v.astype(BF)
    lo = (v - hi.astype(F32)).astype(BF)
    return hi, lo


def dot(a, b):
    return jnp.dot(a, b, preferred_element_type=F32)


def row_loop(rows, chunk, body):
    chunk = min(chunk, rows)

    @pl.loop(0, rows // chunk)
    def _(t):
        body(pl.ds(pl.multiple_of(t * chunk, chunk), chunk))


def kernel(
    dims, gap, codes, flex, diri, modes, cinv, load, mult, res,
    stage, mats_hi, mats_lo, sel, sel_t, xs, xn, xa, vn, state, total, ahead,
    wide_w, mstk, cvec, vsrc, xrecv, comp, gath, part, redu, coef, call, rown, rnb, cpad, cmat, cblk,
    chi, clo, astk, arow, anat, bstk, tsend, tnb, kstk, psend, pnb,
    mat_sem, s1, r1, s2, r2, s3, r3, s4, r4, s5, r5, s6, r6, s7, r7, s8, r8,
):
    Z, X, Y = dims
    ni, rhs = gap.shape
    cap = ni // 4
    nq, np_ = Z * CORES, X * Y
    i = lax.axis_index("sub")
    j = lax.axis_index("layer")
    z, x = i // X, i % X
    subs, layers = Z * X, Y * CORES
    y, core = j // CORES, j % CORES
    q = z * CORES + core
    p = x * Y + y
    opp = (1, 0, 3, 2)

    def inside(di, dj):
        checks = []
        if di:
            checks.append(i + di >= 0 if di < 0 else i + di < subs)
        if dj:
            checks.append(j + dj >= 0 if dj < 0 else j + dj < layers)
        return checks[0] if len(checks) == 1 else jnp.logical_and(*checks)

    def clipped(di, dj):
        return (jnp.clip(i + di, 0, subs - 1), jnp.clip(j + dj, 0, layers - 1))

    has = [None] + [inside(*o) for o in OFFSETS[1:]]
    away = [None] + [clipped(*o) for o in OFFSETS[1:]]
    back = [OFFSETS.index((-o[0], -o[1])) for o in OFFSETS]
    far = len(OFFSETS)

    def q_peer(t):
        return ((t // CORES) * X + x, y * CORES + t % CORES)

    def p_peer(t):
        return (z * X + t // Y, (t % Y) * CORES + core)

    loads = [
        pltpu.make_async_copy(flex, stage.at[0], mat_sem.at[0]),
        pltpu.make_async_copy(diri, stage.at[1], mat_sem.at[1]),
    ]
    for cp in loads:
        cp.start()

    call[...] = jnp.zeros_like(call)
    pnb[...] = jnp.zeros_like(pnb)
    tnb[...] = jnp.zeros_like(tnb)
    for d in range(4):
        @pl.when(jnp.logical_not(has[d + 1]))
        def _():
            rnb[d] = jnp.zeros_like(rnb[d])

            @pl.loop(0, xrecv.shape[0])
            def _(k):
                xrecv[k, pl.ds(d * cap, cap), :] = jnp.zeros((cap, rhs), F32)

    barrier = pltpu.get_barrier_semaphore()

    def greet(device):
        pl.semaphore_signal(barrier, inc=1, device_id=device, device_id_type=MESH)

    @pl.loop(1, nq)
    def _(t):
        greet(q_peer((q + t) % nq))

    @pl.loop(1, np_)
    def _(t):
        greet(p_peer((p + t) % np_))

    count = nq + np_ - 2
    for o in range(1, far):
        @pl.when(has[o])
        def _():
            greet(away[o])

        count = count + has[o].astype(jnp.int32)

    code_row = codes[...]
    for b in range(ni // 128):
        block = slice(b * 128, b * 128 + 128)
        slot = lax.broadcasted_iota(jnp.int32, (128, ni), 0) + b * 128
        sel[block, :] = jnp.where(code_row == slot, 1.0, 0.0).astype(BF)
        column = jnp.broadcast_to(code_row[:, block].astype(F32), (128, 128)).T.astype(jnp.int32)
        for c in range(ni // 128):
            lane = lax.broadcasted_iota(jnp.int32, (128, 128), 1) + c * 128
            sel_t[block, c * 128 : c * 128 + 128] = jnp.where(column == lane, 1.0, 0.0).astype(BF)

    wide = jnp.concatenate([modes[m] for m in range(MODES)] + [jnp.zeros((16 - MODES, ni), F32)], axis=0)
    m1 = wide.astype(BF)
    m2, m3 = split2(wide - m1.astype(F32))
    pieces = dot(jnp.concatenate([m1, m2, m3], axis=0), sel_t[...])
    rown[...] = pieces[:8] + (pieces[16:24] + pieces[32:40])

    comp[0] = jnp.concatenate([load[...], jnp.zeros((8 - MODES, rhs), F32)], axis=0)

    cpad[...] = jnp.zeros_like(cpad)
    cpad[:MODES, : cinv.shape[1]] = cinv[...]
    cols_z = np_ * CORES * MODES
    lanes_z = np_ * CORES * 8
    window = cpad.shape[1] - (Z - 1) * cols_z // 128 * 128
    place = lax.broadcasted_iota(jnp.int32, (window, lanes_z), 0)
    target = lax.broadcasted_iota(jnp.int32, (window, lanes_z), 1)
    live = (place == target // 8 * MODES + target % 8) & (target % 8 < MODES)
    spread = jnp.where(live, 1.0, 0.0).astype(BF)
    slabs = []
    for t in range(Z):
        low = t * cols_z // 128 * 128
        slab = cpad[:, low : low + window]
        shift = t * cols_z % 128
        slabs.append(pltpu.roll(slab, window - shift, 1) if shift else slab)
    slab = jnp.concatenate(slabs, axis=0)
    c1 = slab.astype(BF)
    c2, c3 = split2(slab - c1.astype(F32))
    wide = dot(c1, spread) + (dot(c2, spread) + dot(c3, spread))
    group = lax.broadcasted_iota(jnp.int32, (8, nq * 8), 1) // (CORES * 8)
    for b in range(np_):
        low = b * CORES * 8 // (nq * 8) * (nq * 8)
        out = jnp.zeros((8, nq * 8), F32)
        for t in range(Z):
            piece = wide[8 * t : 8 * t + 8, low : low + nq * 8]
            shift = (t * CORES * 8 - (b * CORES * 8 - low)) % (nq * 8)
            out = jnp.where(group == t, pltpu.roll(piece, shift, 1) if shift else piece, out)
        cmat[b] = out

    pl.semaphore_wait(barrier, count)

    def remote(src, dst, send, recv, device):
        return pltpu.make_async_remote_copy(
            src_ref=src, dst_ref=dst, send_sem=send, recv_sem=recv,
            device_id=device, device_id_type=MESH,
        )

    def wait_bytes(ref, sem):
        pltpu.make_async_copy(ref, ref, sem).wait()

    def gather_start(k):
        gath[k, q] = comp[k]

        @pl.loop(1, nq)
        def _(t):
            remote(comp.at[k], gath.at[k, q], s1.at[k], r1.at[k], q_peer((q + t) % nq)).start()

    def near_start(src_of, dst_of, send, recv, k, many=5):
        for o in range(1, many):
            @pl.when(has[o])
            def _():
                remote(src_of(o), dst_of(back[o]), send.at[k, o], recv.at[k, back[o]], away[o]).start()

    def near_wait(ref_of, sem, k, many=5):
        for o in range(1, many):
            @pl.when(has[o])
            def _():
                wait_bytes(ref_of(o), sem.at[k, o])

    def slots(ref, k):
        return lambda o: ref.at[k, pl.ds((o - 1) * cap, cap), :]

    def rows8(ref, k):
        return lambda o: ref.at[k, pl.ds(8 * o, 8), :]

    gather_start(0)
    near_start(lambda o: rown, lambda o: rnb.at[o - 1], s5, r5, 0)

    @pl.loop(1, np_)
    def _(t):
        peer = (p + t) % np_
        remote(cmat.at[peer], cblk.at[p], s6.at[0], r6.at[0], p_peer(peer)).start()

    cblk[p] = cmat[p]

    def split_mat(n):
        loads[n].wait()

        def body(rows):
            hi, lo = split2(stage[n, rows, :])
            mats_hi[n, rows, :] = hi
            mats_lo[n, rows, :] = lo

        row_loop(ni, 128, body)

    def put_pieces(rows, value, ref):
        hi, lo = split2(value)
        ref[rows, :rhs] = hi
        ref[rows, rhs:] = lo

    def both_halves(both):
        return both[:, :rhs] + both[:, rhs:]

    def to_rows(src, dst):
        def body(rows):
            dst[rows, :] = dot(sel_t[rows, :], src[...]).astype(BF)

        row_loop(ni, TALL, body)

    def multiply(n, src):
        def body(rows):
            both = dot(mats_hi[n, rows, :], src[...]) + dot(mats_lo[n, rows, :], src[...])
            put_pieces(rows, both_halves(both), vn)

        row_loop(ni, TALL, body)

    def to_slots(put):
        row_loop(ni, TALL, lambda rows: put(rows, both_halves(dot(sel[rows, :], vn[...]))))

    def put_ahead(rows, value):
        ahead[rows, :] = value

    def tall_pieces(value):
        hi = value.astype(BF)
        return jnp.concatenate([hi, (value - hi.astype(F32)).astype(BF)], axis=0)

    def skinny(lhs, rhs_pieces):
        out = dot(lhs, rhs_pieces)
        return out[:48, :rhs] + (out[:48, rhs:] + out[48:, :rhs])

    split_mat(0)
    row_loop(ni, CHUNK, lambda rows: put_pieces(rows, -gap[rows, :], vn))
    to_slots(put_ahead)

    def coarse_scatter(k):
        wait_bytes(gath.at[k, pl.ds(0, nq - 1)], r1.at[k])
        g_hi, g_lo = split2(gath[k].reshape(nq * 8, rhs))
        out = dot(chi[...], g_hi) + (dot(chi[...], g_lo) + dot(clo[...], g_hi))
        part[k] = out.reshape(np_, 8, rhs)

        @pl.loop(1, np_)
        def _(t):
            peer = (p + t) % np_
            remote(part.at[k, peer], redu.at[k, p], s2.at[k], r2.at[k], p_peer(peer)).start()

        redu[k, p] = part[k, p]

    def coarse_finish(k):
        wait_bytes(redu.at[k, pl.ds(0, np_ - 1)], r2.at[k])
        coef[k] = jnp.sum(redu[k], axis=0)
        near_start(lambda o: coef.at[k], lambda o: call.at[k, o], s3, r3, k, far)

    near_wait(lambda o: rnb.at[o - 1], r5, 0)
    lane = lax.broadcasted_iota(jnp.int32, (8, ni), 1)
    parts = [rown[...]]
    for d in range(4):
        moved = pltpu.roll(rnb[d], ((d - opp[d]) * cap) % ni, 1)
        live = (lane >= d * cap) & (lane < (d + 1) * cap)
        parts.append(jnp.where(live, -moved, 0.0))
    acols = jnp.concatenate(parts + [jnp.zeros((88, ni), F32)], axis=0)

    def stacked(cols):
        hi = cols.astype(BF).astype(F32)
        low = cols - hi
        return (hi + pltpu.roll(hi, 40, 1) + pltpu.roll(low, 80, 1)).astype(BF)

    arow[...] = tall_pieces(acols[:48])
    for b in range(ni // 128):
        block = slice(b * 128, b * 128 + 128)
        cols = acols[:, block].T
        astk[block, :] = stacked(cols)
        put_pieces(block, cols, xs)

    to_rows(xs, xa)

    def partial_start(k, lhs, pieces):
        psend[k] = skinny(lhs, pieces)
        near_start(rows8(psend, k), rows8(pnb, k), s7, r7, k)

    row_loop(ni, CHUNK, lambda rows: put_pieces(rows, ahead[rows, :], xs))
    partial_start(0, arow[...], xs[...])
    wait_bytes(cblk.at[pl.ds(0, np_ - 1)], r6.at[0])
    hi, lo = split2(cblk[...].reshape(np_ * 8, nq * 8))
    chi[...] = hi
    clo[...] = lo
    coarse_scatter(0)
    def around(k, base):
        picks = []
        for step in OFFSETS[:5]:
            o = OFFSETS.index((base[0] + step[0], base[1] + step[1]))
            picks.append(coef[k] if o == 0 else call[k, o])
        c = jnp.concatenate(picks, axis=0)
        c_hi = c.astype(BF).astype(F32)
        return jnp.concatenate(
            [c_hi, c - c_hi, c_hi, jnp.zeros((8, rhs), F32)], axis=0
        ).astype(BF)

    def prepare(n):
        multiply(n, xa)

        def put(rows, cols):
            mstk[n, rows, :] = stacked(cols)
            put_pieces(rows, cols, xs)

        to_slots(put)
        tsend[n] = skinny(arow[...], xs[...])
        near_start(rows8(tsend, n), rows8(tnb, n), s8, r8, n)

    def prepare_end(n):
        near_wait(rows8(tnb, n), r8, n)
        for o in range(5):
            block = tsend[n, 0:8, :] if o == 0 else tnb[n, 8 * o : 8 * o + 8, :]
            kstk[n, :, o * 128 : o * 128 + 128] = stacked(
                jnp.concatenate([block, jnp.zeros((8, 128), F32)], axis=0)
            )

    def prepare_rows(n):
        out = dot(anat[...], mats_hi[n])
        out = out[:48] + out[48:] + dot(anat[:48, :], mats_lo[n])
        out = dot(tall_pieces(out), sel_t[...])
        bstk[n] = tall_pieces(out[:48] + out[48:])

    def settle(n, last_new):
        share = jnp.where(n == 1, 1.0, 0.0)
        value = wide_w[...] + last_new * dot(astk[...], cvec[...])
        state[n] = value
        total[...] = total[...] + share * value

    prepare(0)
    coarse_finish(0)
    state[...] = jnp.zeros_like(state)
    split_mat(1)
    anat[...] = dot(arow[...], sel[...]).astype(BF)
    prepare_rows(1)
    prepare_end(0)

    @pl.loop(0, 5)
    def _(k):
        n = k % 2
        odd = n == 1
        last_new = jnp.where(odd | (k == 0), 1.0, jnp.where(k == 2, -0.5 / THETA, -RHO1 / DELTA))

        @pl.when(k > 0)
        def _():
            to_slots(put_ahead)

        near_wait(lambda o: call.at[k, o], r3, k, far)
        near_wait(rows8(pnb, k), r7, k)
        hood = [around(k, o) for o in OFFSETS[:5]]
        cvec[...] = hood[0]
        early = psend[k, 0:8, :]
        for o in range(1, 5):
            early = early + pnb[k, 8 * o : 8 * o + 8, :]
        moved = dot(kstk[n], jnp.concatenate(hood, axis=0))
        comp[k + 1] = early + last_new * moved[:8]
        gather_start(k + 1)
        vsrc[k] = ahead[...] + last_new * dot(mstk[n], cvec[...])
        near_start(slots(vsrc, k), slots(xrecv, k), s4, r4, k)

        @pl.when(k == 0)
        def _():
            total[...] = dot(astk[...], cvec[...])

        @pl.when(k > 0)
        def _():
            settle(1 - n, last_new)

        coarse_scatter(k + 1)

        @pl.when(k == 0)
        def _():
            prepare(1)

        @pl.when(k == 1)
        def _():
            prepare_rows(0)

        near_wait(slots(xrecv, k), r4, k)
        scale_old = jnp.where(odd, jnp.where(k == 1, 0.0, RHO1 * RHO0), 1.0)
        scale_new = jnp.where(odd, jnp.where(k == 1, 0.5 / THETA, RHO1 / DELTA), -1.0)

        def fresh(rows):
            jumped = vsrc[k, rows, :] - xrecv[k, rows, :]
            w = scale_old * state[n, rows, :] + scale_new * jumped
            wide_w[rows, :] = w
            put_pieces(rows, w, xs)

        row_loop(ni, CHUNK, fresh)

        @pl.when(k < 4)
        def _():
            partial_start(k + 1, bstk[1 - n], xs[...])
            to_rows(xs, xn)

        coarse_finish(k + 1)

        @pl.when(k < 4)
        def _():
            multiply(1 - n, xn)

        @pl.when(k == 0)
        def _():
            prepare_end(1)

    near_wait(lambda o: call.at[5, o], r3, 5, far)
    cvec[...] = around(5, (0, 0))
    settle(0, 1.0)
    row_loop(ni, CHUNK, lambda rows: put_pieces(rows, total[rows, :], xn))
    row_loop(ni, CHUNK, lambda rows: put_pieces(rows, state[0, rows, :], xs))

    def finish(rows):
        mult[rows, :] = both_halves(dot(sel_t[rows, :], xn[...]))
        res[rows, :] = both_halves(dot(sel_t[rows, :], xs[...]))

    row_loop(ni, TALL, finish)

    near_wait(lambda o: rown, s5, 0)
    wait_bytes(cblk.at[pl.ds(0, np_ - 1)], s6.at[0])
    for n in range(2):
        near_wait(rows8(tsend, n), s8, n)

    @pl.loop(0, 6)
    def _(k):
        wait_bytes(gath.at[k, pl.ds(0, nq - 1)], s1.at[k])
        wait_bytes(redu.at[k, pl.ds(0, np_ - 1)], s2.at[k])
        near_wait(lambda o: coef.at[k], s3, k, far)

    @pl.loop(0, 5)
    def _(k):
        near_wait(slots(vsrc, k), s4, k)
        near_wait(rows8(psend, k), s7, k)


def hand_over(mult, res, mult_out, res_out, held, come, leave):
    half = mult.shape[0] // 2
    pairs = ((mult, mult_out), (res, res_out))
    parts = [(n, h, pl.ds(h * half, half)) for n in range(2) for h in range(2)]
    arriving = [
        pltpu.make_async_copy(pairs[n][0].at[rows], held.at[n, rows], come.at[n, h])
        for n, h, rows in parts
    ]
    leaving = [
        pltpu.make_async_copy(held.at[n, rows], pairs[n][1].at[rows], leave.at[n, h])
        for n, h, rows in parts
    ]
    for copy in arriving:
        copy.start()
    for first, second in zip(arriving, leaving):
        first.wait()
        second.start()
    for copy in leaving:
        copy.wait()


def per_device(dims, local_gap, route_codes, flexibility, dirichlet, rigid_modes, coarse_inverse, rigid_load):
    ni, rhs = local_gap.shape[2:]
    Z, X, Y = dims
    nq, np_ = Z * CORES, X * Y
    cols_z = np_ * CORES * MODES
    window = (max(cols_z * t % 128 for t in range(Z)) + cols_z + 127) // 128 * 128
    far = len(OFFSETS)
    vmem = pl.BlockSpec(memory_space=pltpu.VMEM)
    hbm = pl.BlockSpec(memory_space=pl.ANY)
    field = jax.ShapeDtypeStruct((ni, rhs), F32)
    dma = pltpu.SemaphoreType.DMA
    V = pltpu.VMEM
    mult, res = pl.pallas_call(
        functools.partial(kernel, dims),
        out_shape=(field, field),
        in_specs=[vmem, vmem, hbm, hbm, vmem, vmem, vmem],
        out_specs=(vmem, vmem),
        scratch_shapes=[
            V((2, ni, ni), F32), V((2, ni, ni), BF), V((2, ni, ni), BF),
            V((ni, ni), BF), V((ni, ni), BF),
            V((ni, 2 * rhs), BF), V((ni, 2 * rhs), BF), V((ni, 2 * rhs), BF),
            V((ni, 2 * rhs), BF), V((2, ni, rhs), F32), V((ni, rhs), F32),
            V((ni, rhs), F32), V((ni, rhs), F32), V((2, ni, 128), BF),
            V((128, rhs), BF), V((5, ni, rhs), F32), V((5, ni, rhs), F32),
            V((6, 8, rhs), F32), V((6, nq, 8, rhs), F32),
            V((6, np_, 8, rhs), F32), V((6, np_, 8, rhs), F32),
            V((6, 8, rhs), F32), V((6, far, 8, rhs), F32),
            V((8, ni), F32), V((4, 8, ni), F32), V((8, (Z - 1) * cols_z // 128 * 128 + window), F32),
            V((np_, 8, nq * 8), F32), V((np_, 8, nq * 8), F32),
            V((np_ * 8, nq * 8), BF), V((np_ * 8, nq * 8), BF), V((ni, 128), BF),
            V((96, ni), BF), V((96, ni), BF), V((2, 96, ni), BF),
            V((2, 48, rhs), F32), V((2, 40, rhs), F32), V((2, 16, 640), BF),
            V((5, 48, rhs), F32), V((5, 40, rhs), F32),
            dma((2,)), dma((6,)), dma((6,)), dma((6,)), dma((6,)),
            dma((6, far)), dma((6, far)), dma((5, 5)), dma((5, 5)),
            dma((1, 5)), dma((1, 5)), dma((1,)), dma((1,)),
            dma((5, 5)), dma((5, 5)), dma((2, 5)), dma((2, 5)),
        ],
        compiler_params=pltpu.CompilerParams(
            collective_id=0, has_side_effects=True, vmem_limit_bytes=63 * 1024 * 1024
        ),
    )(
        local_gap[0, 0], route_codes[0], flexibility[0, 0], dirichlet[0, 0],
        rigid_modes.reshape(MODES, 1, ni), coarse_inverse, rigid_load,
    )
    hold = V((2, ni, rhs), F32)
    mult, res = pl.pallas_call(
        hand_over,
        out_shape=(field, field),
        in_specs=[hbm, hbm],
        out_specs=(hbm, hbm),
        scratch_shapes=[hold, dma((2, 2)), dma((2, 2))],
    )(mult, res)
    return mult[None, None], res[None, None]


def solution(mesh):
    placed = (
        P("sub", "layer", None, None),
        P("sub", "layer", None),
        P("sub", "layer", None, None),
        P("sub", "layer", None, None),
        P("sub", "layer", None, None),
        P(("sub", "layer"), None),
        P(("sub", "layer"), None),
    )
    subs, layers = mesh.shape["sub"], mesh.shape["layer"]
    across = 4 if subs % 4 == 0 and subs > 4 else 2
    dims = (subs // across, across, layers // CORES)
    return jax.shard_map(
        functools.partial(per_device, dims),
        mesh=mesh,
        in_specs=placed,
        out_specs=(P("sub", "layer", None, None), P("sub", "layer", None, None)),
        check_vma=False,
    )
```

```python
import functools

import jax
import jax.numpy as jnp
from jax import lax
from jax.experimental import pallas as pl
from jax.experimental.pallas import tpu as pltpu
from jax.sharding import PartitionSpec as P

MESH = pl.DeviceIdType.MESH
THETA = 4.25
DELTA = 3.75
SIGMA = THETA / DELTA
RHO0 = DELTA / THETA
RHO1 = 1.0 / (2.0 * SIGMA - RHO0)
CORES = 2
MODES = 6
BF = jnp.bfloat16
F32 = jnp.float32
CHUNK = 384
TALL = 576
OFFSETS = [
    (0, 0), (-1, 0), (1, 0), (0, -1), (0, 1), (-2, 0), (2, 0),
    (0, -2), (0, 2), (-1, -1), (-1, 1), (1, -1), (1, 1),
]


def split2(v):
    hi = v.astype(BF)
    lo = (v - hi.astype(F32)).astype(BF)
    return hi, lo


def dot(a, b):
    return jnp.dot(a, b, preferred_element_type=F32)


def row_loop(rows, chunk, body):
    chunk = min(chunk, rows)

    @pl.loop(0, rows // chunk)
    def _(t):
        body(pl.ds(pl.multiple_of(t * chunk, chunk), chunk))


def kernel(
    dims, gap, codes, flex, diri, modes, cinv, load, mult, res,
    stage, mats_hi, mats_lo, sel, sel_t, xs, xn, xa, vn, state, total, ahead,
    wide_w, mstk, cvec, vsrc, xrecv, comp, gath, part, redu, coef, call, rown, rnb, cpad, cmat, cblk,
    chi, clo, astk, arow, anat, bstk, tsend, tnb, kstk, psend, pnb,
    mat_sem, s1, r1, s2, r2, s3, r3, s4, r4, s5, r5, s6, r6, s7, r7, s8, r8,
):
    Z, X, Y = dims
    ni, rhs = gap.shape
    cap = ni // 4
    nq, np_ = Z * CORES, X * Y
    i = lax.axis_index("sub")
    j = lax.axis_index("layer")
    z, x = i // X, i % X
    subs, layers = Z * X, Y * CORES
    y, core = j // CORES, j % CORES
    q = z * CORES + core
    p = x * Y + y
    opp = (1, 0, 3, 2)

    def inside(di, dj):
        checks = []
        if di:
            checks.append(i + di >= 0 if di < 0 else i + di < subs)
        if dj:
            checks.append(j + dj >= 0 if dj < 0 else j + dj < layers)
        return checks[0] if len(checks) == 1 else jnp.logical_and(*checks)

    def clipped(di, dj):
        return (jnp.clip(i + di, 0, subs - 1), jnp.clip(j + dj, 0, layers - 1))

    has = [None] + [inside(*o) for o in OFFSETS[1:]]
    away = [None] + [clipped(*o) for o in OFFSETS[1:]]
    back = [OFFSETS.index((-o[0], -o[1])) for o in OFFSETS]
    far = len(OFFSETS)

    def ring(a, n):
        return min(a, n - a)

    line = sorted(
        ((dz, dc) for dz in range(Z) for dc in range(CORES) if dz or dc),
        key=lambda o: -ring(o[0], Z) - 0.5 * o[1],
    )
    plane = sorted(
        ((dx, dy) for dx in range(X) for dy in range(Y) if dx or dy),
        key=lambda o: -ring(o[0], X) - ring(o[1], Y),
    )
    line_to = [
        (((z + dz) % Z) * X + x, y * CORES + (core + dc) % CORES) for dz, dc in line
    ]
    plane_to = [
        (z * X + (x + dx) % X, ((y + dy) % Y) * CORES + core) for dx, dy in plane
    ]
    plane_at = [((x + dx) % X) * Y + (y + dy) % Y for dx, dy in plane]

    loads = [
        pltpu.make_async_copy(flex, stage.at[0], mat_sem.at[0]),
        pltpu.make_async_copy(diri, stage.at[1], mat_sem.at[1]),
    ]
    for cp in loads:
        cp.start()

    for buffer in (call, gath, redu):
        buffer[...] = jnp.zeros_like(buffer)
    pnb[...] = jnp.zeros_like(pnb)
    tnb[...] = jnp.zeros_like(tnb)
    for d in range(4):
        @pl.when(jnp.logical_not(has[d + 1]))
        def _():
            rnb[d] = jnp.zeros_like(rnb[d])

            @pl.loop(0, xrecv.shape[0])
            def _(k):
                xrecv[k, pl.ds(d * cap, cap), :] = jnp.zeros((cap, rhs), F32)

    barrier = pltpu.get_barrier_semaphore()

    def greet(device):
        pl.semaphore_signal(barrier, inc=1, device_id=device, device_id_type=MESH)

    for device in line_to + plane_to:
        greet(device)

    count = nq + np_ - 2
    for o in range(1, far):
        @pl.when(has[o])
        def _():
            greet(away[o])

        count = count + has[o].astype(jnp.int32)

    comp[0] = jnp.concatenate([load[...], jnp.zeros((8 - MODES, rhs), F32)], axis=0)

    cpad[...] = jnp.zeros_like(cpad)
    cpad[:MODES, : cinv.shape[1]] = cinv[...]
    cols_z = np_ * CORES * MODES
    lanes_z = np_ * CORES * 8
    window = cpad.shape[1] - (Z - 1) * cols_z // 128 * 128
    place = lax.broadcasted_iota(jnp.int32, (window, lanes_z), 0)
    target = lax.broadcasted_iota(jnp.int32, (window, lanes_z), 1)
    live = (place == target // 8 * MODES + target % 8) & (target % 8 < MODES)
    spread = jnp.where(live, 1.0, 0.0).astype(BF)
    slabs = []
    for t in range(Z):
        low = t * cols_z // 128 * 128
        slab = cpad[:, low : low + window]
        shift = t * cols_z % 128
        slabs.append(pltpu.roll(slab, window - shift, 1) if shift else slab)
    slab = jnp.concatenate(slabs, axis=0)
    c1 = slab.astype(BF)
    c2, c3 = split2(slab - c1.astype(F32))
    wide = dot(c1, spread) + (dot(c2, spread) + dot(c3, spread))
    group = lax.broadcasted_iota(jnp.int32, (8, nq * 8), 1) // (CORES * 8)
    for b in range(np_):
        low = b * CORES * 8 // (nq * 8) * (nq * 8)
        out = jnp.zeros((8, nq * 8), F32)
        for t in range(Z):
            piece = wide[8 * t : 8 * t + 8, low : low + nq * 8]
            shift = (t * CORES * 8 - (b * CORES * 8 - low)) % (nq * 8)
            out = jnp.where(group == t, pltpu.roll(piece, shift, 1) if shift else piece, out)
        cmat[b] = out

    pl.semaphore_wait(barrier, count)

    def remote(src, dst, send, recv, device):
        return pltpu.make_async_remote_copy(
            src_ref=src, dst_ref=dst, send_sem=send, recv_sem=recv,
            device_id=device, device_id_type=MESH,
        )

    def wait_bytes(ref, sem):
        pltpu.make_async_copy(ref, ref, sem).wait()

    few = pl.ds(0, MODES)

    def gather_start(k):
        gath[k, q] = comp[k]

        for device in line_to:
            remote(comp.at[k, few], gath.at[k, q, few], s1.at[k], r1.at[k], device).start()

    def near_start(src_of, dst_of, send, recv, k, many=5):
        for o in range(1, many):
            @pl.when(has[o])
            def _():
                remote(src_of(o), dst_of(back[o]), send.at[k, o], recv.at[k, back[o]], away[o]).start()

    def near_wait(ref_of, sem, k, many=5):
        for o in range(1, many):
            @pl.when(has[o])
            def _():
                wait_bytes(ref_of(o), sem.at[k, o])

    def slots(ref, k):
        return lambda o: ref.at[k, pl.ds((o - 1) * cap, cap), :]

    def rows8(ref, k):
        return lambda o: ref.at[k, pl.ds(8 * o, 8), :]

    gather_start(0)

    for device, at in zip(plane_to, plane_at):
        remote(cmat.at[at], cblk.at[p], s6.at[0], r6.at[0], device).start()

    cblk[p] = cmat[p]

    code_row = codes[...]
    for b in range(ni // 128):
        block = slice(b * 128, b * 128 + 128)
        slot = lax.broadcasted_iota(jnp.int32, (128, ni), 0) + b * 128
        sel[block, :] = jnp.where(code_row == slot, 1.0, 0.0).astype(BF)
        column = jnp.broadcast_to(code_row[:, block].astype(F32), (128, 128)).T.astype(jnp.int32)
        for c in range(ni // 128):
            lane = lax.broadcasted_iota(jnp.int32, (128, 128), 1) + c * 128
            sel_t[block, c * 128 : c * 128 + 128] = jnp.where(column == lane, 1.0, 0.0).astype(BF)

    wide = jnp.concatenate([modes[m] for m in range(MODES)] + [jnp.zeros((16 - MODES, ni), F32)], axis=0)
    m1 = wide.astype(BF)
    m2, m3 = split2(wide - m1.astype(F32))
    pieces = dot(jnp.concatenate([m1, m2, m3], axis=0), sel_t[...])
    rown[...] = pieces[:8] + (pieces[16:24] + pieces[32:40])

    near_start(lambda o: rown, lambda o: rnb.at[o - 1], s5, r5, 0)

    def split_mat(n):
        loads[n].wait()

        def body(rows):
            hi, lo = split2(stage[n, rows, :])
            mats_hi[n, rows, :] = hi
            mats_lo[n, rows, :] = lo

        row_loop(ni, 128, body)

    def put_pieces(rows, value, ref):
        hi, lo = split2(value)
        ref[rows, :rhs] = hi
        ref[rows, rhs:] = lo

    def both_halves(both):
        return both[:, :rhs] + both[:, rhs:]

    def to_rows(src, dst):
        def body(rows):
            dst[rows, :] = dot(sel_t[rows, :], src[...]).astype(BF)

        row_loop(ni, TALL, body)

    def multiply(n, src):
        def body(rows):
            both = dot(mats_hi[n, rows, :], src[...]) + dot(mats_lo[n, rows, :], src[...])
            put_pieces(rows, both_halves(both), vn)

        row_loop(ni, TALL, body)

    def to_slots(put):
        row_loop(ni, TALL, lambda rows: put(rows, both_halves(dot(sel[rows, :], vn[...]))))

    def put_ahead(rows, value):
        ahead[rows, :] = value

    def tall_pieces(value):
        hi = value.astype(BF)
        return jnp.concatenate([hi, (value - hi.astype(F32)).astype(BF)], axis=0)

    def skinny(lhs, rhs_pieces):
        out = dot(lhs, rhs_pieces)
        return out[:48, :rhs] + (out[:48, rhs:] + out[48:, :rhs])


    def coarse_scatter(k):
        wait_bytes(gath.at[k, pl.ds(0, nq - 1), few], r1.at[k])
        g_hi, g_lo = split2(gath[k].reshape(nq * 8, rhs))
        out = dot(chi[...], g_hi) + (dot(chi[...], g_lo) + dot(clo[...], g_hi))
        part[k] = out.reshape(np_, 8, rhs)

        for device, at in zip(plane_to, plane_at):
            remote(part.at[k, at, few], redu.at[k, p, few], s2.at[k], r2.at[k], device).start()

        redu[k, p] = part[k, p]

    def coarse_finish(k):
        wait_bytes(redu.at[k, pl.ds(0, np_ - 1), few], r2.at[k])
        coef[k] = jnp.sum(redu[k], axis=0)
        near_start(lambda o: coef.at[k, few], lambda o: call.at[k, o, few], s3, r3, k, far)

    wait_bytes(cblk.at[pl.ds(0, np_ - 1)], r6.at[0])
    hi, lo = split2(cblk[...].reshape(np_ * 8, nq * 8))
    chi[...] = hi
    clo[...] = lo
    coarse_scatter(0)
    split_mat(0)
    row_loop(ni, CHUNK, lambda rows: put_pieces(rows, -gap[rows, :], vn))
    to_slots(put_ahead)

    near_wait(lambda o: rnb.at[o - 1], r5, 0)
    lane = lax.broadcasted_iota(jnp.int32, (8, ni), 1)
    parts = [rown[...]]
    for d in range(4):
        moved = pltpu.roll(rnb[d], ((d - opp[d]) * cap) % ni, 1)
        live = (lane >= d * cap) & (lane < (d + 1) * cap)
        parts.append(jnp.where(live, -moved, 0.0))
    acols = jnp.concatenate(parts + [jnp.zeros((88, ni), F32)], axis=0)

    def stacked(cols):
        hi = cols.astype(BF).astype(F32)
        low = cols - hi
        return (hi + pltpu.roll(hi, 40, 1) + pltpu.roll(low, 80, 1)).astype(BF)

    arow[...] = tall_pieces(acols[:48])
    for b in range(ni // 128):
        block = slice(b * 128, b * 128 + 128)
        cols = acols[:, block].T
        astk[block, :] = stacked(cols)
        put_pieces(block, cols, xs)

    to_rows(xs, xa)

    def partial_start(k, lhs, pieces):
        psend[k] = skinny(lhs, pieces)
        near_start(rows8(psend, k), rows8(pnb, k), s7, r7, k)

    row_loop(ni, CHUNK, lambda rows: put_pieces(rows, ahead[rows, :], xs))
    partial_start(0, arow[...], xs[...])
    def around(k, base):
        picks = []
        for step in OFFSETS[:5]:
            o = OFFSETS.index((base[0] + step[0], base[1] + step[1]))
            picks.append(coef[k] if o == 0 else call[k, o])
        c = jnp.concatenate(picks, axis=0)
        c_hi = c.astype(BF).astype(F32)
        return jnp.concatenate(
            [c_hi, c - c_hi, c_hi, jnp.zeros((8, rhs), F32)], axis=0
        ).astype(BF)

    def prepare(n):
        multiply(n, xa)

        def put(rows, cols):
            mstk[n, rows, :] = stacked(cols)
            put_pieces(rows, cols, xs)

        to_slots(put)
        tsend[n] = skinny(arow[...], xs[...])
        near_start(rows8(tsend, n), rows8(tnb, n), s8, r8, n)

    def prepare_end(n):
        near_wait(rows8(tnb, n), r8, n)
        for o in range(5):
            block = tsend[n, 0:8, :] if o == 0 else tnb[n, 8 * o : 8 * o + 8, :]
            kstk[n, :, o * 128 : o * 128 + 128] = stacked(
                jnp.concatenate([block, jnp.zeros((8, 128), F32)], axis=0)
            )

    def prepare_rows(n):
        out = dot(anat[...], mats_hi[n])
        out = out[:48] + out[48:] + dot(anat[:48, :], mats_lo[n])
        out = dot(tall_pieces(out), sel_t[...])
        bstk[n] = tall_pieces(out[:48] + out[48:])

    def settle(n, last_new):
        share = jnp.where(n == 1, 1.0, 0.0)
        value = wide_w[...] + last_new * dot(astk[...], cvec[...])
        state[n] = value
        total[...] = total[...] + share * value

    prepare(0)
    coarse_finish(0)
    state[...] = jnp.zeros_like(state)
    prepare_end(0)

    @pl.loop(0, 5)
    def _(k):
        n = k % 2
        odd = n == 1
        last_new = jnp.where(odd | (k == 0), 1.0, jnp.where(k == 2, -0.5 / THETA, -RHO1 / DELTA))

        @pl.when(k > 0)
        def _():
            to_slots(put_ahead)

        near_wait(lambda o: call.at[k, o, few], r3, k, far)
        near_wait(rows8(pnb, k), r7, k)
        hood = [around(k, o) for o in OFFSETS[:5]]
        cvec[...] = hood[0]
        early = psend[k, 0:8, :]
        for o in range(1, 5):
            early = early + pnb[k, 8 * o : 8 * o + 8, :]
        moved = dot(kstk[n], jnp.concatenate(hood, axis=0))
        comp[k + 1] = early + last_new * moved[:8]
        gather_start(k + 1)
        vsrc[k] = ahead[...] + last_new * dot(mstk[n], cvec[...])
        near_start(slots(vsrc, k), slots(xrecv, k), s4, r4, k)

        @pl.when(k == 0)
        def _():
            total[...] = dot(astk[...], cvec[...])
            split_mat(1)
            anat[...] = dot(arow[...], sel[...]).astype(BF)
            prepare_rows(1)

        @pl.when(k > 0)
        def _():
            settle(1 - n, last_new)

        coarse_scatter(k + 1)

        @pl.when(k == 0)
        def _():
            prepare(1)

        @pl.when(k == 1)
        def _():
            prepare_rows(0)

        near_wait(slots(xrecv, k), r4, k)
        scale_old = jnp.where(odd, jnp.where(k == 1, 0.0, RHO1 * RHO0), 1.0)
        scale_new = jnp.where(odd, jnp.where(k == 1, 0.5 / THETA, RHO1 / DELTA), -1.0)

        def fresh(rows):
            jumped = vsrc[k, rows, :] - xrecv[k, rows, :]
            w = scale_old * state[n, rows, :] + scale_new * jumped
            wide_w[rows, :] = w
            put_pieces(rows, w, xs)

        row_loop(ni, CHUNK, fresh)

        @pl.when(k < 4)
        def _():
            partial_start(k + 1, bstk[1 - n], xs[...])
            to_rows(xs, xn)

        coarse_finish(k + 1)

        @pl.when(k < 4)
        def _():
            multiply(1 - n, xn)

        @pl.when(k == 0)
        def _():
            prepare_end(1)

    near_wait(lambda o: call.at[5, o, few], r3, 5, far)
    cvec[...] = around(5, (0, 0))
    settle(0, 1.0)
    row_loop(ni, CHUNK, lambda rows: put_pieces(rows, total[rows, :], xn))
    row_loop(ni, CHUNK, lambda rows: put_pieces(rows, state[0, rows, :], xs))

    def finish(rows):
        mult[rows, :] = both_halves(dot(sel_t[rows, :], xn[...]))
        res[rows, :] = both_halves(dot(sel_t[rows, :], xs[...]))

    row_loop(ni, TALL, finish)

    near_wait(lambda o: rown, s5, 0)
    wait_bytes(cblk.at[pl.ds(0, np_ - 1)], s6.at[0])
    for n in range(2):
        near_wait(rows8(tsend, n), s8, n)

    @pl.loop(0, 6)
    def _(k):
        wait_bytes(gath.at[k, pl.ds(0, nq - 1), few], s1.at[k])
        wait_bytes(redu.at[k, pl.ds(0, np_ - 1), few], s2.at[k])
        near_wait(lambda o: coef.at[k, few], s3, k, far)

    @pl.loop(0, 5)
    def _(k):
        near_wait(slots(vsrc, k), s4, k)
        near_wait(rows8(psend, k), s7, k)


def hand_over(mult, res, mult_out, res_out, held, come, leave):
    half = mult.shape[0] // 2
    pairs = ((mult, mult_out), (res, res_out))
    parts = [(n, h, pl.ds(h * half, half)) for n in range(2) for h in range(2)]
    arriving = [
        pltpu.make_async_copy(pairs[n][0].at[rows], held.at[n, rows], come.at[n, h])
        for n, h, rows in parts
    ]
    leaving = [
        pltpu.make_async_copy(held.at[n, rows], pairs[n][1].at[rows], leave.at[n, h])
        for n, h, rows in parts
    ]
    for copy in arriving:
        copy.start()
    for first, second in zip(arriving, leaving):
        first.wait()
        second.start()
    for copy in leaving:
        copy.wait()


def per_device(dims, local_gap, route_codes, flexibility, dirichlet, rigid_modes, coarse_inverse, rigid_load):
    ni, rhs = local_gap.shape[2:]
    Z, X, Y = dims
    nq, np_ = Z * CORES, X * Y
    cols_z = np_ * CORES * MODES
    window = (max(cols_z * t % 128 for t in range(Z)) + cols_z + 127) // 128 * 128
    far = len(OFFSETS)
    vmem = pl.BlockSpec(memory_space=pltpu.VMEM)
    hbm = pl.BlockSpec(memory_space=pl.ANY)
    field = jax.ShapeDtypeStruct((ni, rhs), F32)
    dma = pltpu.SemaphoreType.DMA
    V = pltpu.VMEM
    mult, res = pl.pallas_call(
        functools.partial(kernel, dims),
        out_shape=(field, field),
        in_specs=[vmem, vmem, hbm, hbm, vmem, vmem, vmem],
        out_specs=(vmem, vmem),
        scratch_shapes=[
            V((2, ni, ni), F32), V((2, ni, ni), BF), V((2, ni, ni), BF),
            V((ni, ni), BF), V((ni, ni), BF),
            V((ni, 2 * rhs), BF), V((ni, 2 * rhs), BF), V((ni, 2 * rhs), BF),
            V((ni, 2 * rhs), BF), V((2, ni, rhs), F32), V((ni, rhs), F32),
            V((ni, rhs), F32), V((ni, rhs), F32), V((2, ni, 128), BF),
            V((128, rhs), BF), V((5, ni, rhs), F32), V((5, ni, rhs), F32),
            V((6, 8, rhs), F32), V((6, nq, 8, rhs), F32),
            V((6, np_, 8, rhs), F32), V((6, np_, 8, rhs), F32),
            V((6, 8, rhs), F32), V((6, far, 8, rhs), F32),
            V((8, ni), F32), V((4, 8, ni), F32), V((8, (Z - 1) * cols_z // 128 * 128 + window), F32),
            V((np_, 8, nq * 8), F32), V((np_, 8, nq * 8), F32),
            V((np_ * 8, nq * 8), BF), V((np_ * 8, nq * 8), BF), V((ni, 128), BF),
            V((96, ni), BF), V((96, ni), BF), V((2, 96, ni), BF),
            V((2, 48, rhs), F32), V((2, 40, rhs), F32), V((2, 16, 640), BF),
            V((5, 48, rhs), F32), V((5, 40, rhs), F32),
            dma((2,)), dma((6,)), dma((6,)), dma((6,)), dma((6,)),
            dma((6, far)), dma((6, far)), dma((5, 5)), dma((5, 5)),
            dma((1, 5)), dma((1, 5)), dma((1,)), dma((1,)),
            dma((5, 5)), dma((5, 5)), dma((2, 5)), dma((2, 5)),
        ],
        compiler_params=pltpu.CompilerParams(
            collective_id=0, has_side_effects=True, vmem_limit_bytes=63 * 1024 * 1024
        ),
    )(
        local_gap[0, 0], route_codes[0], flexibility[0, 0], dirichlet[0, 0],
        rigid_modes.reshape(MODES, 1, ni), coarse_inverse, rigid_load,
    )
    hold = V((2, ni, rhs), F32)
    mult, res = pl.pallas_call(
        hand_over,
        out_shape=(field, field),
        in_specs=[hbm, hbm],
        out_specs=(hbm, hbm),
        scratch_shapes=[hold, dma((2, 2)), dma((2, 2))],
    )(mult, res)
    return mult[None, None], res[None, None]


def solution(mesh):
    placed = (
        P("sub", "layer", None, None),
        P("sub", "layer", None),
        P("sub", "layer", None, None),
        P("sub", "layer", None, None),
        P("sub", "layer", None, None),
        P(("sub", "layer"), None),
        P(("sub", "layer"), None),
    )
    subs, layers = mesh.shape["sub"], mesh.shape["layer"]
    across = 4 if subs % 4 == 0 and subs > 4 else 2
    dims = (subs // across, across, layers // CORES)
    return jax.shard_map(
        functools.partial(per_device, dims),
        mesh=mesh,
        in_specs=placed,
        out_specs=(P("sub", "layer", None, None), P("sub", "layer", None, None)),
        check_vma=False,
    )
```

```python
import functools

import jax
import jax.numpy as jnp
from jax import lax
from jax.experimental import pallas as pl
from jax.experimental.pallas import tpu as pltpu
from jax.sharding import PartitionSpec as P

MESH = pl.DeviceIdType.MESH
THETA = 4.25
DELTA = 3.75
SIGMA = THETA / DELTA
RHO0 = DELTA / THETA
RHO1 = 1.0 / (2.0 * SIGMA - RHO0)
CORES = 2
MODES = 6
BF = jnp.bfloat16
F32 = jnp.float32
CHUNK = 384
TALL = 576
OFFSETS = [
    (0, 0), (-1, 0), (1, 0), (0, -1), (0, 1), (-2, 0), (2, 0),
    (0, -2), (0, 2), (-1, -1), (-1, 1), (1, -1), (1, 1),
]


def split2(v):
    hi = v.astype(BF)
    lo = (v - hi.astype(F32)).astype(BF)
    return hi, lo


def dot(a, b):
    return jnp.dot(a, b, preferred_element_type=F32)


def row_loop(rows, chunk, body):
    chunk = min(chunk, rows)

    @pl.loop(0, rows // chunk)
    def _(t):
        body(pl.ds(pl.multiple_of(t * chunk, chunk), chunk))


def kernel(
    dims, gap, codes, flex, diri, modes, cinv, load, mult, res,
    stage, mats_hi, mats_lo, sel, sel_t, xs, xn, xa, vn, state, total, ahead,
    wide_w, mstk, cvec, vsrc, xrecv, comp, gath, part, redu, coef, call, rown, rnb, cpad, cmat, cblk,
    chi, clo, astk, arow, anat, bstk, tsend, tnb, kstk, psend, pnb,
    mat_sem, s1, r1, s2, r2, s3, r3, s4, r4, s5, r5, s6, r6, s7, r7, s8, r8,
):
    Z, X, Y = dims
    ni, rhs = gap.shape
    cap = ni // 4
    nq, np_ = Z * CORES, X * Y
    i = lax.axis_index("sub")
    j = lax.axis_index("layer")
    z, x = i // X, i % X
    subs, layers = Z * X, Y * CORES
    y, core = j // CORES, j % CORES
    q = z * CORES + core
    p = x * Y + y
    opp = (1, 0, 3, 2)

    def inside(di, dj):
        checks = []
        if di:
            checks.append(i + di >= 0 if di < 0 else i + di < subs)
        if dj:
            checks.append(j + dj >= 0 if dj < 0 else j + dj < layers)
        return checks[0] if len(checks) == 1 else jnp.logical_and(*checks)

    def clipped(di, dj):
        return (jnp.clip(i + di, 0, subs - 1), jnp.clip(j + dj, 0, layers - 1))

    has = [None] + [inside(*o) for o in OFFSETS[1:]]
    away = [None] + [clipped(*o) for o in OFFSETS[1:]]
    back = [OFFSETS.index((-o[0], -o[1])) for o in OFFSETS]
    far = len(OFFSETS)

    def ring(a, n):
        return min(a, n - a)

    line = sorted(
        ((dz, dc) for dz in range(Z) for dc in range(CORES) if dz or dc),
        key=lambda o: -ring(o[0], Z) - 0.5 * o[1],
    )
    plane = sorted(
        ((dx, dy) for dx in range(X) for dy in range(Y) if dx or dy),
        key=lambda o: -ring(o[0], X) - ring(o[1], Y),
    )
    line_to = [
        (((z + dz) % Z) * X + x, y * CORES + (core + dc) % CORES) for dz, dc in line
    ]
    plane_to = [
        (z * X + (x + dx) % X, ((y + dy) % Y) * CORES + core) for dx, dy in plane
    ]
    plane_at = [((x + dx) % X) * Y + (y + dy) % Y for dx, dy in plane]

    loads = [
        pltpu.make_async_copy(flex, stage.at[0], mat_sem.at[0]),
        pltpu.make_async_copy(diri, stage.at[1], mat_sem.at[1]),
    ]
    for cp in loads:
        cp.start()

    for buffer in (call, gath, redu):
        buffer[...] = jnp.zeros_like(buffer)
    pnb[...] = jnp.zeros_like(pnb)
    tnb[...] = jnp.zeros_like(tnb)
    for d in range(4):
        @pl.when(jnp.logical_not(has[d + 1]))
        def _():
            rnb[d] = jnp.zeros_like(rnb[d])

            @pl.loop(0, xrecv.shape[0])
            def _(k):
                xrecv[k, pl.ds(d * cap, cap), :] = jnp.zeros((cap, rhs), F32)

    barrier = pltpu.get_barrier_semaphore()

    def greet(device):
        pl.semaphore_signal(barrier, inc=1, device_id=device, device_id_type=MESH)

    for device in line_to + plane_to:
        greet(device)

    count = nq + np_ - 2
    for o in range(1, far):
        @pl.when(has[o])
        def _():
            greet(away[o])

        count = count + has[o].astype(jnp.int32)

    comp[0] = jnp.concatenate([load[...], jnp.zeros((8 - MODES, rhs), F32)], axis=0)

    cpad[...] = jnp.zeros_like(cpad)
    cpad[:MODES, : cinv.shape[1]] = cinv[...]
    cols_z = np_ * CORES * MODES
    lanes_z = np_ * CORES * 8
    window = cpad.shape[1] - (Z - 1) * cols_z // 128 * 128
    place = lax.broadcasted_iota(jnp.int32, (window, lanes_z), 0)
    target = lax.broadcasted_iota(jnp.int32, (window, lanes_z), 1)
    live = (place == target // 8 * MODES + target % 8) & (target % 8 < MODES)
    spread = jnp.where(live, 1.0, 0.0).astype(BF)
    slabs = []
    for t in range(Z):
        low = t * cols_z // 128 * 128
        slab = cpad[:, low : low + window]
        shift = t * cols_z % 128
        slabs.append(pltpu.roll(slab, window - shift, 1) if shift else slab)
    slab = jnp.concatenate(slabs, axis=0)
    c1 = slab.astype(BF)
    c2, c3 = split2(slab - c1.astype(F32))
    wide = dot(c1, spread) + (dot(c2, spread) + dot(c3, spread))
    group = lax.broadcasted_iota(jnp.int32, (8, nq * 8), 1) // (CORES * 8)
    for b in range(np_):
        low = b * CORES * 8 // (nq * 8) * (nq * 8)
        out = jnp.zeros((8, nq * 8), F32)
        for t in range(Z):
            piece = wide[8 * t : 8 * t + 8, low : low + nq * 8]
            shift = (t * CORES * 8 - (b * CORES * 8 - low)) % (nq * 8)
            out = jnp.where(group == t, pltpu.roll(piece, shift, 1) if shift else piece, out)
        cmat[b] = out

    pl.semaphore_wait(barrier, count)

    def remote(src, dst, send, recv, device):
        return pltpu.make_async_remote_copy(
            src_ref=src, dst_ref=dst, send_sem=send, recv_sem=recv,
            device_id=device, device_id_type=MESH,
        )

    def wait_bytes(ref, sem):
        pltpu.make_async_copy(ref, ref, sem).wait()

    few = pl.ds(0, MODES)

    def gather_start(k):
        gath[k, q] = comp[k]

        for device in line_to:
            remote(comp.at[k, few], gath.at[k, q, few], s1.at[k], r1.at[k], device).start()

    def near_start(src_of, dst_of, send, recv, k, many=5):
        for o in range(1, many):
            @pl.when(has[o])
            def _():
                remote(src_of(o), dst_of(back[o]), send.at[k, o], recv.at[k, back[o]], away[o]).start()

    def near_wait(ref_of, sem, k, many=5):
        for o in range(1, many):
            @pl.when(has[o])
            def _():
                wait_bytes(ref_of(o), sem.at[k, o])

    def slots(ref, k):
        return lambda o: ref.at[k, pl.ds((o - 1) * cap, cap), :]

    def rows8(ref, k):
        return lambda o: ref.at[k, pl.ds(8 * o, 8), :]

    gather_start(0)

    for device, at in zip(plane_to, plane_at):
        remote(cmat.at[at], cblk.at[p], s6.at[0], r6.at[0], device).start()

    cblk[p] = cmat[p]

    code_row = codes[...]
    for b in range(ni // 128):
        block = slice(b * 128, b * 128 + 128)
        slot = lax.broadcasted_iota(jnp.int32, (128, ni), 0) + b * 128
        sel[block, :] = jnp.where(code_row == slot, 1.0, 0.0).astype(BF)
        column = jnp.broadcast_to(code_row[:, block].astype(F32), (128, 128)).T.astype(jnp.int32)
        for c in range(ni // 128):
            lane = lax.broadcasted_iota(jnp.int32, (128, 128), 1) + c * 128
            sel_t[block, c * 128 : c * 128 + 128] = jnp.where(column == lane, 1.0, 0.0).astype(BF)

    wide = jnp.concatenate([modes[m] for m in range(MODES)] + [jnp.zeros((16 - MODES, ni), F32)], axis=0)
    m1 = wide.astype(BF)
    m2, m3 = split2(wide - m1.astype(F32))
    pieces = dot(jnp.concatenate([m1, m2, m3], axis=0), sel_t[...])
    rown[...] = pieces[:8] + (pieces[16:24] + pieces[32:40])

    near_start(lambda o: rown, lambda o: rnb.at[o - 1], s5, r5, 0)

    def split_mat(n):
        loads[n].wait()

        def body(rows):
            hi, lo = split2(stage[n, rows, :])
            mats_hi[n, rows, :] = hi
            mats_lo[n, rows, :] = lo

        row_loop(ni, 128, body)

    def put_pieces(rows, value, ref):
        hi, lo = split2(value)
        ref[rows, :rhs] = hi
        ref[rows, rhs:] = lo

    def both_halves(both):
        return both[:, :rhs] + both[:, rhs:]

    def to_rows(src, dst):
        def body(rows):
            dst[rows, :] = dot(sel_t[rows, :], src[...]).astype(BF)

        row_loop(ni, TALL, body)

    def multiply(n, src):
        def body(rows):
            both = dot(mats_hi[n, rows, :], src[...]) + dot(mats_lo[n, rows, :], src[...])
            put_pieces(rows, both_halves(both), vn)

        row_loop(ni, TALL, body)

    def to_slots(put):
        row_loop(ni, TALL, lambda rows: put(rows, both_halves(dot(sel[rows, :], vn[...]))))

    def put_ahead(rows, value):
        ahead[rows, :] = value

    def tall_pieces(value):
        hi = value.astype(BF)
        return jnp.concatenate([hi, (value - hi.astype(F32)).astype(BF)], axis=0)

    def skinny(lhs, rhs_pieces):
        out = dot(lhs, rhs_pieces)
        return out[:48, :rhs] + (out[:48, rhs:] + out[48:, :rhs])


    def coarse_scatter(k):
        wait_bytes(gath.at[k, pl.ds(0, nq - 1), few], r1.at[k])
        g_hi, g_lo = split2(gath[k].reshape(nq * 8, rhs))
        out = dot(chi[...], g_hi) + (dot(chi[...], g_lo) + dot(clo[...], g_hi))
        part[k] = out.reshape(np_, 8, rhs)

        for device, at in zip(plane_to, plane_at):
            remote(part.at[k, at, few], redu.at[k, p, few], s2.at[k], r2.at[k], device).start()

        redu[k, p] = part[k, p]

    def coarse_finish(k):
        wait_bytes(redu.at[k, pl.ds(0, np_ - 1), few], r2.at[k])
        coef[k] = jnp.sum(redu[k], axis=0)
        near_start(lambda o: coef.at[k, few], lambda o: call.at[k, o, few], s3, r3, k, far)

    split_mat(0)
    row_loop(ni, CHUNK, lambda rows: put_pieces(rows, -gap[rows, :], vn))
    to_slots(put_ahead)

    near_wait(lambda o: rnb.at[o - 1], r5, 0)
    lane = lax.broadcasted_iota(jnp.int32, (8, ni), 1)
    parts = [rown[...]]
    for d in range(4):
        moved = pltpu.roll(rnb[d], ((d - opp[d]) * cap) % ni, 1)
        live = (lane >= d * cap) & (lane < (d + 1) * cap)
        parts.append(jnp.where(live, -moved, 0.0))
    acols = jnp.concatenate(parts + [jnp.zeros((88, ni), F32)], axis=0)

    def stacked(cols):
        hi = cols.astype(BF).astype(F32)
        low = cols - hi
        return (hi + pltpu.roll(hi, 40, 1) + pltpu.roll(low, 80, 1)).astype(BF)

    arow[...] = tall_pieces(acols[:48])
    for b in range(ni // 128):
        block = slice(b * 128, b * 128 + 128)
        cols = acols[:, block].T
        astk[block, :] = stacked(cols)
        put_pieces(block, cols, xs)

    wait_bytes(cblk.at[pl.ds(0, np_ - 1)], r6.at[0])
    hi, lo = split2(cblk[...].reshape(np_ * 8, nq * 8))
    chi[...] = hi
    clo[...] = lo
    coarse_scatter(0)
    to_rows(xs, xa)

    def partial_start(k, lhs, pieces):
        psend[k] = skinny(lhs, pieces)
        near_start(rows8(psend, k), rows8(pnb, k), s7, r7, k)

    row_loop(ni, CHUNK, lambda rows: put_pieces(rows, ahead[rows, :], xs))
    partial_start(0, arow[...], xs[...])
    def around(k, base):
        picks = []
        for step in OFFSETS[:5]:
            o = OFFSETS.index((base[0] + step[0], base[1] + step[1]))
            picks.append(coef[k] if o == 0 else call[k, o])
        c = jnp.concatenate(picks, axis=0)
        c_hi = c.astype(BF).astype(F32)
        return jnp.concatenate(
            [c_hi, c - c_hi, c_hi, jnp.zeros((8, rhs), F32)], axis=0
        ).astype(BF)

    def prepare(n):
        multiply(n, xa)
        if n == 0:
            coarse_finish(0)

        def put(rows, cols):
            mstk[n, rows, :] = stacked(cols)
            put_pieces(rows, cols, xs)

        to_slots(put)
        tsend[n] = skinny(arow[...], xs[...])
        near_start(rows8(tsend, n), rows8(tnb, n), s8, r8, n)

    def prepare_end(n):
        near_wait(rows8(tnb, n), r8, n)
        for o in range(5):
            block = tsend[n, 0:8, :] if o == 0 else tnb[n, 8 * o : 8 * o + 8, :]
            kstk[n, :, o * 128 : o * 128 + 128] = stacked(
                jnp.concatenate([block, jnp.zeros((8, 128), F32)], axis=0)
            )

    def prepare_rows(n):
        out = dot(anat[...], mats_hi[n])
        out = out[:48] + out[48:] + dot(anat[:48, :], mats_lo[n])
        out = dot(tall_pieces(out), sel_t[...])
        bstk[n] = tall_pieces(out[:48] + out[48:])

    def settle(n, last_new):
        share = jnp.where(n == 1, 1.0, 0.0)
        value = wide_w[...] + last_new * dot(astk[...], cvec[...])
        state[n] = value
        total[...] = total[...] + share * value

    prepare(0)
    state[...] = jnp.zeros_like(state)
    prepare_end(0)

    @pl.loop(0, 5)
    def _(k):
        n = k % 2
        odd = n == 1
        last_new = jnp.where(odd | (k == 0), 1.0, jnp.where(k == 2, -0.5 / THETA, -RHO1 / DELTA))

        @pl.when(k > 0)
        def _():
            to_slots(put_ahead)

        near_wait(lambda o: call.at[k, o, few], r3, k, far)
        near_wait(rows8(pnb, k), r7, k)
        hood = [around(k, o) for o in OFFSETS[:5]]
        cvec[...] = hood[0]
        early = psend[k, 0:8, :]
        for o in range(1, 5):
            early = early + pnb[k, 8 * o : 8 * o + 8, :]
        moved = dot(kstk[n], jnp.concatenate(hood, axis=0))
        comp[k + 1] = early + last_new * moved[:8]
        gather_start(k + 1)
        vsrc[k] = ahead[...] + last_new * dot(mstk[n], cvec[...])
        near_start(slots(vsrc, k), slots(xrecv, k), s4, r4, k)

        @pl.when(k == 0)
        def _():
            total[...] = dot(astk[...], cvec[...])
            split_mat(1)
            anat[...] = dot(arow[...], sel[...]).astype(BF)
            prepare_rows(1)

        @pl.when(k > 0)
        def _():
            settle(1 - n, last_new)

        coarse_scatter(k + 1)

        @pl.when(k == 0)
        def _():
            prepare(1)

        @pl.when(k == 1)
        def _():
            prepare_rows(0)

        coarse_finish(k + 1)
        near_wait(slots(xrecv, k), r4, k)
        scale_old = jnp.where(odd, jnp.where(k == 1, 0.0, RHO1 * RHO0), 1.0)
        scale_new = jnp.where(odd, jnp.where(k == 1, 0.5 / THETA, RHO1 / DELTA), -1.0)

        def fresh(rows):
            jumped = vsrc[k, rows, :] - xrecv[k, rows, :]
            w = scale_old * state[n, rows, :] + scale_new * jumped
            wide_w[rows, :] = w
            put_pieces(rows, w, xs)

        row_loop(ni, CHUNK, fresh)

        @pl.when(k < 4)
        def _():
            partial_start(k + 1, bstk[1 - n], xs[...])
            to_rows(xs, xn)
            multiply(1 - n, xn)

        @pl.when(k == 0)
        def _():
            prepare_end(1)

    near_wait(lambda o: call.at[5, o, few], r3, 5, far)
    cvec[...] = around(5, (0, 0))
    settle(0, 1.0)
    row_loop(ni, CHUNK, lambda rows: put_pieces(rows, total[rows, :], xn))
    row_loop(ni, CHUNK, lambda rows: put_pieces(rows, state[0, rows, :], xs))

    def finish(rows):
        mult[rows, :] = both_halves(dot(sel_t[rows, :], xn[...]))
        res[rows, :] = both_halves(dot(sel_t[rows, :], xs[...]))

    row_loop(ni, TALL, finish)

    near_wait(lambda o: rown, s5, 0)
    wait_bytes(cblk.at[pl.ds(0, np_ - 1)], s6.at[0])
    for n in range(2):
        near_wait(rows8(tsend, n), s8, n)

    @pl.loop(0, 6)
    def _(k):
        wait_bytes(gath.at[k, pl.ds(0, nq - 1), few], s1.at[k])
        wait_bytes(redu.at[k, pl.ds(0, np_ - 1), few], s2.at[k])
        near_wait(lambda o: coef.at[k, few], s3, k, far)

    @pl.loop(0, 5)
    def _(k):
        near_wait(slots(vsrc, k), s4, k)
        near_wait(rows8(psend, k), s7, k)


def hand_over(mult, res, mult_out, res_out, held, come, leave):
    half = mult.shape[0] // 2
    pairs = ((mult, mult_out), (res, res_out))
    parts = [(n, h, pl.ds(h * half, half)) for n in range(2) for h in range(2)]
    arriving = [
        pltpu.make_async_copy(pairs[n][0].at[rows], held.at[n, rows], come.at[n, h])
        for n, h, rows in parts
    ]
    leaving = [
        pltpu.make_async_copy(held.at[n, rows], pairs[n][1].at[rows], leave.at[n, h])
        for n, h, rows in parts
    ]
    for copy in arriving:
        copy.start()
    for first, second in zip(arriving, leaving):
        first.wait()
        second.start()
    for copy in leaving:
        copy.wait()


def per_device(dims, local_gap, route_codes, flexibility, dirichlet, rigid_modes, coarse_inverse, rigid_load):
    ni, rhs = local_gap.shape[2:]
    Z, X, Y = dims
    nq, np_ = Z * CORES, X * Y
    cols_z = np_ * CORES * MODES
    window = (max(cols_z * t % 128 for t in range(Z)) + cols_z + 127) // 128 * 128
    far = len(OFFSETS)
    vmem = pl.BlockSpec(memory_space=pltpu.VMEM)
    hbm = pl.BlockSpec(memory_space=pl.ANY)
    field = jax.ShapeDtypeStruct((ni, rhs), F32)
    dma = pltpu.SemaphoreType.DMA
    V = pltpu.VMEM
    mult, res = pl.pallas_call(
        functools.partial(kernel, dims),
        out_shape=(field, field),
        in_specs=[vmem, vmem, hbm, hbm, vmem, vmem, vmem],
        out_specs=(vmem, vmem),
        scratch_shapes=[
            V((2, ni, ni), F32), V((2, ni, ni), BF), V((2, ni, ni), BF),
            V((ni, ni), BF), V((ni, ni), BF),
            V((ni, 2 * rhs), BF), V((ni, 2 * rhs), BF), V((ni, 2 * rhs), BF),
            V((ni, 2 * rhs), BF), V((2, ni, rhs), F32), V((ni, rhs), F32),
            V((ni, rhs), F32), V((ni, rhs), F32), V((2, ni, 128), BF),
            V((128, rhs), BF), V((5, ni, rhs), F32), V((5, ni, rhs), F32),
            V((6, 8, rhs), F32), V((6, nq, 8, rhs), F32),
            V((6, np_, 8, rhs), F32), V((6, np_, 8, rhs), F32),
            V((6, 8, rhs), F32), V((6, far, 8, rhs), F32),
            V((8, ni), F32), V((4, 8, ni), F32), V((8, (Z - 1) * cols_z // 128 * 128 + window), F32),
            V((np_, 8, nq * 8), F32), V((np_, 8, nq * 8), F32),
            V((np_ * 8, nq * 8), BF), V((np_ * 8, nq * 8), BF), V((ni, 128), BF),
            V((96, ni), BF), V((96, ni), BF), V((2, 96, ni), BF),
            V((2, 48, rhs), F32), V((2, 40, rhs), F32), V((2, 16, 640), BF),
            V((5, 48, rhs), F32), V((5, 40, rhs), F32),
            dma((2,)), dma((6,)), dma((6,)), dma((6,)), dma((6,)),
            dma((6, far)), dma((6, far)), dma((5, 5)), dma((5, 5)),
            dma((1, 5)), dma((1, 5)), dma((1,)), dma((1,)),
            dma((5, 5)), dma((5, 5)), dma((2, 5)), dma((2, 5)),
        ],
        compiler_params=pltpu.CompilerParams(
            collective_id=0, has_side_effects=True, vmem_limit_bytes=63 * 1024 * 1024
        ),
    )(
        local_gap[0, 0], route_codes[0], flexibility[0, 0], dirichlet[0, 0],
        rigid_modes.reshape(MODES, 1, ni), coarse_inverse, rigid_load,
    )
    hold = V((2, ni, rhs), F32)
    mult, res = pl.pallas_call(
        hand_over,
        out_shape=(field, field),
        in_specs=[hbm, hbm],
        out_specs=(hbm, hbm),
        scratch_shapes=[hold, dma((2, 2)), dma((2, 2))],
    )(mult, res)
    return mult[None, None], res[None, None]


def solution(mesh):
    placed = (
        P("sub", "layer", None, None),
        P("sub", "layer", None),
        P("sub", "layer", None, None),
        P("sub", "layer", None, None),
        P("sub", "layer", None, None),
        P(("sub", "layer"), None),
        P(("sub", "layer"), None),
    )
    subs, layers = mesh.shape["sub"], mesh.shape["layer"]
    across = 4 if subs % 4 == 0 and subs > 4 else 2
    dims = (subs // across, across, layers // CORES)
    return jax.shard_map(
        functools.partial(per_device, dims),
        mesh=mesh,
        in_specs=placed,
        out_specs=(P("sub", "layer", None, None), P("sub", "layer", None, None)),
        check_vma=False,
    )
```

```python
import functools

import jax
import jax.numpy as jnp
from jax import lax
from jax.experimental import pallas as pl
from jax.experimental.pallas import tpu as pltpu
from jax.sharding import PartitionSpec as P

MESH = pl.DeviceIdType.MESH
THETA = 4.25
DELTA = 3.75
SIGMA = THETA / DELTA
RHO0 = DELTA / THETA
RHO1 = 1.0 / (2.0 * SIGMA - RHO0)
CORES = 2
MODES = 6
BF = jnp.bfloat16
F32 = jnp.float32
CHUNK = 384
TALL = 576
OFFSETS = [
    (0, 0), (-1, 0), (1, 0), (0, -1), (0, 1), (-2, 0), (2, 0),
    (0, -2), (0, 2), (-1, -1), (-1, 1), (1, -1), (1, 1),
]


def split2(v):
    hi = v.astype(BF)
    lo = (v - hi.astype(F32)).astype(BF)
    return hi, lo


def dot(a, b):
    return jnp.dot(a, b, preferred_element_type=F32)


def row_loop(rows, chunk, body):
    chunk = min(chunk, rows)

    @pl.loop(0, rows // chunk)
    def _(t):
        body(pl.ds(pl.multiple_of(t * chunk, chunk), chunk))


def kernel(
    dims, gap, codes, flex, diri, modes, cinv, load, mult, res,
    stage, mats_hi, mats_lo, sel, sel_t, xs, xn, xa, vn, state, total,
    wide_w, masend, marecv, mstk, cvec, hood, vsrc, xrecv, comp, gath, part, redu, coef, call, rown, rnb, cpad, cmat, cblk,
    chi, clo, astk, arow, anat, bstk, tsend, tnb, kstk, psend, pnb,
    mat_sem, s1, r1, s2, r2, s3, r3, s4, r4, s5, r5, s6, r6, s7, r7, s8, r8, s9, r9,
):
    Z, X, Y = dims
    ni, rhs = gap.shape
    cap = ni // 4
    nq, np_ = Z * CORES, X * Y
    i = lax.axis_index("sub")
    j = lax.axis_index("layer")
    z, x = i // X, i % X
    subs, layers = Z * X, Y * CORES
    y, core = j // CORES, j % CORES
    q = z * CORES + core
    p = x * Y + y
    opp = (1, 0, 3, 2)

    def inside(di, dj):
        checks = []
        if di:
            checks.append(i + di >= 0 if di < 0 else i + di < subs)
        if dj:
            checks.append(j + dj >= 0 if dj < 0 else j + dj < layers)
        return checks[0] if len(checks) == 1 else jnp.logical_and(*checks)

    def clipped(di, dj):
        return (jnp.clip(i + di, 0, subs - 1), jnp.clip(j + dj, 0, layers - 1))

    has = [None] + [inside(*o) for o in OFFSETS[1:]]
    away = [None] + [clipped(*o) for o in OFFSETS[1:]]
    back = [OFFSETS.index((-o[0], -o[1])) for o in OFFSETS]
    far = len(OFFSETS)

    def ring(a, n):
        return min(a, n - a)

    line = sorted(
        ((dz, dc) for dz in range(Z) for dc in range(CORES) if dz or dc),
        key=lambda o: -ring(o[0], Z) - 0.5 * o[1],
    )
    plane = sorted(
        ((dx, dy) for dx in range(X) for dy in range(Y) if dx or dy),
        key=lambda o: -ring(o[0], X) - ring(o[1], Y),
    )
    line_to = [
        (((z + dz) % Z) * X + x, y * CORES + (core + dc) % CORES) for dz, dc in line
    ]
    plane_to = [
        (z * X + (x + dx) % X, ((y + dy) % Y) * CORES + core) for dx, dy in plane
    ]
    plane_at = [((x + dx) % X) * Y + (y + dy) % Y for dx, dy in plane]

    loads = [
        pltpu.make_async_copy(flex, stage.at[0], mat_sem.at[0]),
        pltpu.make_async_copy(diri, stage.at[1], mat_sem.at[1]),
    ]
    for cp in loads:
        cp.start()

    for buffer in (call, gath, redu):
        buffer[...] = jnp.zeros_like(buffer)
    pnb[...] = jnp.zeros_like(pnb)
    tnb[...] = jnp.zeros_like(tnb)
    for d in range(4):
        @pl.when(jnp.logical_not(has[d + 1]))
        def _():
            rnb[d] = jnp.zeros_like(rnb[d])

            @pl.loop(0, xrecv.shape[0])
            def _(k):
                xrecv[k, pl.ds(d * cap, cap), :] = jnp.zeros((cap, rhs), F32)

            @pl.loop(0, 2)
            def _(n):
                marecv[n, pl.ds(d * cap, cap), :] = jnp.zeros((cap, 128), F32)

    barrier = pltpu.get_barrier_semaphore()

    def greet(device):
        pl.semaphore_signal(barrier, inc=1, device_id=device, device_id_type=MESH)

    for device in line_to + plane_to:
        greet(device)

    count = nq + np_ - 2
    for o in range(1, far):
        @pl.when(has[o])
        def _():
            greet(away[o])

        count = count + has[o].astype(jnp.int32)

    comp[0] = jnp.concatenate([load[...], jnp.zeros((8 - MODES, rhs), F32)], axis=0)

    cpad[...] = jnp.zeros_like(cpad)
    cpad[:MODES, : cinv.shape[1]] = cinv[...]
    cols_z = np_ * CORES * MODES
    lanes_z = np_ * CORES * 8
    window = cpad.shape[1] - (Z - 1) * cols_z // 128 * 128
    place = lax.broadcasted_iota(jnp.int32, (window, lanes_z), 0)
    target = lax.broadcasted_iota(jnp.int32, (window, lanes_z), 1)
    live = (place == target // 8 * MODES + target % 8) & (target % 8 < MODES)
    spread = jnp.where(live, 1.0, 0.0).astype(BF)
    slabs = []
    for t in range(Z):
        low = t * cols_z // 128 * 128
        slab = cpad[:, low : low + window]
        shift = t * cols_z % 128
        slabs.append(pltpu.roll(slab, window - shift, 1) if shift else slab)
    slab = jnp.concatenate(slabs, axis=0)
    c1 = slab.astype(BF)
    c2, c3 = split2(slab - c1.astype(F32))
    wide = dot(c1, spread) + (dot(c2, spread) + dot(c3, spread))
    group = lax.broadcasted_iota(jnp.int32, (8, nq * 8), 1) // (CORES * 8)
    for b in range(np_):
        low = b * CORES * 8 // (nq * 8) * (nq * 8)
        out = jnp.zeros((8, nq * 8), F32)
        for t in range(Z):
            piece = wide[8 * t : 8 * t + 8, low : low + nq * 8]
            shift = (t * CORES * 8 - (b * CORES * 8 - low)) % (nq * 8)
            out = jnp.where(group == t, pltpu.roll(piece, shift, 1) if shift else piece, out)
        cmat[b] = out

    pl.semaphore_wait(barrier, count)

    def remote(src, dst, send, recv, device):
        return pltpu.make_async_remote_copy(
            src_ref=src, dst_ref=dst, send_sem=send, recv_sem=recv,
            device_id=device, device_id_type=MESH,
        )

    def wait_bytes(ref, sem):
        pltpu.make_async_copy(ref, ref, sem).wait()

    few = pl.ds(0, MODES)

    def gather_start(k):
        gath[k, q] = comp[k]

        for device in line_to:
            remote(comp.at[k, few], gath.at[k, q, few], s1.at[k], r1.at[k], device).start()

    def near_start(src_of, dst_of, send, recv, k, many=5):
        for o in range(1, many):
            @pl.when(has[o])
            def _():
                remote(src_of(o), dst_of(back[o]), send.at[k, o], recv.at[k, back[o]], away[o]).start()

    def near_wait(ref_of, sem, k, many=5):
        for o in range(1, many):
            @pl.when(has[o])
            def _():
                wait_bytes(ref_of(o), sem.at[k, o])

    def slots(ref, k):
        return lambda o: ref.at[k, pl.ds((o - 1) * cap, cap), :]

    def rows8(ref, k):
        return lambda o: ref.at[k, pl.ds(8 * o, 8), :]

    gather_start(0)

    for device, at in zip(plane_to, plane_at):
        remote(cmat.at[at], cblk.at[p], s6.at[0], r6.at[0], device).start()

    cblk[p] = cmat[p]

    code_row = codes[...]
    for b in range(ni // 128):
        block = slice(b * 128, b * 128 + 128)
        slot = lax.broadcasted_iota(jnp.int32, (128, ni), 0) + b * 128
        sel[block, :] = jnp.where(code_row == slot, 1.0, 0.0).astype(BF)
        column = jnp.broadcast_to(code_row[:, block].astype(F32), (128, 128)).T.astype(jnp.int32)
        for c in range(ni // 128):
            lane = lax.broadcasted_iota(jnp.int32, (128, 128), 1) + c * 128
            sel_t[block, c * 128 : c * 128 + 128] = jnp.where(column == lane, 1.0, 0.0).astype(BF)

    wide = jnp.concatenate([modes[m] for m in range(MODES)] + [jnp.zeros((16 - MODES, ni), F32)], axis=0)
    m1 = wide.astype(BF)
    m2, m3 = split2(wide - m1.astype(F32))
    pieces = dot(jnp.concatenate([m1, m2, m3], axis=0), sel_t[...])
    rown[...] = pieces[:8] + (pieces[16:24] + pieces[32:40])

    near_start(lambda o: rown, lambda o: rnb.at[o - 1], s5, r5, 0)

    def split_mat(n):
        loads[n].wait()

        def body(rows):
            hi, lo = split2(stage[n, rows, :])
            mats_hi[n, rows, :] = hi
            mats_lo[n, rows, :] = lo

        row_loop(ni, 128, body)

    def put_pieces(rows, value, ref):
        hi, lo = split2(value)
        ref[rows, :rhs] = hi
        ref[rows, rhs:] = lo

    def both_halves(both):
        return both[:, :rhs] + both[:, rhs:]

    def to_rows(src, dst):
        def body(rows):
            dst[rows, :] = dot(sel_t[rows, :], src[...]).astype(BF)

        row_loop(ni, TALL, body)

    def multiply(n, src):
        def body(rows):
            both = dot(mats_hi[n, rows, :], src[...]) + dot(mats_lo[n, rows, :], src[...])
            put_pieces(rows, both_halves(both), vn)

        row_loop(ni, TALL, body)

    def to_slots(put):
        row_loop(ni, TALL, lambda rows: put(rows, both_halves(dot(sel[rows, :], vn[...]))))

    def bulk_start(k):
        def put(rows, value):
            vsrc[k, rows, :] = value

        to_slots(put)
        near_start(slots(vsrc, k), slots(xrecv, k), s4, r4, k)

    def tall_pieces(value):
        hi = value.astype(BF)
        return jnp.concatenate([hi, (value - hi.astype(F32)).astype(BF)], axis=0)

    def skinny(lhs, rhs_pieces):
        out = dot(lhs, rhs_pieces)
        return out[:48, :rhs] + (out[:48, rhs:] + out[48:, :rhs])


    def coarse_scatter(k):
        wait_bytes(gath.at[k, pl.ds(0, nq - 1), few], r1.at[k])
        g_hi, g_lo = split2(gath[k].reshape(nq * 8, rhs))
        out = dot(chi[...], g_hi) + (dot(chi[...], g_lo) + dot(clo[...], g_hi))
        part[k] = out.reshape(np_, 8, rhs)

        for device, at in zip(plane_to, plane_at):
            remote(part.at[k, at, few], redu.at[k, p, few], s2.at[k], r2.at[k], device).start()

        redu[k, p] = part[k, p]

    def coarse_finish(k):
        wait_bytes(redu.at[k, pl.ds(0, np_ - 1), few], r2.at[k])
        coef[k] = jnp.sum(redu[k], axis=0)
        near_start(lambda o: coef.at[k, few], lambda o: call.at[k, o, few], s3, r3, k, far)

    split_mat(0)
    row_loop(ni, CHUNK, lambda rows: put_pieces(rows, -gap[rows, :], vn))
    bulk_start(0)

    near_wait(lambda o: rnb.at[o - 1], r5, 0)
    lane = lax.broadcasted_iota(jnp.int32, (8, ni), 1)
    parts = [rown[...]]
    for d in range(4):
        moved = pltpu.roll(rnb[d], ((d - opp[d]) * cap) % ni, 1)
        live = (lane >= d * cap) & (lane < (d + 1) * cap)
        parts.append(jnp.where(live, -moved, 0.0))
    acols = jnp.concatenate(parts + [jnp.zeros((88, ni), F32)], axis=0)

    def stacked(cols):
        hi = cols.astype(BF).astype(F32)
        low = cols - hi
        return (hi + pltpu.roll(hi, 40, 1) + pltpu.roll(low, 80, 1)).astype(BF)

    arow[...] = tall_pieces(acols[:48])
    for b in range(ni // 128):
        block = slice(b * 128, b * 128 + 128)
        cols = acols[:, block].T
        astk[block, :] = stacked(cols)
        put_pieces(block, cols, xs)

    wait_bytes(cblk.at[pl.ds(0, np_ - 1)], r6.at[0])
    hi, lo = split2(cblk[...].reshape(np_ * 8, nq * 8))
    chi[...] = hi
    clo[...] = lo
    coarse_scatter(0)
    to_rows(xs, xa)

    def partial_start(k, lhs, pieces):
        psend[k] = skinny(lhs, pieces)
        near_start(rows8(psend, k), rows8(pnb, k), s7, r7, k)

    row_loop(ni, CHUNK, lambda rows: put_pieces(rows, vsrc[0, rows, :], xs))
    partial_start(0, arow[...], xs[...])
    def around(k, base):
        picks = []
        for step in OFFSETS[:5]:
            o = OFFSETS.index((base[0] + step[0], base[1] + step[1]))
            picks.append(coef[k] if o == 0 else call[k, o])
        c = jnp.concatenate(picks, axis=0)
        c_hi = c.astype(BF).astype(F32)
        return jnp.concatenate(
            [c_hi, c - c_hi, c_hi, jnp.zeros((8, rhs), F32)], axis=0
        ).astype(BF)

    def prepare(n):
        multiply(n, xa)
        if n == 0:
            coarse_finish(0)

        def put(rows, cols):
            masend[n, rows, :] = cols
            mstk[n, rows, :128] = stacked(cols)
            put_pieces(rows, cols, xs)

        to_slots(put)
        tsend[n] = skinny(arow[...], xs[...])
        near_start(rows8(tsend, n), rows8(tnb, n), s8, r8, n)
        near_start(slots(masend, n), slots(marecv, n), s9, r9, n)

    def prepare_near(n):
        near_wait(slots(marecv, n), r9, n)

        def body(rows):
            mstk[n, rows, 128:] = stacked(-marecv[n, rows, :])

        row_loop(ni, CHUNK, body)

    def prepare_end(n):
        near_wait(rows8(tnb, n), r8, n)
        for o in range(5):
            block = tsend[n, 0:8, :] if o == 0 else tnb[n, 8 * o : 8 * o + 8, :]
            kstk[n, :, o * 128 : o * 128 + 128] = stacked(
                jnp.concatenate([block, jnp.zeros((8, 128), F32)], axis=0)
            )

    def prepare_rows(n):
        out = dot(anat[...], mats_hi[n])
        out = out[:48] + out[48:] + dot(anat[:48, :], mats_lo[n])
        out = dot(tall_pieces(out), sel_t[...])
        bstk[n] = tall_pieces(out[:48] + out[48:])

    def settle(n, last_new):
        share = jnp.where(n == 1, 1.0, 0.0)
        value = wide_w[...] + last_new * dot(astk[...], cvec[...])
        state[n] = value
        total[...] = total[...] + share * value

    prepare(0)
    state[...] = jnp.zeros_like(state)
    prepare_end(0)

    @pl.loop(0, 5)
    def _(k):
        n = k % 2
        odd = n == 1
        last_new = jnp.where(odd | (k == 0), 1.0, jnp.where(k == 2, -0.5 / THETA, -RHO1 / DELTA))

        near_wait(lambda o: call.at[k, o, few], r3, k, far)
        near_wait(rows8(pnb, k), r7, k)
        for o in range(5):
            hood[o] = around(k, OFFSETS[o])
        cvec[...] = hood[0]
        early = psend[k, 0:8, :]
        for o in range(1, 5):
            early = early + pnb[k, 8 * o : 8 * o + 8, :]
        moved = dot(kstk[n], hood[...].reshape(640, rhs))
        comp[k + 1] = early + last_new * moved[:8]
        gather_start(k + 1)

        @pl.when(k == 0)
        def _():
            total[...] = dot(astk[...], cvec[...])
            split_mat(1)
            anat[...] = dot(arow[...], sel[...]).astype(BF)
            prepare_rows(1)

        @pl.when(k > 0)
        def _():
            settle(1 - n, last_new)

        coarse_scatter(k + 1)

        @pl.when(k == 0)
        def _():
            prepare(1)
            prepare_near(0)

        @pl.when(k == 1)
        def _():
            prepare_rows(0)
            prepare_near(1)

        near_wait(slots(xrecv, k), r4, k)
        scale_old = jnp.where(odd, jnp.where(k == 1, 0.0, RHO1 * RHO0), 1.0)
        scale_new = jnp.where(odd, jnp.where(k == 1, 0.5 / THETA, RHO1 / DELTA), -1.0)

        for d in range(4):
            rows = slice(d * cap, (d + 1) * cap)
            both = jnp.concatenate([hood[0], hood[d + 1]], axis=0)
            jumped = vsrc[k, rows, :] - xrecv[k, rows, :] + last_new * dot(mstk[n, rows, :], both)
            w = scale_old * state[n, rows, :] + scale_new * jumped
            wide_w[rows, :] = w
            put_pieces(rows, w, xs)

        @pl.when(k < 4)
        def _():
            partial_start(k + 1, bstk[1 - n], xs[...])
            to_rows(xs, xn)

        coarse_finish(k + 1)

        @pl.when(k < 4)
        def _():
            multiply(1 - n, xn)
            bulk_start(k + 1)

        @pl.when(k == 0)
        def _():
            prepare_end(1)

    near_wait(lambda o: call.at[5, o, few], r3, 5, far)
    cvec[...] = around(5, (0, 0))
    settle(0, 1.0)
    row_loop(ni, CHUNK, lambda rows: put_pieces(rows, total[rows, :], xn))
    row_loop(ni, CHUNK, lambda rows: put_pieces(rows, state[0, rows, :], xs))

    def finish(rows):
        mult[rows, :] = both_halves(dot(sel_t[rows, :], xn[...]))
        res[rows, :] = both_halves(dot(sel_t[rows, :], xs[...]))

    row_loop(ni, TALL, finish)

    near_wait(lambda o: rown, s5, 0)
    wait_bytes(cblk.at[pl.ds(0, np_ - 1)], s6.at[0])
    for n in range(2):
        near_wait(rows8(tsend, n), s8, n)
        near_wait(slots(masend, n), s9, n)

    @pl.loop(0, 6)
    def _(k):
        wait_bytes(gath.at[k, pl.ds(0, nq - 1), few], s1.at[k])
        wait_bytes(redu.at[k, pl.ds(0, np_ - 1), few], s2.at[k])
        near_wait(lambda o: coef.at[k, few], s3, k, far)

    @pl.loop(0, 5)
    def _(k):
        near_wait(slots(vsrc, k), s4, k)
        near_wait(rows8(psend, k), s7, k)


def hand_over(mult, res, mult_out, res_out, held, come, leave):
    half = mult.shape[0] // 2
    pairs = ((mult, mult_out), (res, res_out))
    parts = [(n, h, pl.ds(h * half, half)) for n in range(2) for h in range(2)]
    arriving = [
        pltpu.make_async_copy(pairs[n][0].at[rows], held.at[n, rows], come.at[n, h])
        for n, h, rows in parts
    ]
    leaving = [
        pltpu.make_async_copy(held.at[n, rows], pairs[n][1].at[rows], leave.at[n, h])
        for n, h, rows in parts
    ]
    for copy in arriving:
        copy.start()
    for first, second in zip(arriving, leaving):
        first.wait()
        second.start()
    for copy in leaving:
        copy.wait()


def per_device(dims, local_gap, route_codes, flexibility, dirichlet, rigid_modes, coarse_inverse, rigid_load):
    ni, rhs = local_gap.shape[2:]
    Z, X, Y = dims
    nq, np_ = Z * CORES, X * Y
    cols_z = np_ * CORES * MODES
    window = (max(cols_z * t % 128 for t in range(Z)) + cols_z + 127) // 128 * 128
    far = len(OFFSETS)
    vmem = pl.BlockSpec(memory_space=pltpu.VMEM)
    hbm = pl.BlockSpec(memory_space=pl.ANY)
    field = jax.ShapeDtypeStruct((ni, rhs), F32)
    dma = pltpu.SemaphoreType.DMA
    V = pltpu.VMEM
    mult, res = pl.pallas_call(
        functools.partial(kernel, dims),
        out_shape=(field, field),
        in_specs=[vmem, vmem, hbm, hbm, vmem, vmem, vmem],
        out_specs=(vmem, vmem),
        scratch_shapes=[
            V((2, ni, ni), F32), V((2, ni, ni), BF), V((2, ni, ni), BF),
            V((ni, ni), BF), V((ni, ni), BF),
            V((ni, 2 * rhs), BF), V((ni, 2 * rhs), BF), V((ni, 2 * rhs), BF),
            V((ni, 2 * rhs), BF), V((2, ni, rhs), F32), V((ni, rhs), F32),
            V((ni, rhs), F32), V((2, ni, 128), F32), V((2, ni, 128), F32),
            V((2, ni, 256), BF), V((128, rhs), BF), V((5, 128, rhs), BF), V((5, ni, rhs), F32), V((5, ni, rhs), F32),
            V((6, 8, rhs), F32), V((6, nq, 8, rhs), F32),
            V((6, np_, 8, rhs), F32), V((6, np_, 8, rhs), F32),
            V((6, 8, rhs), F32), V((6, far, 8, rhs), F32),
            V((8, ni), F32), V((4, 8, ni), F32), V((8, (Z - 1) * cols_z // 128 * 128 + window), F32),
            V((np_, 8, nq * 8), F32), V((np_, 8, nq * 8), F32),
            V((np_ * 8, nq * 8), BF), V((np_ * 8, nq * 8), BF), V((ni, 128), BF),
            V((96, ni), BF), V((96, ni), BF), V((2, 96, ni), BF),
            V((2, 48, rhs), F32), V((2, 40, rhs), F32), V((2, 16, 640), BF),
            V((5, 48, rhs), F32), V((5, 40, rhs), F32),
            dma((2,)), dma((6,)), dma((6,)), dma((6,)), dma((6,)),
            dma((6, far)), dma((6, far)), dma((5, 5)), dma((5, 5)),
            dma((1, 5)), dma((1, 5)), dma((1,)), dma((1,)),
            dma((5, 5)), dma((5, 5)), dma((2, 5)), dma((2, 5)),
            dma((2, 5)), dma((2, 5)),
        ],
        compiler_params=pltpu.CompilerParams(
            collective_id=0, has_side_effects=True, vmem_limit_bytes=63 * 1024 * 1024
        ),
    )(
        local_gap[0, 0], route_codes[0], flexibility[0, 0], dirichlet[0, 0],
        rigid_modes.reshape(MODES, 1, ni), coarse_inverse, rigid_load,
    )
    hold = V((2, ni, rhs), F32)
    mult, res = pl.pallas_call(
        hand_over,
        out_shape=(field, field),
        in_specs=[hbm, hbm],
        out_specs=(hbm, hbm),
        scratch_shapes=[hold, dma((2, 2)), dma((2, 2))],
    )(mult, res)
    return mult[None, None], res[None, None]


def solution(mesh):
    placed = (
        P("sub", "layer", None, None),
        P("sub", "layer", None),
        P("sub", "layer", None, None),
        P("sub", "layer", None, None),
        P("sub", "layer", None, None),
        P(("sub", "layer"), None),
        P(("sub", "layer"), None),
    )
    subs, layers = mesh.shape["sub"], mesh.shape["layer"]
    across = 4 if subs % 4 == 0 and subs > 4 else 2
    dims = (subs // across, across, layers // CORES)
    return jax.shard_map(
        functools.partial(per_device, dims),
        mesh=mesh,
        in_specs=placed,
        out_specs=(P("sub", "layer", None, None), P("sub", "layer", None, None)),
        check_vma=False,
    )
```

```python
import functools

import jax
import jax.numpy as jnp
from jax import lax
from jax.experimental import pallas as pl
from jax.experimental.pallas import tpu as pltpu
from jax.sharding import PartitionSpec as P

MESH = pl.DeviceIdType.MESH
THETA = 4.25
DELTA = 3.75
SIGMA = THETA / DELTA
RHO0 = DELTA / THETA
RHO1 = 1.0 / (2.0 * SIGMA - RHO0)
CORES = 2
MODES = 6
BF = jnp.bfloat16
F32 = jnp.float32
CHUNK = 384
TALL = 576
OFFSETS = [
    (0, 0), (-1, 0), (1, 0), (0, -1), (0, 1), (-2, 0), (2, 0),
    (0, -2), (0, 2), (-1, -1), (-1, 1), (1, -1), (1, 1),
]


def split2(v):
    hi = v.astype(BF)
    lo = (v - hi.astype(F32)).astype(BF)
    return hi, lo


def dot(a, b):
    return jnp.dot(a, b, preferred_element_type=F32)


def row_loop(rows, chunk, body):
    chunk = min(chunk, rows)

    @pl.loop(0, rows // chunk)
    def _(t):
        body(pl.ds(pl.multiple_of(t * chunk, chunk), chunk))


def kernel(
    dims, gap, codes, flex, diri, modes, cinv, load, mult, res,
    stage, mats_hi, mats_lo, sel, sel_t, xs, xn, xa, vn, state, total, ahead,
    wide_w, mstk, cvec, vsrc, xrecv, comp, gath, part, redu, coef, call, rown, rnb, cpad, cmat, cblk,
    chi, clo, astk, arow, anat, bstk, tsend, tnb, kstk, psend, pnb,
    mat_sem, s1, r1, s2, r2, s3, r3, s4, r4, s5, r5, s6, r6, s7, r7, s8, r8,
):
    Z, X, Y = dims
    ni, rhs = gap.shape
    cap = ni // 4
    nq, np_ = Z * CORES, X * Y
    i = lax.axis_index("sub")
    j = lax.axis_index("layer")
    z, x = i // X, i % X
    subs, layers = Z * X, Y * CORES
    y, core = j // CORES, j % CORES
    q = z * CORES + core
    p = x * Y + y
    opp = (1, 0, 3, 2)

    def inside(di, dj):
        checks = []
        if di:
            checks.append(i + di >= 0 if di < 0 else i + di < subs)
        if dj:
            checks.append(j + dj >= 0 if dj < 0 else j + dj < layers)
        return checks[0] if len(checks) == 1 else jnp.logical_and(*checks)

    def clipped(di, dj):
        return (jnp.clip(i + di, 0, subs - 1), jnp.clip(j + dj, 0, layers - 1))

    has = [None] + [inside(*o) for o in OFFSETS[1:]]
    away = [None] + [clipped(*o) for o in OFFSETS[1:]]
    back = [OFFSETS.index((-o[0], -o[1])) for o in OFFSETS]
    far = len(OFFSETS)

    def ring(a, n):
        return min(a, n - a)

    line = sorted(
        ((dz, dc) for dz in range(Z) for dc in range(CORES) if dz or dc),
        key=lambda o: -ring(o[0], Z) - 0.5 * o[1],
    )
    plane = sorted(
        ((dx, dy) for dx in range(X) for dy in range(Y) if dx or dy),
        key=lambda o: -ring(o[0], X) - ring(o[1], Y),
    )
    line_to = [
        (((z + dz) % Z) * X + x, y * CORES + (core + dc) % CORES) for dz, dc in line
    ]
    plane_to = [
        (z * X + (x + dx) % X, ((y + dy) % Y) * CORES + core) for dx, dy in plane
    ]
    plane_at = [((x + dx) % X) * Y + (y + dy) % Y for dx, dy in plane]

    loads = [
        pltpu.make_async_copy(flex, stage.at[0], mat_sem.at[0]),
        pltpu.make_async_copy(diri, stage.at[1], mat_sem.at[1]),
    ]
    for cp in loads:
        cp.start()

    for buffer in (call, gath, redu):
        buffer[...] = jnp.zeros_like(buffer)
    pnb[...] = jnp.zeros_like(pnb)
    tnb[...] = jnp.zeros_like(tnb)
    for d in range(4):
        @pl.when(jnp.logical_not(has[d + 1]))
        def _():
            rnb[d] = jnp.zeros_like(rnb[d])

            @pl.loop(0, xrecv.shape[0])
            def _(k):
                xrecv[k, pl.ds(d * cap, cap), :] = jnp.zeros((cap, rhs), F32)

    barrier = pltpu.get_barrier_semaphore()

    def greet(device):
        pl.semaphore_signal(barrier, inc=1, device_id=device, device_id_type=MESH)

    for device in line_to + plane_to:
        greet(device)

    count = nq + np_ - 2
    for o in range(1, far):
        @pl.when(has[o])
        def _():
            greet(away[o])

        count = count + has[o].astype(jnp.int32)

    comp[0] = jnp.concatenate([load[...], jnp.zeros((8 - MODES, rhs), F32)], axis=0)

    cpad[...] = jnp.zeros_like(cpad)
    cpad[:MODES, : cinv.shape[1]] = cinv[...]
    cols_z = np_ * CORES * MODES
    lanes_z = np_ * CORES * 8
    window = cpad.shape[1] - (Z - 1) * cols_z // 128 * 128
    place = lax.broadcasted_iota(jnp.int32, (window, lanes_z), 0)
    target = lax.broadcasted_iota(jnp.int32, (window, lanes_z), 1)
    live = (place == target // 8 * MODES + target % 8) & (target % 8 < MODES)
    spread = jnp.where(live, 1.0, 0.0).astype(BF)
    slabs = []
    for t in range(Z):
        low = t * cols_z // 128 * 128
        slab = cpad[:, low : low + window]
        shift = t * cols_z % 128
        slabs.append(pltpu.roll(slab, window - shift, 1) if shift else slab)
    slab = jnp.concatenate(slabs, axis=0)
    c1 = slab.astype(BF)
    c2, c3 = split2(slab - c1.astype(F32))
    wide = dot(c1, spread) + (dot(c2, spread) + dot(c3, spread))
    group = lax.broadcasted_iota(jnp.int32, (8, nq * 8), 1) // (CORES * 8)
    for b in range(np_):
        low = b * CORES * 8 // (nq * 8) * (nq * 8)
        out = jnp.zeros((8, nq * 8), F32)
        for t in range(Z):
            piece = wide[8 * t : 8 * t + 8, low : low + nq * 8]
            shift = (t * CORES * 8 - (b * CORES * 8 - low)) % (nq * 8)
            out = jnp.where(group == t, pltpu.roll(piece, shift, 1) if shift else piece, out)
        cmat[b] = out

    pl.semaphore_wait(barrier, count)

    def remote(src, dst, send, recv, device):
        return pltpu.make_async_remote_copy(
            src_ref=src, dst_ref=dst, send_sem=send, recv_sem=recv,
            device_id=device, device_id_type=MESH,
        )

    def wait_bytes(ref, sem):
        pltpu.make_async_copy(ref, ref, sem).wait()

    few = pl.ds(0, MODES)

    def gather_start(k):
        gath[k, q] = comp[k]

        for device in line_to:
            remote(comp.at[k, few], gath.at[k, q, few], s1.at[k], r1.at[k], device).start()

    def near_start(src_of, dst_of, send, recv, k, many=5):
        for o in range(1, many):
            @pl.when(has[o])
            def _():
                remote(src_of(o), dst_of(back[o]), send.at[k, o], recv.at[k, back[o]], away[o]).start()

    def near_wait(ref_of, sem, k, many=5):
        for o in range(1, many):
            @pl.when(has[o])
            def _():
                wait_bytes(ref_of(o), sem.at[k, o])

    def slots(ref, k):
        return lambda o: ref.at[k, pl.ds((o - 1) * cap, cap), :]

    def rows8(ref, k):
        return lambda o: ref.at[k, pl.ds(8 * o, 8), :]

    gather_start(0)

    for device, at in zip(plane_to, plane_at):
        remote(cmat.at[at], cblk.at[p], s6.at[0], r6.at[0], device).start()

    cblk[p] = cmat[p]

    code_row = codes[...]
    for b in range(ni // 128):
        block = slice(b * 128, b * 128 + 128)
        slot = lax.broadcasted_iota(jnp.int32, (128, ni), 0) + b * 128
        sel[block, :] = jnp.where(code_row == slot, 1.0, 0.0).astype(BF)
        column = jnp.broadcast_to(code_row[:, block].astype(F32), (128, 128)).T.astype(jnp.int32)
        for c in range(ni // 128):
            lane = lax.broadcasted_iota(jnp.int32, (128, 128), 1) + c * 128
            sel_t[block, c * 128 : c * 128 + 128] = jnp.where(column == lane, 1.0, 0.0).astype(BF)

    wide = jnp.concatenate([modes[m] for m in range(MODES)] + [jnp.zeros((16 - MODES, ni), F32)], axis=0)
    m1 = wide.astype(BF)
    m2, m3 = split2(wide - m1.astype(F32))
    pieces = dot(jnp.concatenate([m1, m2, m3], axis=0), sel_t[...])
    rown[...] = pieces[:8] + (pieces[16:24] + pieces[32:40])

    near_start(lambda o: rown, lambda o: rnb.at[o - 1], s5, r5, 0)

    def split_mat(n):
        loads[n].wait()

        def body(rows):
            hi, lo = split2(stage[n, rows, :])
            mats_hi[n, rows, :] = hi
            mats_lo[n, rows, :] = lo

        row_loop(ni, 128, body)

    def put_pieces(rows, value, ref):
        hi, lo = split2(value)
        ref[rows, :rhs] = hi
        ref[rows, rhs:] = lo

    def both_halves(both):
        return both[:, :rhs] + both[:, rhs:]

    def to_rows(src, dst):
        def body(rows):
            dst[rows, :] = dot(sel_t[rows, :], src[...]).astype(BF)

        row_loop(ni, TALL, body)

    def multiply(n, src):
        def body(rows):
            both = dot(mats_hi[n, rows, :], src[...]) + dot(mats_lo[n, rows, :], src[...])
            put_pieces(rows, both_halves(both), vn)

        row_loop(ni, TALL, body)

    def to_slots(put):
        row_loop(ni, TALL, lambda rows: put(rows, both_halves(dot(sel[rows, :], vn[...]))))

    def put_ahead(rows, value):
        ahead[rows, :] = value

    def tall_pieces(value):
        hi = value.astype(BF)
        return jnp.concatenate([hi, (value - hi.astype(F32)).astype(BF)], axis=0)

    def skinny(lhs, rhs_pieces):
        out = dot(lhs, rhs_pieces)
        return out[:48, :rhs] + (out[:48, rhs:] + out[48:, :rhs])


    def coarse_scatter(k):
        wait_bytes(gath.at[k, pl.ds(0, nq - 1), few], r1.at[k])
        g_hi, g_lo = split2(gath[k].reshape(nq * 8, rhs))
        out = dot(chi[...], g_hi) + (dot(chi[...], g_lo) + dot(clo[...], g_hi))
        part[k] = out.reshape(np_, 8, rhs)

        for device, at in zip(plane_to, plane_at):
            remote(part.at[k, at, few], redu.at[k, p, few], s2.at[k], r2.at[k], device).start()

        redu[k, p] = part[k, p]

    def coarse_finish(k):
        wait_bytes(redu.at[k, pl.ds(0, np_ - 1), few], r2.at[k])
        coef[k] = jnp.sum(redu[k], axis=0)
        near_start(lambda o: coef.at[k, few], lambda o: call.at[k, o, few], s3, r3, k, far)

    split_mat(0)
    row_loop(ni, CHUNK, lambda rows: put_pieces(rows, -gap[rows, :], vn))
    to_slots(put_ahead)

    near_wait(lambda o: rnb.at[o - 1], r5, 0)
    lane = lax.broadcasted_iota(jnp.int32, (8, ni), 1)
    parts = [rown[...]]
    for d in range(4):
        moved = pltpu.roll(rnb[d], ((d - opp[d]) * cap) % ni, 1)
        live = (lane >= d * cap) & (lane < (d + 1) * cap)
        parts.append(jnp.where(live, -moved, 0.0))
    acols = jnp.concatenate(parts + [jnp.zeros((88, ni), F32)], axis=0)

    def stacked(cols):
        hi = cols.astype(BF).astype(F32)
        low = cols - hi
        return (hi + pltpu.roll(hi, 40, 1) + pltpu.roll(low, 80, 1)).astype(BF)

    arow[...] = tall_pieces(acols[:48])
    for b in range(ni // 128):
        block = slice(b * 128, b * 128 + 128)
        cols = acols[:, block].T
        astk[block, :] = stacked(cols)
        put_pieces(block, cols, xs)

    wait_bytes(cblk.at[pl.ds(0, np_ - 1)], r6.at[0])
    hi, lo = split2(cblk[...].reshape(np_ * 8, nq * 8))
    chi[...] = hi
    clo[...] = lo
    coarse_scatter(0)
    to_rows(xs, xa)

    def partial_start(k, lhs, pieces):
        psend[k] = skinny(lhs, pieces)
        near_start(rows8(psend, k), rows8(pnb, k), s7, r7, k)

    row_loop(ni, CHUNK, lambda rows: put_pieces(rows, ahead[rows, :], xs))
    partial_start(0, arow[...], xs[...])
    def around(k, base):
        picks = []
        for step in OFFSETS[:5]:
            o = OFFSETS.index((base[0] + step[0], base[1] + step[1]))
            picks.append(coef[k] if o == 0 else call[k, o])
        c = jnp.concatenate(picks, axis=0)
        c_hi = c.astype(BF).astype(F32)
        return jnp.concatenate(
            [c_hi, c - c_hi, c_hi, jnp.zeros((8, rhs), F32)], axis=0
        ).astype(BF)

    def prepare(n):
        multiply(n, xa)
        if n == 0:
            coarse_finish(0)

        def put(rows, cols):
            mstk[n, rows, :] = stacked(cols)
            put_pieces(rows, cols, xs)

        to_slots(put)
        tsend[n] = skinny(arow[...], xs[...])
        near_start(rows8(tsend, n), rows8(tnb, n), s8, r8, n)

    def prepare_end(n):
        near_wait(rows8(tnb, n), r8, n)
        for o in range(5):
            block = tsend[n, 0:8, :] if o == 0 else tnb[n, 8 * o : 8 * o + 8, :]
            kstk[n, :, o * 128 : o * 128 + 128] = stacked(
                jnp.concatenate([block, jnp.zeros((8, 128), F32)], axis=0)
            )

    def prepare_rows(n):
        out = dot(anat[...], mats_hi[n])
        out = out[:48] + out[48:] + dot(anat[:48, :], mats_lo[n])
        out = dot(tall_pieces(out), sel_t[...])
        bstk[n] = tall_pieces(out[:48] + out[48:])

    def settle(n, last_new):
        share = jnp.where(n == 1, 1.0, 0.0)
        value = wide_w[...] + last_new * dot(astk[...], cvec[...])
        state[n] = value
        total[...] = total[...] + share * value

    prepare(0)
    state[...] = jnp.zeros_like(state)
    prepare_end(0)

    @pl.loop(0, 5)
    def _(k):
        n = k % 2
        odd = n == 1
        last_new = jnp.where(odd | (k == 0), 1.0, jnp.where(k == 2, -0.5 / THETA, -RHO1 / DELTA))

        @pl.when(k > 0)
        def _():
            to_slots(put_ahead)

        near_wait(lambda o: call.at[k, o, few], r3, k, far)
        near_wait(rows8(pnb, k), r7, k)
        hood = [around(k, o) for o in OFFSETS[:5]]
        cvec[...] = hood[0]
        early = psend[k, 0:8, :]
        for o in range(1, 5):
            early = early + pnb[k, 8 * o : 8 * o + 8, :]
        moved = dot(kstk[n], jnp.concatenate(hood, axis=0))
        comp[k + 1] = early + last_new * moved[:8]
        gather_start(k + 1)
        vsrc[k] = ahead[...] + last_new * dot(mstk[n], cvec[...])
        near_start(slots(vsrc, k), slots(xrecv, k), s4, r4, k)

        @pl.when(k == 0)
        def _():
            total[...] = dot(astk[...], cvec[...])
            split_mat(1)
            anat[...] = dot(arow[...], sel[...]).astype(BF)
            prepare_rows(1)

        @pl.when(k > 0)
        def _():
            settle(1 - n, last_new)

        coarse_scatter(k + 1)

        @pl.when(k == 0)
        def _():
            prepare(1)

        @pl.when(k == 1)
        def _():
            prepare_rows(0)

        near_wait(slots(xrecv, k), r4, k)
        scale_old = jnp.where(odd, jnp.where(k == 1, 0.0, RHO1 * RHO0), 1.0)
        scale_new = jnp.where(odd, jnp.where(k == 1, 0.5 / THETA, RHO1 / DELTA), -1.0)

        def fresh(rows):
            jumped = vsrc[k, rows, :] - xrecv[k, rows, :]
            w = scale_old * state[n, rows, :] + scale_new * jumped
            wide_w[rows, :] = w
            put_pieces(rows, w, xs)

        row_loop(ni, CHUNK, fresh)

        @pl.when(k < 4)
        def _():
            partial_start(k + 1, bstk[1 - n], xs[...])
            to_rows(xs, xn)

        coarse_finish(k + 1)

        @pl.when(k < 4)
        def _():
            multiply(1 - n, xn)

        @pl.when(k == 0)
        def _():
            prepare_end(1)

    near_wait(lambda o: call.at[5, o, few], r3, 5, far)
    cvec[...] = around(5, (0, 0))
    settle(0, 1.0)
    row_loop(ni, CHUNK, lambda rows: put_pieces(rows, total[rows, :], xn))
    row_loop(ni, CHUNK, lambda rows: put_pieces(rows, state[0, rows, :], xs))

    def finish(rows):
        mult[rows, :] = both_halves(dot(sel_t[rows, :], xn[...]))
        res[rows, :] = both_halves(dot(sel_t[rows, :], xs[...]))

    row_loop(ni, TALL, finish)

    near_wait(lambda o: rown, s5, 0)
    wait_bytes(cblk.at[pl.ds(0, np_ - 1)], s6.at[0])
    for n in range(2):
        near_wait(rows8(tsend, n), s8, n)

    @pl.loop(0, 6)
    def _(k):
        wait_bytes(gath.at[k, pl.ds(0, nq - 1), few], s1.at[k])
        wait_bytes(redu.at[k, pl.ds(0, np_ - 1), few], s2.at[k])
        near_wait(lambda o: coef.at[k, few], s3, k, far)

    @pl.loop(0, 5)
    def _(k):
        near_wait(slots(vsrc, k), s4, k)
        near_wait(rows8(psend, k), s7, k)


def hand_over(mult, res, mult_out, res_out, held, come, leave):
    half = mult.shape[0] // 2
    pairs = ((mult, mult_out), (res, res_out))
    parts = [(n, h, pl.ds(h * half, half)) for n in range(2) for h in range(2)]
    arriving = [
        pltpu.make_async_copy(pairs[n][0].at[rows], held.at[n, rows], come.at[n, h])
        for n, h, rows in parts
    ]
    leaving = [
        pltpu.make_async_copy(held.at[n, rows], pairs[n][1].at[rows], leave.at[n, h])
        for n, h, rows in parts
    ]
    for copy in arriving:
        copy.start()
    for first, second in zip(arriving, leaving):
        first.wait()
        second.start()
    for copy in leaving:
        copy.wait()


def per_device(dims, local_gap, route_codes, flexibility, dirichlet, rigid_modes, coarse_inverse, rigid_load):
    ni, rhs = local_gap.shape[2:]
    Z, X, Y = dims
    nq, np_ = Z * CORES, X * Y
    cols_z = np_ * CORES * MODES
    window = (max(cols_z * t % 128 for t in range(Z)) + cols_z + 127) // 128 * 128
    far = len(OFFSETS)
    vmem = pl.BlockSpec(memory_space=pltpu.VMEM)
    hbm = pl.BlockSpec(memory_space=pl.ANY)
    field = jax.ShapeDtypeStruct((ni, rhs), F32)
    dma = pltpu.SemaphoreType.DMA
    V = pltpu.VMEM
    mult, res = pl.pallas_call(
        functools.partial(kernel, dims),
        out_shape=(field, field),
        in_specs=[vmem, vmem, hbm, hbm, vmem, vmem, vmem],
        out_specs=(vmem, vmem),
        scratch_shapes=[
            V((2, ni, ni), F32), V((2, ni, ni), BF), V((2, ni, ni), BF),
            V((ni, ni), BF), V((ni, ni), BF),
            V((ni, 2 * rhs), BF), V((ni, 2 * rhs), BF), V((ni, 2 * rhs), BF),
            V((ni, 2 * rhs), BF), V((2, ni, rhs), F32), V((ni, rhs), F32),
            V((ni, rhs), F32), V((ni, rhs), F32), V((2, ni, 128), BF),
            V((128, rhs), BF), V((5, ni, rhs), F32), V((5, ni, rhs), F32),
            V((6, 8, rhs), F32), V((6, nq, 8, rhs), F32),
            V((6, np_, 8, rhs), F32), V((6, np_, 8, rhs), F32),
            V((6, 8, rhs), F32), V((6, far, 8, rhs), F32),
            V((8, ni), F32), V((4, 8, ni), F32), V((8, (Z - 1) * cols_z // 128 * 128 + window), F32),
            V((np_, 8, nq * 8), F32), V((np_, 8, nq * 8), F32),
            V((np_ * 8, nq * 8), BF), V((np_ * 8, nq * 8), BF), V((ni, 128), BF),
            V((96, ni), BF), V((96, ni), BF), V((2, 96, ni), BF),
            V((2, 48, rhs), F32), V((2, 40, rhs), F32), V((2, 16, 640), BF),
            V((5, 48, rhs), F32), V((5, 40, rhs), F32),
            dma((2,)), dma((6,)), dma((6,)), dma((6,)), dma((6,)),
            dma((6, far)), dma((6, far)), dma((5, 5)), dma((5, 5)),
            dma((1, 5)), dma((1, 5)), dma((1,)), dma((1,)),
            dma((5, 5)), dma((5, 5)), dma((2, 5)), dma((2, 5)),
        ],
        compiler_params=pltpu.CompilerParams(
            collective_id=0, has_side_effects=True, vmem_limit_bytes=63 * 1024 * 1024
        ),
    )(
        local_gap[0, 0], route_codes[0], flexibility[0, 0], dirichlet[0, 0],
        rigid_modes.reshape(MODES, 1, ni), coarse_inverse, rigid_load,
    )
    hold = V((2, ni, rhs), F32)
    mult, res = pl.pallas_call(
        hand_over,
        out_shape=(field, field),
        in_specs=[hbm, hbm],
        out_specs=(hbm, hbm),
        scratch_shapes=[hold, dma((2, 2)), dma((2, 2))],
    )(mult, res)
    return mult[None, None], res[None, None]


def solution(mesh):
    placed = (
        P("sub", "layer", None, None),
        P("sub", "layer", None),
        P("sub", "layer", None, None),
        P("sub", "layer", None, None),
        P("sub", "layer", None, None),
        P(("sub", "layer"), None),
        P(("sub", "layer"), None),
    )
    subs, layers = mesh.shape["sub"], mesh.shape["layer"]
    across = 4 if subs % 4 == 0 and subs > 4 else 2
    dims = (subs // across, across, layers // CORES)
    return jax.shard_map(
        functools.partial(per_device, dims),
        mesh=mesh,
        in_specs=placed,
        out_specs=(P("sub", "layer", None, None), P("sub", "layer", None, None)),
        check_vma=False,
    )
```
